128 devices in a mesh: grp: 2 (over x_lo), gr: 8 (over z, x_hi), gc: 8 (over y, core).
Axes of the slice: x: 4 (x_hi: 2, x_lo: 2; x = x_hi * 2 + x_lo), y: 4, z: 4, core: 2. Of those that a mesh axis runs over, the one named last changes fastest.
Arguments:
- embeddings: bfloat16 [131072, 768], P(('grp', 'gr', 'gc')), parts along dimension 0, may hold values from -2000 to 2000
- sorted_slot: int32 [131072], P(('grp', 'gr', 'gc')), parts along dimension 0, may hold values from 0 to 65535, as said below
- cluster_ids: int32 [131072], P(('grp', 'gr', 'gc')), parts along dimension 0, may hold values from 0 to 31, never falling along the last dimension, each value on 1 to 5120 neighbouring positions
- block_list: int32 [128, 4], P(('grp', 'gr', 'gc')), parts along dimension 0, may hold values 0 or 1
Outputs:
- dedup_weight: float32 [131072], P(('grp', 'gr', 'gc')), parts along dimension 0
The draws below stay inside these ranges and needn't reach their ends.
There are 2 independent parts, one for each index of `grp`. The reference program is written for one: setup_inputs(seed, part) draws one part's arguments, and reference() takes and returns one part's arrays. A program takes and returns all parts, laid end to end along the dimension named above; each array names one. Nothing has to cross between parts.
Inputs may be any that keep to these rules, and one draw needn't show every extreme that they name: `sorted_slot`: a permutation; the 1024 encoder-order rows of each block hold exactly 16 positions in each block of cluster-sorted rows. `cluster_ids`: ids never fall along the cluster-sorted rows.
All inputs are finite; a program needn't handle non-finite values. No bound on the sum of `block_list` on one device may be relied on, other than what follows from the above.
Results may differ from the reference program's by a relative error of at most 0.00044.
Values may be sent and summed in bfloat16 or wider, within the bound.
No kernel may reach another device: no remote copies, remote signals or barrier semaphores. Data moves between devices by JAX's collectives and lax.ppermute only.
A program may use at most 64 MiB of HBM per device.

```python
import math
import jax
import jax.numpy as jnp
import numpy as np
from jax import lax

D = 768
ROWS_DEV = 1024
SHIFTS = 4
BLOCKS = 64
ROWS = 65536
CLUSTERS = 32


def draw_sorted_slot(key, part):
    per_pair = ROWS_DEV // BLOCKS
    key_pair = jax.random.split(jax.random.fold_in(key, 11), 2)
    counting = jnp.arange(ROWS_DEV, dtype=jnp.int32)
    within = jax.vmap(jax.random.permutation, in_axes=(0, None))(jax.random.split(key_pair[0], BLOCKS), counting)
    spread = jax.vmap(jax.random.permutation, in_axes=(0, None))(jax.random.split(key_pair[1], BLOCKS), counting)
    target = counting // per_pair
    column = counting % per_pair
    source = jnp.arange(BLOCKS, dtype=jnp.int32)[:, None]
    position = target[None, :] * ROWS_DEV + within[target[None, :], source * per_pair + column[None, :]]
    encoder_row = source * ROWS_DEV + spread
    result = jnp.zeros((ROWS,), jnp.int32).at[encoder_row.reshape(-1)].set(position.reshape(-1).astype(jnp.int32))
    return result


def draw_embeddings(key, part):
    key_list = jax.random.split(jax.random.fold_in(key, 23), 5)
    latent = jnp.clip(jax.random.normal(key_list[0], (ROWS, 8), jnp.float32), -4.0, 4.0)
    jitter = jnp.clip(jax.random.normal(key_list[1], (ROWS, D), jnp.float32), -4.0, 4.0)
    row_scale = jnp.exp(jax.random.uniform(key_list[2], (ROWS,), jnp.float32, 0.0, math.log(10.0)))
    directions = jnp.clip(jax.random.normal(key_list[3], (D,), jnp.float32), -4.0, 4.0)
    col_scale = jnp.exp(jax.random.uniform(key_list[4], (D,), jnp.float32, 0.0, math.log(10.0)))
    mixed = jnp.take(latent, jnp.arange(D, dtype=jnp.int32) % 8, axis=1) * directions[None, :]
    values = (mixed + jitter) * col_scale[None, :] * row_scale[:, None]
    return values.astype(jnp.bfloat16)


def place_ends(drawn, rng, low, top_value):
    longest = drawn.shape.index(max(drawn.shape))
    spots = []
    for shift in (0, 1):
        where = [jax.random.randint(jax.random.fold_in(rng, axis), (), 0, length) for axis, length in enumerate(drawn.shape)]
        where[longest] = (where[longest] + shift) % drawn.shape[longest]
        spots.append(tuple(where))
    return drawn.at[spots[0]].set(low).at[spots[1]].set(top_value)


def split_up(amount, total, reach, skew):
    portions = [(1 << 20) // math.isqrt(rank ** skew) + 1 for rank in range(2, amount + 1)]
    surplus, given = total - reach - (amount - 1), [1] * (amount - 1)
    while surplus > 0:
        movable = [i for i in range(amount - 1) if given[i] < reach]
        whole, left = sum([portions[i] for i in movable]), surplus
        for i in movable:
            more = min(reach - given[i], max(1, left * portions[i] // whole), surplus)
            given[i] = given[i] + more
            surplus = surplus - more
    return np.array([reach] + given)


def uneven_parts(stream_key, number_of, total, reach, lean):
    if number_of == 2:
        one = jax.random.randint(stream_key, (), max(1, total - reach), min(reach, total - 1) + 1)
        return jnp.stack([one, total - one])
    lengths = jnp.asarray(split_up(number_of, total, reach, lean), jnp.int32)
    twos = (number_of - 1) // 2
    source_of, receiver = lengths[1:1 + 2 * twos:2], lengths[2:2 + 2 * twos:2]
    margin = jnp.minimum(source_of - 1, reach - receiver)
    shifted = jax.random.randint(jax.random.fold_in(stream_key, 1), (twos,), 0, 1 << 20) % (margin + 1)
    lengths = lengths.at[1:1 + 2 * twos:2].set(source_of - shifted).at[2:2 + 2 * twos:2].set(receiver + shifted)
    return lengths[jax.random.permutation(jax.random.fold_in(stream_key, 2), number_of)]


def setup_inputs(seed: int = 0, part: int = 0) -> dict:
    keys = jax.random.split(jax.random.key(seed), 5)
    own_keys = jax.random.split(jax.random.fold_in(keys[4], part), 5)
    embeddings = draw_embeddings(jax.random.fold_in(jax.random.fold_in(keys[4], part), 71), part)
    sorted_slot = draw_sorted_slot(jax.random.fold_in(jax.random.fold_in(keys[4], part), 71), part)
    cluster_ids = jnp.searchsorted(jnp.cumsum(uneven_parts(own_keys[2], CLUSTERS, ROWS, (SHIFTS + 1) * ROWS_DEV, 2)), jnp.arange(ROWS), side="right").astype(jnp.int32)
    block_list = place_ends((jax.random.randint(own_keys[3], (BLOCKS, SHIFTS), 0, 2) < 1).astype(jnp.int32), jax.random.fold_in(own_keys[3], 1), 0, 1)
    return dict(embeddings=embeddings, sorted_slot=sorted_slot, cluster_ids=cluster_ids, block_list=block_list)


sharpness = 20.0
threshold = 0.8

def normalize(sorted_rows):
    values = sorted_rows.astype(jnp.float32)
    inverse = lax.rsqrt(lax.optimization_barrier(jnp.mean(values * values, axis=-1, keepdims=True)) + 1e-06) / math.sqrt(sorted_rows.shape[-1])
    return (values * inverse).astype(jnp.bfloat16)

def reference(embeddings, sorted_slot, cluster_ids, block_list):
    placed = jnp.zeros_like(embeddings).at[sorted_slot].set(embeddings)
    unit_rows = normalize(placed)
    window_blocks = 2 * SHIFTS + 1
    pad_rows = SHIFTS * ROWS_DEV
    units_pad = jnp.pad(unit_rows, ((pad_rows, pad_rows), (0, 0)))
    ids_pad = jnp.pad(cluster_ids, (pad_rows, pad_rows), constant_values=-1)
    list_pad = jnp.pad(block_list.astype(jnp.float32), ((SHIFTS, SHIFTS), (0, 0)))

    def one_block(block_id):
        first_row = (block_id * ROWS_DEV).astype(jnp.int32)
        my_rows = lax.dynamic_slice_in_dim(unit_rows, first_row, ROWS_DEV, 0)
        my_ids = lax.dynamic_slice_in_dim(cluster_ids, first_row, ROWS_DEV, 0)
        window = lax.dynamic_slice_in_dim(units_pad, first_row, window_blocks * ROWS_DEV, 0)
        window_ids = lax.dynamic_slice_in_dim(ids_pad, first_row, window_blocks * ROWS_DEV, 0)
        ahead_flags = lax.dynamic_slice(list_pad, (block_id + SHIFTS, jnp.int32(0)), (1, SHIFTS))[0]
        mask_slab = lax.dynamic_slice(list_pad, (block_id, jnp.int32(0)), (SHIFTS, SHIFTS))
        behind_flags = jnp.diagonal(mask_slab[::-1])[::-1]
        factors = jnp.concatenate([behind_flags, jnp.ones((1,), jnp.float32), ahead_flags])
        col_factor = jnp.repeat(factors, ROWS_DEV) * (window_ids >= 0).astype(jnp.float32)
        cosine = jnp.dot(my_rows, window.T, preferred_element_type=jnp.float32)
        same_cluster = my_ids[:, None] == window_ids[None, :]
        kinship = jnp.where(same_cluster, 1.0, 0.5)
        row_iota = lax.broadcasted_iota(jnp.int32, cosine.shape, 0)
        col_iota = lax.broadcasted_iota(jnp.int32, cosine.shape, 1)
        keep = col_iota != row_iota + pad_rows
        pair_terms = jnp.where(keep, kinship * jax.nn.sigmoid(sharpness * (cosine - threshold)), 0.0) * col_factor[None, :]
        dup_load = lax.optimization_barrier(jnp.sum(pair_terms, axis=1))
        return 1.0 / (1.0 + dup_load)
    weights = lax.map(one_block, jnp.arange(BLOCKS, dtype=jnp.int32))
    return weights.reshape(-1)
```

```python
import functools
import math

import jax
import jax.numpy as jnp
from jax import lax
from jax.experimental import pallas as pl
from jax.experimental.pallas import tpu as pltpu
from jax.sharding import PartitionSpec as P

SHIFTS = 4
ROWS = 1024
WIDTH = 768
LANES = 128
CHUNKS = 2
PART = ROWS // CHUNKS
AXES = ("gr", "gc")

sharpness = 20.0
threshold = 0.8

F32 = jnp.float32
BF16 = jnp.bfloat16
VMEM = pl.BlockSpec(memory_space=pltpu.VMEM)
ANY = pl.BlockSpec(memory_space=pl.ANY)


def iota(shape, axis):
    return lax.broadcasted_iota(jnp.int32, shape, axis)


def one_hot(rows, first, wanted):
    hit = iota((rows, wanted.shape[1]), 0) + first == wanted
    return jnp.where(hit, 1.0, 0.0).astype(BF16)


def nt(a, b):
    return lax.dot_general(a, b, (((1,), (1,)), ((), ())), preferred_element_type=F32)


def front_kernel(devices, emb_ref, slot_ref, out_ref, land_ref, unit_ref):
    per_pair = ROWS // devices
    for step in range(4):
        part = pl.ds(step * 256, 256)
        values = emb_ref[part, :].astype(F32)
        mean = jnp.sum(values * values, axis=1, keepdims=True) * (1.0 / WIDTH)
        inverse = lax.rsqrt(mean + 1e-06) * (1.0 / math.sqrt(WIDTH))
        unit_ref[part, :] = (values * inverse).astype(BF16)
    slot = slot_ref[...]
    target = slot // ROWS
    low = slot - target * ROWS
    goes = iota((devices, ROWS), 0) == target
    goes_b = jnp.where(goes, 1.0, 0.0).astype(BF16)
    before = jnp.where(iota((ROWS, ROWS), 0) < iota((ROWS, ROWS), 1), 1.0, 0.0).astype(BF16)
    count = jnp.dot(goes_b, before, preferred_element_type=F32)
    rank = jnp.sum(jnp.where(goes, count, 0.0), axis=0, keepdims=True)
    dest = target * per_pair + rank.astype(jnp.int32)
    low_hi = low // 32
    low_lo = low - low_hi * 32
    which = iota((8, ROWS), 0)
    digits = jnp.where(which == 0, low_hi.astype(F32), jnp.where(which == 1, low_lo.astype(F32), 0.0)).astype(BF16)
    for step in range(4):
        part = pl.ds(step * 256, 256)
        place = one_hot(256, step * 256, dest)
        out_ref[part, :] = jnp.dot(place, unit_ref[...], preferred_element_type=F32).astype(BF16)
        sent = nt(digits, place)
        land_ref[:, part] = (sent[0:1, :] * 32.0 + sent[1:2, :]).astype(jnp.int32)


def meta_kernel(land_ref, ids_ref, list_ref, out_ref):
    ids = jnp.broadcast_to(ids_ref[...].astype(F32), (8, ROWS)).astype(BF16)
    arrived = jnp.zeros((8, ROWS), F32)
    for step in range(4):
        place = one_hot(256, step * 256, land_ref[...])
        arrived = arrived + jnp.dot(ids[:, step * 256:(step + 1) * 256], place, preferred_element_type=F32)
    out_ref[:, 0:ROWS] = arrived[0:1, :].astype(jnp.int32)
    out_ref[:, ROWS:ROWS + LANES] = list_ref[...]


def weight_of(meta_ref, shift):
    entries = meta_ref[:, ROWS:ROWS + LANES].astype(F32)
    return jnp.sum(jnp.where(iota((1, LANES), 1) == shift - 1, entries, 0.0), axis=1, keepdims=True)


def ids_row(meta_ref, part=None):
    where = slice(0, ROWS) if part is None else slice(part * PART, (part + 1) * PART)
    return meta_ref[:, where].astype(F32)


def as_column(row):
    return jnp.transpose(jnp.broadcast_to(row, (LANES, row.shape[1])))


def tile_terms(scores, id_col, id_row, masked):
    rows, cols = scores.shape
    over_cols, over_rows = None, []
    for lane in range(cols // LANES):
        cut = slice(lane * LANES, (lane + 1) * LANES)
        half = jnp.tanh(scores[:, cut] * (0.5 * sharpness) - 0.5 * sharpness * threshold)
        factor = jnp.where(id_col == id_row[:, cut], 0.5, 0.25)
        term = factor * (1.0 + half)
        if masked:
            term = jnp.where(iota(term.shape, 0) == iota(term.shape, 1) + lane * LANES, 0.0, term)
        over_cols = term if over_cols is None else over_cols + term
        over_rows.append(jnp.sum(term.reshape(rows // 8, 8, LANES), axis=0))
    return over_cols, jnp.concatenate(over_rows, axis=1)


def pair(a_ref, a_base, a_rows, a_col, b_ref, b_base, b_rows, b_row, weight, row_acc, row_base, col_acc, col_base):
    height, breadth = 256, 512

    def step(i, carry):
        a_at = pl.multiple_of(i * height, height)
        a = a_ref[pl.ds(a_base + a_at, height), :]
        col = a_col[pl.ds(a_at, height), :]
        total = None
        for j in range(b_rows // breadth):
            scores = nt(a, b_ref[pl.ds(b_base + j * breadth, breadth), :])
            by_row, by_col = tile_terms(scores, col, b_row[:, j * breadth:(j + 1) * breadth], False)
            total = by_row if total is None else total + by_row
            at = pl.ds(col_base + j * breadth, breadth)
            col_acc[:, at] = col_acc[:, at] + weight * by_col
        at = pl.ds(row_base + a_at, height)
        row_acc[at, :] = row_acc[at, :] + weight * total
        return carry

    lax.fori_loop(0, a_rows // height, step, 0)


def own_pair(ref, col_ref, row, row_acc, col_acc):
    size = 256
    for i in range(ROWS // size):
        a = ref[i * size:(i + 1) * size, :]
        col = col_ref[i * size:(i + 1) * size, :]
        for j in range(i, ROWS // size):
            cut = slice(j * size, (j + 1) * size)
            by_row, by_col = tile_terms(nt(a, ref[cut, :]), col, row[:, cut], i == j)
            at = slice(i * size, (i + 1) * size)
            row_acc[at, :] = row_acc[at, :] + by_row
            if j > i:
                col_acc[:, cut] = col_acc[:, cut] + by_col


def fold_rows(acc):
    return jnp.sum(jnp.transpose(acc[...]), axis=0, keepdims=True)


def fold_cols(acc):
    return jnp.sum(acc[...], axis=0, keepdims=True)


def fetch(copies):
    started = []
    for source, target, sem in copies:
        copy = pltpu.make_async_copy(source, target, sem)
        copy.start()
        started.append(copy)
    return started


def stage0_kernel(core_ref, meta, meta_sw, own, sw, own_out, sw_out, v_own, v_sw, col, row_acc, col_acc, sw_acc, sems):
    got = fetch([(own, v_own, sems.at[0]), (sw, v_sw, sems.at[1])])
    row_acc[...] = jnp.zeros_like(row_acc)
    col_acc[...] = jnp.zeros_like(col_acc)
    sw_acc[...] = jnp.zeros_like(sw_acc)
    col[...] = as_column(ids_row(meta))
    got[0].wait()
    own_pair(v_own, col, ids_row(meta), row_acc, col_acc)
    got[1].wait()

    @pl.when(core_ref[0] == 1)
    def _():
        pair(v_own, 0, ROWS, col, v_sw, 0, ROWS, ids_row(meta_sw), weight_of(meta_sw, 1), row_acc, 0, sw_acc, 0)

    own_out[...] = fold_rows(row_acc) + fold_cols(col_acc)
    sw_out[...] = fold_cols(sw_acc)


def stage1_kernel(
    core_ref, meta, meta_sw, meta_m, meta_p, own, sw, m0, p0, own_in, sw_in,
    own_out, sw_out, m_out, p_out,
    v_own, v_sw, v_m, v_p, m_col, p_col, own_acc, sw_acc, m_acc, p_acc, p_row_acc, sems,
):
    got = fetch([(m0, v_m, sems.at[0]), (own, v_own, sems.at[1]), (p0, v_p, sems.at[2]), (sw, v_sw, sems.at[3])])
    for acc in (own_acc, sw_acc, m_acc, p_acc, p_row_acc):
        acc[...] = jnp.zeros_like(acc)
    m_col[...] = as_column(ids_row(meta_m, 0))
    p_col[...] = as_column(ids_row(meta_p, 0))
    got[0].wait()
    got[1].wait()
    pair(v_m, 0, PART, m_col, v_own, 0, ROWS, ids_row(meta), weight_of(meta_m, 2), m_acc, 0, own_acc, 0)
    got[2].wait()
    pair(v_m, 0, PART, m_col, v_p, 0, PART, ids_row(meta_p, 0), weight_of(meta_m, 4), m_acc, 0, p_acc, 0)
    got[3].wait()

    @pl.when(core_ref[0] == 0)
    def _():
        pair(v_m, 0, PART, m_col, v_sw, 0, ROWS, ids_row(meta_sw), weight_of(meta_m, 3), m_acc, 0, sw_acc, 0)
        pair(v_p, 0, PART, p_col, v_sw, 0, ROWS, ids_row(meta_sw), weight_of(meta_sw, 1), p_row_acc, 0, sw_acc, 0)

    own_out[...] = own_in[...] + fold_cols(own_acc)
    sw_out[...] = sw_in[...] + fold_cols(sw_acc)
    m_out[...] = fold_rows(m_acc)
    p_out[...] = fold_cols(p_acc) + fold_rows(p_row_acc)


def stage2_kernel(
    core_ref, meta, meta_sw, meta_m, meta_p, meta_x, own, sw, m0, p0, x0, m1, p1, own_in, sw_in, m_in, p_in,
    own_out, sw_out, m_out, p_out, x_out,
    v_own, v_sw, v_m, v_p, v_x, m_col, p_col, own_acc, sw_acc, m_acc, p_acc, p_row_acc, x_acc, sems,
):
    first, second = pl.ds(0, PART), pl.ds(PART, PART)
    got = fetch([
        (m1, v_m.at[second, :], sems.at[0]), (own, v_own, sems.at[1]), (p0, v_p.at[first, :], sems.at[2]),
        (p1, v_p.at[second, :], sems.at[3]), (m0, v_m.at[first, :], sems.at[4]),
        (sw, v_sw, sems.at[5]), (x0, v_x, sems.at[6]),
    ])
    for acc in (own_acc, sw_acc, m_acc, p_acc, p_row_acc, x_acc):
        acc[...] = jnp.zeros_like(acc)
    m_col[...] = as_column(ids_row(meta_m))
    p_col[...] = as_column(ids_row(meta_p, 1))
    m_col1 = m_col.at[second, :]
    got[0].wait()
    got[1].wait()
    pair(v_m, PART, PART, m_col1, v_own, 0, ROWS, ids_row(meta), weight_of(meta_m, 2), m_acc, PART, own_acc, 0)
    got[2].wait()
    got[3].wait()
    w_mp = weight_of(meta_m, 4)
    pair(v_m, PART, PART, m_col1, v_p, 0, ROWS, ids_row(meta_p), w_mp, m_acc, PART, p_acc, 0)
    got[4].wait()
    pair(v_m, 0, PART, m_col, v_p, PART, PART, ids_row(meta_p, 1), w_mp, m_acc, 0, p_acc, PART)
    got[5].wait()
    got[6].wait()

    @pl.when(core_ref[0] == 0)
    def _():
        pair(v_m, PART, PART, m_col1, v_sw, 0, ROWS, ids_row(meta_sw), weight_of(meta_m, 3), m_acc, PART, sw_acc, 0)
        pair(v_p, PART, PART, p_col, v_sw, 0, ROWS, ids_row(meta_sw), weight_of(meta_sw, 1), p_row_acc, PART, sw_acc, 0)

    @pl.when(core_ref[0] == 1)
    def _():
        pair(v_m, 0, ROWS, m_col, v_x, 0, PART, ids_row(meta_x, 0), weight_of(meta_m, 3), m_acc, 0, x_acc, 0)

    own_out[...] = own_in[...] + fold_cols(own_acc)
    sw_out[...] = sw_in[...] + fold_cols(sw_acc)
    m_out[...] = fold_rows(m_acc)
    m_out[:, 0:PART] = m_out[:, 0:PART] + m_in[...]
    p_out[...] = fold_cols(p_acc) + fold_rows(p_row_acc)
    p_out[:, 0:PART] = p_out[:, 0:PART] + p_in[...]
    x_out[...] = fold_cols(x_acc)


def stage3_kernel(core_ref, meta_m, meta_x, m0, m1, x1, m_in, m_out, x_out, v_m, v_x, m_col, m_acc, x_acc, sems):
    m_out[...] = m_in[...]
    x_out[...] = jnp.zeros_like(x_out)

    @pl.when(core_ref[0] == 1)
    def _():
        first, second = pl.ds(0, PART), pl.ds(PART, PART)
        got = fetch([(m0, v_m.at[first, :], sems.at[0]), (m1, v_m.at[second, :], sems.at[1]), (x1, v_x, sems.at[2])])
        m_acc[...] = jnp.zeros_like(m_acc)
        x_acc[...] = jnp.zeros_like(x_acc)
        m_col[...] = as_column(ids_row(meta_m))
        for copy in got:
            copy.wait()
        pair(v_m, 0, ROWS, m_col, v_x, 0, PART, ids_row(meta_x, 1), weight_of(meta_m, 3), m_acc, 0, x_acc, 0)
        m_out[...] = m_in[...] + fold_rows(m_acc)
        x_out[...] = fold_cols(x_acc)


def end_kernel(land_ref, *refs):
    out_ref = refs[-1]
    load = refs[0][...]
    for ref in refs[1:-1]:
        load = load + ref[...]
    result = 1.0 / (1.0 + load)
    high = result.astype(BF16).astype(F32)
    mid = (result - high).astype(BF16).astype(F32)
    low = result - high - mid
    which = iota((8, ROWS), 0)
    parts = jnp.where(which == 0, high, jnp.where(which == 1, mid, jnp.where(which == 2, low, 0.0))).astype(BF16)
    for step in range(4):
        placed = nt(parts, one_hot(256, step * 256, land_ref[...]))
        out_ref[:, step * 256:(step + 1) * 256] = placed[0:1, :] + placed[1:2, :] + placed[2:3, :]


def vec(n):
    return jax.ShapeDtypeStruct((1, n), F32)


def rows_vmem(n):
    return pltpu.VMEM((n, WIDTH), BF16)


def call(kernel, out_shape, in_specs, scratch, tasks, args, mib=40):
    single = not isinstance(out_shape, (list, tuple))
    return pl.pallas_call(
        kernel,
        out_shape=out_shape,
        in_specs=in_specs,
        out_specs=VMEM if single else [VMEM] * len(out_shape),
        scratch_shapes=scratch,
        compiler_params=pltpu.CompilerParams(vmem_limit_bytes=mib << 20),
        cost_estimate=pl.CostEstimate(
            flops=int(tasks * 2 * ROWS * ROWS * WIDTH),
            transcendentals=int(tasks * ROWS * ROWS),
            bytes_accessed=int((1 + tasks) * 2 * ROWS * WIDTH),
        ),
    )(*args)


def move(value, devices, change, only=None):
    pairs = [
        (p, change(p))
        for p in range(devices)
        if 0 <= change(p) < devices and (only is None or p % 2 == only)
    ]
    return lax.ppermute(value, AXES, pairs)


def local(embeddings, sorted_slot, cluster_ids, block_list):
    devices = lax.axis_size(AXES)
    position = lax.axis_index(AXES)
    core = (position % 2).astype(jnp.int32).reshape(1)
    SMEM = pl.BlockSpec(memory_space=pltpu.SMEM)
    move_d = functools.partial(move, devices=devices)
    acc_rows, acc_cols = (lambda n: pltpu.VMEM((n, LANES), F32)), (lambda n: pltpu.VMEM((8, n), F32))
    sems = lambda n: pltpu.SemaphoreType.DMA((n,))

    outgoing, land_out = call(
        functools.partial(front_kernel, devices),
        [jax.ShapeDtypeStruct((ROWS, WIDTH), BF16), jax.ShapeDtypeStruct((1, ROWS), jnp.int32)],
        [VMEM, VMEM], [rows_vmem(ROWS)], 1, (embeddings, sorted_slot.reshape(1, ROWS)),
    )
    own = lax.all_to_all(outgoing, AXES, split_axis=0, concat_axis=0, tiled=True)
    land = lax.all_to_all(
        land_out.reshape(devices, ROWS // devices), AXES, split_axis=0, concat_axis=0, tiled=True
    ).reshape(1, ROWS)
    reach = position + 1 + jnp.arange(SHIFTS, dtype=jnp.int32)
    entries = jnp.pad(jnp.where(reach[None, :] < devices, block_list, 0), ((0, 0), (0, LANES - SHIFTS)))
    meta = call(
        meta_kernel, jax.ShapeDtypeStruct((1, ROWS + LANES), jnp.int32), [VMEM] * 3, [], 0.2,
        (land, cluster_ids.reshape(1, ROWS), entries),
    )
    swap = lambda p: p ^ 1
    up, down = (lambda p: p + 2), (lambda p: p - 2)
    meta_sw = move_d(meta, change=swap)
    meta_m = move_d(meta, change=up)
    meta_p = move_d(meta, change=down)
    meta_x = move_d(meta_p, change=swap, only=0)

    sw = move_d(own, change=swap)
    halves = [own[i * PART:(i + 1) * PART] for i in range(CHUNKS)]
    m = [move_d(h, change=up) for h in halves]
    p = [move_d(h, change=down) for h in halves]
    x = [move_d(h, change=swap, only=0) for h in p]

    own_s, sw_s = call(
        stage0_kernel, [vec(ROWS)] * 2, [SMEM] + [VMEM] * 2 + [ANY] * 2,
        [rows_vmem(ROWS)] * 2 + [acc_rows(ROWS)] * 2 + [acc_cols(ROWS)] * 2 + [sems(2)],
        1.6, (core, meta, meta_sw, own, sw),
    )
    own_s, sw_s, m_s, p_s = call(
        stage1_kernel, [vec(ROWS)] * 2 + [vec(PART)] * 2, [SMEM] + [VMEM] * 4 + [ANY] * 4 + [VMEM] * 2,
        [rows_vmem(ROWS)] * 2 + [rows_vmem(PART)] * 2 + [acc_rows(PART)] * 2
        + [acc_cols(ROWS)] * 2 + [acc_rows(PART), acc_cols(PART), acc_rows(PART)] + [sems(4)],
        1.7, (core, meta, meta_sw, meta_m, meta_p, own, sw, m[0], p[0], own_s, sw_s),
    )
    own_s, sw_s, m_s, p_s, x_s = call(
        stage2_kernel, [vec(ROWS)] * 4 + [vec(PART)], [SMEM] + [VMEM] * 5 + [ANY] * 7 + [VMEM] * 4,
        [rows_vmem(ROWS)] * 4 + [rows_vmem(PART)] + [acc_rows(ROWS), acc_rows(PART)]
        + [acc_cols(ROWS)] * 2 + [acc_rows(ROWS), acc_cols(ROWS), acc_rows(ROWS), acc_cols(PART)] + [sems(7)],
        2.2, (core, meta, meta_sw, meta_m, meta_p, meta_x, own, sw, m[0], p[0], x[0], m[1], p[1], own_s, sw_s, m_s, p_s),
    )
    m_s, x_s1 = call(
        stage3_kernel, [vec(ROWS), vec(PART)], [SMEM] + [VMEM] * 2 + [ANY] * 3 + [VMEM],
        [rows_vmem(ROWS), rows_vmem(PART), acc_rows(ROWS), acc_rows(ROWS), acc_cols(PART), sems(3)],
        0.5, (core, meta_m, meta_x, m[0], m[1], x[1], m_s),
    )
    x_all = jnp.concatenate([x_s, x_s1], axis=1)
    returned = [
        own_s,
        move_d(sw_s, change=swap),
        move_d(p_s, change=up),
        move_d(m_s, change=down),
        move_d(x_all, change=lambda q: q + 1, only=1),
    ]
    weights = call(end_kernel, vec(ROWS), [VMEM] * 6, [], 0.2, (land, *returned))
    return weights.reshape(ROWS)


def solution(mesh):
    in_specs = (
        P(("grp", "gr", "gc"), None),
        P(("grp", "gr", "gc")),
        P(("grp", "gr", "gc")),
        P(("grp", "gr", "gc"), None),
    )
    out_specs = P(("grp", "gr", "gc"))
    return jax.shard_map(local, mesh=mesh, in_specs=in_specs, out_specs=out_specs, check_vma=False)
```

```python
import functools
import math

import jax
import jax.numpy as jnp
from jax import lax
from jax.experimental import pallas as pl
from jax.experimental.pallas import tpu as pltpu
from jax.sharding import PartitionSpec as P

SHIFTS = 4
ROWS = 1024
WIDTH = 768
LANES = 128
SIZES = (640, 384)
STARTS = tuple(sum(SIZES[:i]) for i in range(len(SIZES)))
TAIL = 16
DIGITS = 32
AXES = ("gr", "gc")

sharpness = 20.0
threshold = 0.8

F32 = jnp.float32
BF16 = jnp.bfloat16
VMEM = pl.BlockSpec(memory_space=pltpu.VMEM)
ANY = pl.BlockSpec(memory_space=pl.ANY)
HBM = pl.BlockSpec(memory_space=pltpu.HBM)
SMEM = pl.BlockSpec(memory_space=pltpu.SMEM)


def iota(shape, axis):
    return lax.broadcasted_iota(jnp.int32, shape, axis)


def one_hot(rows, first, wanted):
    hit = iota((rows, wanted.shape[1]), 0) + first == wanted
    return jnp.where(hit, 1.0, 0.0).astype(BF16)


def nt(a, b):
    return lax.dot_general(a, b, (((1,), (1,)), ((), ())), preferred_element_type=F32)


def as_column(row):
    return jnp.transpose(jnp.broadcast_to(row, (LANES, row.shape[1])))


def front_kernel(devices, slot_ref, emb_ref, out_ref, raw_ref, unit_ref, sems):
    per_pair = ROWS // devices
    size = 256
    copies = []
    for step in range(ROWS // size):
        part = pl.ds(step * size, size)
        copy = pltpu.make_async_copy(emb_ref.at[part, :], raw_ref.at[part, :], sems.at[step])
        copy.start()
        copies.append(copy)
    slot = slot_ref[...]
    target = slot // ROWS
    low = slot - target * ROWS
    goes = iota((devices, ROWS), 0) == target
    goes_b = jnp.where(goes, 1.0, 0.0).astype(BF16)
    before = jnp.where(iota((ROWS, ROWS), 0) < iota((ROWS, ROWS), 1), 1.0, 0.0).astype(BF16)
    count = jnp.dot(goes_b, before, preferred_element_type=F32)
    rank = jnp.sum(jnp.where(goes, count, 0.0), axis=0, keepdims=True)
    dest = target * per_pair + rank.astype(jnp.int32)
    high = low // DIGITS
    lane = iota((ROWS, LANES), 1)
    digits = jnp.where(
        lane == 0,
        as_column(high.astype(F32)),
        jnp.where(lane == 1, as_column((low - high * DIGITS).astype(F32)), 0.0),
    )
    unit_ref[:, WIDTH:] = digits.astype(BF16)
    for step in range(ROWS // size):
        part = pl.ds(step * size, size)
        copies[step].wait()
        values = raw_ref[part, :].astype(F32)
        mean = jnp.sum(values * values, axis=1, keepdims=True) * (1.0 / WIDTH)
        inverse = lax.rsqrt(mean + 1e-06) * (1.0 / math.sqrt(WIDTH))
        unit_ref[part, 0:WIDTH] = (values * inverse).astype(BF16)
    for step in range(ROWS // size):
        part = pl.ds(step * size, size)
        place = one_hot(size, step * size, dest)
        out_ref[part, :] = jnp.dot(place, unit_ref[...], preferred_element_type=F32).astype(BF16)


def split_kernel(got_ref, ids_ref, list_ref, *outs):
    chunks, land_ref = outs[:-1], outs[-1]
    for size, start, out in zip(SIZES, STARTS, chunks):
        out[0:size, :] = got_ref[start:start + size, 0:WIDTH]
    digits = jnp.transpose(got_ref[:, WIDTH:].astype(F32))
    land = (digits[0:1, :] * DIGITS + digits[1:2, :]).astype(jnp.int32)
    land_ref[...] = land
    ids = jnp.broadcast_to(ids_ref[...].astype(F32), (8, ROWS)).astype(BF16)
    arrived = jnp.zeros((8, ROWS), F32)
    for step in range(4):
        place = one_hot(256, step * 256, land)
        arrived = arrived + jnp.dot(ids[:, step * 256:(step + 1) * 256], place, preferred_element_type=F32)
    entries = jnp.broadcast_to(list_ref[...].astype(F32), (TAIL, LANES)).astype(BF16)
    for size, start, out in zip(SIZES, STARTS, chunks):
        own = jnp.broadcast_to(arrived[0:1, start:start + size], (TAIL, size)).astype(BF16)
        out[size:size + TAIL, 0:WIDTH - LANES] = jnp.zeros((TAIL, WIDTH - LANES), BF16)
        out[size:size + TAIL, 0:size] = own
        out[size:size + TAIL, WIDTH - LANES:] = entries


def weight_of(ref, size, shift):
    entries = ref[size:size + TAIL, WIDTH - LANES:].astype(F32)[0:1, :]
    return jnp.sum(jnp.where(iota((1, LANES), 1) == shift - 1, entries, 0.0), axis=1, keepdims=True)


def ids_row(ref, size):
    return ref[size:size + TAIL, 0:size].astype(F32)[0:1, :]


def tile_terms(scores, id_col, id_row, masked):
    rows, cols = scores.shape
    over_cols, over_rows = None, []
    for lane in range(cols // LANES):
        cut = slice(lane * LANES, (lane + 1) * LANES)
        half = jnp.tanh(scores[:, cut] * (0.5 * sharpness) - 0.5 * sharpness * threshold)
        factor = jnp.where(id_col == id_row[:, cut], 0.5, 0.25)
        term = factor * (1.0 + half)
        if masked:
            term = jnp.where(iota(term.shape, 0) == iota(term.shape, 1) + lane * LANES, 0.0, term)
        over_cols = term if over_cols is None else over_cols + term
        over_rows.append(jnp.sum(term.reshape(rows // 8, 8, LANES), axis=0))
    return over_cols, jnp.concatenate(over_rows, axis=1)


def cuts(size, width):
    return [(at, min(width, size - at)) for at in range(0, size, width)]


def pair(a_ref, a_size, a_col, b_ref, b_size, weight, row_acc, col_acc):
    b_row = ids_row(b_ref, b_size)
    height = 128

    def step(i, carry):
        at = pl.ds(pl.multiple_of(i * height, height), height)
        a = a_ref[at, :]
        col = a_col[at, :]
        total = None
        for start, width in cuts(b_size, 512):
            part = slice(start, start + width)
            by_row, by_col = tile_terms(nt(a, b_ref[part, :]), col, b_row[:, part], False)
            total = by_row if total is None else total + by_row
            col_acc[:, part] = col_acc[:, part] + weight * by_col
        row_acc[at, :] = row_acc[at, :] + weight * total
        return carry

    lax.fori_loop(0, a_size // height, step, 0)


def own_pair(ref, size, col_ref, row_acc, col_acc):
    row = ids_row(ref, size)
    for i, height in cuts(size, 256):
        a = ref[i:i + height, :]
        col = col_ref[i:i + height, :]
        for j, width in cuts(size, 256):
            if j < i:
                continue
            by_row, by_col = tile_terms(nt(a, ref[j:j + width, :]), col, row[:, j:j + width], i == j)
            row_acc[i:i + height, :] = row_acc[i:i + height, :] + by_row
            if j > i:
                col_acc[:, j:j + width] = col_acc[:, j:j + width] + by_col


ROLES = ("own", "sw", "m", "p", "x")


def stage_kernel(blocks, tasks, first, *refs):
    core_ref, refs = refs[0], refs[1:]
    sources, refs = refs[:len(blocks)], refs[len(blocks):]
    sums_in, refs = ((None,) * len(ROLES), refs) if first else (refs[:len(ROLES)], refs[len(ROLES):])
    sums_out, refs = refs[:len(ROLES)], refs[len(ROLES):]
    held, refs = dict(zip(blocks, refs[:len(blocks)])), refs[len(blocks):]
    a_sides, b_sides = sides(tasks)
    cols, refs = dict(zip(a_sides, refs[:len(a_sides)])), refs[len(a_sides):]
    row_acc, refs = dict(zip(a_sides, refs[:len(a_sides)])), refs[len(a_sides):]
    col_acc, refs = dict(zip(b_sides, refs[:len(b_sides)])), refs[len(b_sides):]
    sems = refs[0]

    waiting = {}
    for i, block in enumerate(blocks):
        waiting[block] = pltpu.make_async_copy(sources[i], held[block], sems.at[i])
        waiting[block].start()
    for acc in (*row_acc.values(), *col_acc.values()):
        acc[...] = jnp.zeros_like(acc)
    have_cols = set()

    def need(block):
        if block in waiting:
            waiting.pop(block).wait()

    for core, a, b, holder, shift in tasks:
        for block in (a, b, holder):
            if block is not None:
                need(block)
        if a not in have_cols:
            cols[a][...] = as_column(ids_row(held[a], SIZES[a[1]]))
            have_cols.add(a)

        def run(a=a, b=b, holder=holder, shift=shift):
            if a == b:
                own_pair(held[a], SIZES[a[1]], cols[a], row_acc[a], col_acc[b])
            else:
                weight = 1.0 if holder is None else weight_of(held[holder], SIZES[holder[1]], shift)
                pair(held[a], SIZES[a[1]], cols[a], held[b], SIZES[b[1]], weight, row_acc[a], col_acc[b])

        if core is None:
            run()
        else:
            pl.when(core_ref[0] == core)(run)
    for block in list(waiting):
        need(block)
    for n, role in enumerate(ROLES):
        sums_out[n][...] = jnp.zeros((1, ROWS), F32) if first else sums_in[n][...]
    for accs, fold in ((row_acc, fold_rows), (col_acc, fold_cols)):
        for (role, chunk), acc in accs.items():
            out = sums_out[ROLES.index(role)]
            at = slice(STARTS[chunk], STARTS[chunk] + SIZES[chunk])
            out[:, at] = out[:, at] + fold(acc)


def sides(tasks):
    a_sides, b_sides = [], []
    for _, a, b, _, _ in tasks:
        if a not in a_sides:
            a_sides.append(a)
        if b not in b_sides:
            b_sides.append(b)
    return a_sides, b_sides


def fold_rows(acc):
    return jnp.sum(jnp.transpose(acc[...]), axis=0, keepdims=True)


def fold_cols(acc):
    return jnp.sum(acc[...], axis=0, keepdims=True)


def run_stage(core, arrays, tasks, sums):
    blocks = []
    for _, a, b, holder, _ in tasks:
        for block in (a, b, holder):
            if block is not None and block not in blocks:
                blocks.append(block)
    a_sides, b_sides = sides(tasks)
    scratch = [pltpu.VMEM((SIZES[c] + TAIL, WIDTH), BF16) for _, c in blocks]
    scratch += [pltpu.VMEM((SIZES[c], LANES), F32) for _, c in a_sides] * 2
    scratch += [pltpu.VMEM((8, SIZES[c]), F32) for _, c in b_sides]
    scratch.append(pltpu.SemaphoreType.DMA((len(blocks),)))
    work = sum(SIZES[a[1]] * SIZES[b[1]] * (0.5 if core_of is not None else 1.0) for core_of, a, b, _, _ in tasks) / ROWS**2
    first = sums is None
    return call(
        functools.partial(stage_kernel, blocks, tasks, first), [vec(ROWS)] * len(ROLES),
        [SMEM] + [ANY] * len(blocks) + ([] if first else [VMEM] * len(ROLES)),
        scratch, work, (core, *(arrays[b] for b in blocks), *(() if first else sums)),
    )


def end_kernel(land_ref, *refs):
    out_ref = refs[-1]
    load = refs[0][...]
    for ref in refs[1:-1]:
        load = load + ref[...]
    result = 1.0 / (1.0 + load)
    high = result.astype(BF16).astype(F32)
    mid = (result - high).astype(BF16).astype(F32)
    low = result - high - mid
    which = iota((8, ROWS), 0)
    parts = jnp.where(which == 0, high, jnp.where(which == 1, mid, jnp.where(which == 2, low, 0.0))).astype(BF16)
    for step in range(4):
        placed = nt(parts, one_hot(256, step * 256, land_ref[...]))
        out_ref[:, step * 256:(step + 1) * 256] = placed[0:1, :] + placed[1:2, :] + placed[2:3, :]


def vec(n):
    return jax.ShapeDtypeStruct((1, n), F32)


def call(kernel, out_shape, in_specs, scratch, tasks, args, mib=40):
    single = not isinstance(out_shape, (list, tuple))
    return pl.pallas_call(
        kernel,
        out_shape=out_shape,
        in_specs=in_specs,
        out_specs=VMEM if single else [VMEM] * len(out_shape),
        scratch_shapes=scratch,
        compiler_params=pltpu.CompilerParams(vmem_limit_bytes=mib << 20),
        cost_estimate=pl.CostEstimate(
            flops=int(tasks * 2 * ROWS * ROWS * WIDTH),
            transcendentals=int(tasks * ROWS * ROWS),
            bytes_accessed=int((1 + tasks) * 2 * ROWS * WIDTH),
        ),
    )(*args)


def move(value, devices, change, only=None):
    pairs = [
        (p, change(p))
        for p in range(devices)
        if 0 <= change(p) < devices and (only is None or p % 2 == only)
    ]
    return lax.ppermute(value, AXES, pairs)


def local(embeddings, sorted_slot, cluster_ids, block_list):
    devices = lax.axis_size(AXES)
    position = lax.axis_index(AXES)
    core = (position % 2).astype(jnp.int32).reshape(1)
    move_d = functools.partial(move, devices=devices)
    chunks = range(len(SIZES))

    outgoing = call(
        functools.partial(front_kernel, devices),
        jax.ShapeDtypeStruct((ROWS, WIDTH + LANES), BF16), [VMEM, HBM],
        [pltpu.VMEM((ROWS, WIDTH), BF16), pltpu.VMEM((ROWS, WIDTH + LANES), BF16), pltpu.SemaphoreType.DMA((4,))],
        1, (sorted_slot.reshape(1, ROWS), embeddings),
    )
    arrived = lax.all_to_all(outgoing, AXES, split_axis=0, concat_axis=0, tiled=True)
    reach = position + 1 + jnp.arange(SHIFTS, dtype=jnp.int32)
    entries = jnp.pad(jnp.where(reach[None, :] < devices, block_list, 0), ((0, 0), (0, LANES - SHIFTS)))
    *own, land = call(
        split_kernel,
        [jax.ShapeDtypeStruct((size + TAIL, WIDTH), BF16) for size in SIZES] + [jax.ShapeDtypeStruct((1, ROWS), jnp.int32)],
        [VMEM] * 3, [], 0.3, (arrived, cluster_ids.reshape(1, ROWS), entries),
    )
    swap = lambda p: p ^ 1
    up, down = (lambda p: p + 2), (lambda p: p - 2)
    arrays = {("own", c): own[c] for c in chunks}
    for c in chunks:
        arrays["m", c] = move_d(own[c], change=up)
        arrays["p", c] = move_d(own[c], change=down)
    for c in chunks:
        arrays["sw", c] = move_d(own[c], change=swap)
    for c in chunks:
        arrays["x", c] = move_d(arrays["p", c], change=swap, only=0)

    whole = lambda role: [(role, c) for c in chunks]
    tasks = [(None, ("own", a), ("own", b), None, 0) for a in chunks for b in chunks if a <= b]
    tasks += [(1, a, b, ("sw", 0), 1) for a in whole("own") for b in whole("sw")]
    sums = run_stage(core, arrays, tasks, None)
    for c in chunks:
        m, p = ("m", c), ("p", c)
        tasks = [(None, m, b, m, 2) for b in whole("own")]
        tasks += [(None, m, ("p", d), m, 4) for d in range(c)]
        tasks += [(None, ("m", d), p, m, 4) for d in range(c + 1)]
        tasks += [(0, m, b, m, 3) for b in whole("sw")]
        tasks += [(0, p, b, ("sw", 0), 1) for b in whole("sw")]
        tasks += [(1, ("m", d), ("x", c - 1), m, 3) for d in range(c + 1) if c > 0]
        tasks += [(1, m, ("x", e), m, 3) for e in range(c - 1)]
        sums = run_stage(core, arrays, tasks, sums)
    last = chunks[-1]
    own_s, sw_s, m_s, p_s, x_s = sums
    sw_back, p_back = move_d(sw_s, change=swap), move_d(p_s, change=up)
    tasks = [(1, ("m", d), ("x", last), ("m", last), 3) for d in chunks]
    _, _, m_s, _, x_s = run_stage(core, arrays, tasks, sums)
    returned = [own_s, sw_back, p_back, move_d(m_s, change=down), move_d(x_s, change=lambda q: q + 1, only=1)]
    weights = call(end_kernel, vec(ROWS), [VMEM] * 6, [], 0.2, (land, *returned))
    return weights.reshape(ROWS)


def solution(mesh):
    in_specs = (
        P(("grp", "gr", "gc"), None),
        P(("grp", "gr", "gc")),
        P(("grp", "gr", "gc")),
        P(("grp", "gr", "gc"), None),
    )
    out_specs = P(("grp", "gr", "gc"))
    return jax.shard_map(local, mesh=mesh, in_specs=in_specs, out_specs=out_specs, check_vma=False)
```

```python
import functools
import math

import jax
import jax.numpy as jnp
from jax import lax
from jax.experimental import pallas as pl
from jax.experimental.pallas import tpu as pltpu
from jax.sharding import PartitionSpec as P

SHIFTS = 4
ROWS = 1024
WIDTH = 768
LANES = 128
HINT = 20
SIZES = (768, 256)
STARTS = tuple(sum(SIZES[:i]) for i in range(len(SIZES)))
TAIL = 16
DIGITS = 32
AXES = ("gr", "gc")

sharpness = 20.0
threshold = 0.8

F32 = jnp.float32
BF16 = jnp.bfloat16
VMEM = pl.BlockSpec(memory_space=pltpu.VMEM)
ANY = pl.BlockSpec(memory_space=pl.ANY)
HBM = pl.BlockSpec(memory_space=pltpu.HBM)
SMEM = pl.BlockSpec(memory_space=pltpu.SMEM)


def iota(shape, axis):
    return lax.broadcasted_iota(jnp.int32, shape, axis)


def one_hot(rows, first, wanted):
    hit = iota((rows, wanted.shape[1]), 0) + first == wanted
    return jnp.where(hit, 1.0, 0.0).astype(BF16)


def nt(a, b):
    return lax.dot_general(a, b, (((1,), (1,)), ((), ())), preferred_element_type=F32)


def as_column(row):
    return jnp.transpose(jnp.broadcast_to(row, (LANES, row.shape[1])))


def front_kernel(devices, slot_hbm, emb_ref, out_hbm, slot_ref, raw_ref, unit_ref, out_ref, sems):
    per_pair = ROWS // devices
    size = 256
    parts = [pl.ds(at, size) for at in range(0, ROWS, size)]
    slots = pltpu.make_async_copy(slot_hbm, slot_ref, sems.at[len(parts)])
    slots.start()
    copies = []
    for n, part in enumerate(parts):
        copies.append(pltpu.make_async_copy(emb_ref.at[part, :], raw_ref.at[part, :], sems.at[n]))
        copies[n].start()
    before = jnp.where(iota((ROWS, ROWS), 0) < iota((ROWS, ROWS), 1), 1.0, 0.0).astype(BF16)
    slots.wait()
    slot = slot_ref[...]
    target = slot // ROWS
    low = slot - target * ROWS
    goes = iota((devices, ROWS), 0) == target
    goes_b = jnp.where(goes, 1.0, 0.0).astype(BF16)
    count = jnp.dot(goes_b, before, preferred_element_type=F32)
    rank = jnp.sum(jnp.where(goes, count, 0.0), axis=0, keepdims=True)
    dest = target * per_pair + rank.astype(jnp.int32)
    high = low // DIGITS
    lane = iota((ROWS, LANES), 1)
    digits = jnp.where(
        lane == 0,
        as_column(high.astype(F32)),
        jnp.where(lane == 1, as_column((low - high * DIGITS).astype(F32)), 0.0),
    )
    unit_ref[:, WIDTH:] = digits.astype(BF16)
    for n, part in enumerate(parts):
        copies[n].wait()
        values = raw_ref[part, :].astype(F32)
        mean = jnp.sum(values * values, axis=1, keepdims=True) * (1.0 / WIDTH)
        inverse = lax.rsqrt(mean + 1e-06) * (1.0 / math.sqrt(WIDTH))
        unit_ref[part, 0:WIDTH] = (values * inverse).astype(BF16)
    back = []
    for n, part in enumerate(parts):
        place = one_hot(size, n * size, dest)
        out_ref[part, :] = jnp.dot(place, unit_ref[...], preferred_element_type=F32).astype(BF16)
        back.append(pltpu.make_async_copy(out_ref.at[part, :], out_hbm.at[part, :], sems.at[n]))
        back[n].start()
    for copy in back:
        copy.wait()


def split_kernel(got_ref, ids_ref, list_ref, *outs):
    chunks, land_ref = outs[:-1], outs[-1]
    for size, start, out in zip(SIZES, STARTS, chunks):
        out[0:size, :] = got_ref[start:start + size, 0:WIDTH]
    digits = jnp.transpose(got_ref[:, WIDTH:].astype(F32))
    land = (digits[0:1, :] * DIGITS + digits[1:2, :]).astype(jnp.int32)
    land_ref[...] = land
    ids = jnp.broadcast_to(ids_ref[...].astype(F32), (8, ROWS)).astype(BF16)
    arrived = jnp.zeros((8, ROWS), F32)
    for step in range(4):
        place = one_hot(256, step * 256, land)
        arrived = arrived + jnp.dot(ids[:, step * 256:(step + 1) * 256], place, preferred_element_type=F32)
    entries = list_ref[...].astype(F32)
    for size, start, out in zip(SIZES, STARTS, chunks):
        first = iota((TAIL, LANES), 0) == 0
        for at in range(0, WIDTH, LANES):
            lanes = slice(at, at + LANES)
            own = arrived[0:1, start + at:start + at + LANES] if at < size else jnp.zeros((1, LANES), F32)
            out[size:size + TAIL, lanes] = jnp.where(first, own, entries).astype(BF16)


def weight_of(ref, size, shift):
    entries = ref[size:size + TAIL, 0:LANES].astype(F32)[1:2, :]
    return jnp.sum(jnp.where(iota((1, LANES), 1) == shift - 1, entries, 0.0), axis=1, keepdims=True)


def ids_row(ref, size):
    return ref[size:size + TAIL, 0:size].astype(F32)[0:1, :]


def tile_terms(scores, id_col, id_row, masked):
    rows, cols = scores.shape
    over_cols, over_rows = None, []
    for lane in range(cols // LANES):
        cut = slice(lane * LANES, (lane + 1) * LANES)
        half = jnp.tanh(scores[:, cut] * (0.5 * sharpness) - 0.5 * sharpness * threshold)
        factor = jnp.where(id_col == id_row[:, cut], 0.5, 0.25)
        term = factor * (1.0 + half)
        if masked:
            term = jnp.where(iota(term.shape, 0) == iota(term.shape, 1) + lane * LANES, 0.0, term)
        over_cols = term if over_cols is None else over_cols + term
        over_rows.append(jnp.sum(term.reshape(rows // 8, 8, LANES), axis=0))
    return over_cols, jnp.concatenate(over_rows, axis=1)


def cuts(size, width):
    return [(at, min(width, size - at)) for at in range(0, size, width)]


def pair(a_ref, a_size, a_col, b_ref, b_size, weight, row_acc, col_acc):
    b_row = ids_row(b_ref, b_size)
    for j, width in cuts(b_size, 256):
        part = slice(j, j + width)
        b = b_ref[part, :]
        down = None
        for i, height in cuts(a_size, 256):
            at = slice(i, i + height)
            by_row, by_col = tile_terms(nt(a_ref[at, :], b), a_col[at, :], b_row[:, part], False)
            row_acc[at, :] = row_acc[at, :] + weight * by_row
            down = by_col if down is None else down + by_col
        col_acc[:, part] = col_acc[:, part] + weight * down


def own_pair(ref, size, col_ref, row_acc, col_acc):
    row = ids_row(ref, size)
    for i, height in cuts(size, 256):
        a = ref[i:i + height, :]
        col = col_ref[i:i + height, :]
        for j, width in cuts(size, 256):
            if j < i:
                continue
            by_row, by_col = tile_terms(nt(a, ref[j:j + width, :]), col, row[:, j:j + width], i == j)
            row_acc[i:i + height, :] = row_acc[i:i + height, :] + by_row
            if j > i:
                col_acc[:, j:j + width] = col_acc[:, j:j + width] + by_col


ROLES = ("own", "sw", "m", "p", "x")


def stage_kernel(blocks, tasks, first, *refs):
    core_ref, refs = refs[0], refs[1:]
    sources, refs = refs[:len(blocks)], refs[len(blocks):]
    sums_in, refs = ((None,) * len(ROLES), refs) if first else (refs[:len(ROLES)], refs[len(ROLES):])
    sums_out, refs = refs[:len(ROLES)], refs[len(ROLES):]
    held, refs = dict(zip(blocks, refs[:len(blocks)])), refs[len(blocks):]
    a_sides, b_sides = sides(tasks)
    cols, refs = dict(zip(a_sides, refs[:len(a_sides)])), refs[len(a_sides):]
    row_acc, refs = dict(zip(a_sides, refs[:len(a_sides)])), refs[len(a_sides):]
    col_acc, refs = dict(zip(b_sides, refs[:len(b_sides)])), refs[len(b_sides):]
    sems = refs[0]

    waiting = {}
    for i, block in enumerate(blocks):
        waiting[block] = pltpu.make_async_copy(sources[i], held[block], sems.at[i])
        waiting[block].start()
    for acc in (*row_acc.values(), *col_acc.values()):
        acc[...] = jnp.zeros_like(acc)
    have_cols = set()

    def need(block):
        if block in waiting:
            waiting.pop(block).wait()

    for core, a, b, holder, shift in tasks:
        for block in (a, b, holder):
            if block is not None:
                need(block)
        if a not in have_cols:
            cols[a][...] = as_column(ids_row(held[a], SIZES[a[1]]))
            have_cols.add(a)

        def run(a=a, b=b, holder=holder, shift=shift):
            if a == b:
                own_pair(held[a], SIZES[a[1]], cols[a], row_acc[a], col_acc[b])
            else:
                weight = 1.0 if holder is None else weight_of(held[holder], SIZES[holder[1]], shift)
                pair(held[a], SIZES[a[1]], cols[a], held[b], SIZES[b[1]], weight, row_acc[a], col_acc[b])

        if core is None:
            run()
        else:
            pl.when(core_ref[0] == core)(run)
    for block in list(waiting):
        need(block)
    for n, role in enumerate(ROLES):
        sums_out[n][...] = jnp.zeros((1, ROWS), F32) if first else sums_in[n][...]
    for accs, fold in ((row_acc, fold_rows), (col_acc, fold_cols)):
        for (role, chunk), acc in accs.items():
            out = sums_out[ROLES.index(role)]
            at = slice(STARTS[chunk], STARTS[chunk] + SIZES[chunk])
            out[:, at] = out[:, at] + fold(acc)


def sides(tasks):
    a_sides, b_sides = [], []
    for _, a, b, _, _ in tasks:
        if a not in a_sides:
            a_sides.append(a)
        if b not in b_sides:
            b_sides.append(b)
    return a_sides, b_sides


def fold_rows(acc):
    return jnp.sum(jnp.transpose(acc[...]), axis=0, keepdims=True)


def fold_cols(acc):
    return jnp.sum(acc[...], axis=0, keepdims=True)


def run_stage(core, arrays, tasks, sums):
    blocks = []
    for _, a, b, holder, _ in tasks:
        for block in (a, b, holder):
            if block is not None and block not in blocks:
                blocks.append(block)
    a_sides, b_sides = sides(tasks)
    scratch = [pltpu.VMEM((SIZES[c] + TAIL, WIDTH), BF16) for _, c in blocks]
    scratch += [pltpu.VMEM((SIZES[c], LANES), F32) for _, c in a_sides] * 2
    scratch += [pltpu.VMEM((8, SIZES[c]), F32) for _, c in b_sides]
    scratch.append(pltpu.SemaphoreType.DMA((len(blocks),)))
    work = sum(SIZES[a[1]] * SIZES[b[1]] * (0.5 if core_of is not None else 1.0) for core_of, a, b, _, _ in tasks) / ROWS**2
    first = sums is None
    return call(
        functools.partial(stage_kernel, blocks, tasks, first), [vec(ROWS)] * len(ROLES),
        [SMEM] + [ANY] * len(blocks) + ([] if first else [VMEM] * len(ROLES)),
        scratch, work, (core, *(arrays[b] for b in blocks), *(() if first else sums)),
    )


def end_kernel(land_ref, *refs):
    out_ref = refs[-1]
    load = refs[0][...]
    for ref in refs[1:-1]:
        load = load + ref[...]
    result = 1.0 / (1.0 + load)
    high = result.astype(BF16).astype(F32)
    mid = (result - high).astype(BF16).astype(F32)
    low = result - high - mid
    which = iota((8, ROWS), 0)
    parts = jnp.where(which == 0, high, jnp.where(which == 1, mid, jnp.where(which == 2, low, 0.0))).astype(BF16)
    for step in range(4):
        placed = nt(parts, one_hot(256, step * 256, land_ref[...]))
        out_ref[:, step * 256:(step + 1) * 256] = placed[0:1, :] + placed[1:2, :] + placed[2:3, :]


def vec(n):
    return jax.ShapeDtypeStruct((1, n), F32)


def call(kernel, out_shape, in_specs, scratch, tasks, args, mib=40, out_spec=VMEM):
    single = not isinstance(out_shape, (list, tuple))
    return pl.pallas_call(
        kernel,
        out_shape=out_shape,
        in_specs=in_specs,
        out_specs=out_spec if single else [out_spec] * len(out_shape),
        scratch_shapes=scratch,
        compiler_params=pltpu.CompilerParams(vmem_limit_bytes=mib << 20),
        cost_estimate=pl.CostEstimate(
            flops=int(HINT * tasks * 2 * ROWS * ROWS * WIDTH),
            transcendentals=int(HINT * tasks * ROWS * ROWS),
            bytes_accessed=int(HINT * (1 + tasks) * 2 * ROWS * WIDTH),
        ),
    )(*args)


def move(value, devices, change, only=None):
    pairs = [
        (p, change(p))
        for p in range(devices)
        if 0 <= change(p) < devices and (only is None or p % 2 == only)
    ]
    return lax.ppermute(value, AXES, pairs)


def local(embeddings, sorted_slot, cluster_ids, block_list):
    devices = lax.axis_size(AXES)
    position = lax.axis_index(AXES)
    core = (position % 2).astype(jnp.int32).reshape(1)
    move_d = functools.partial(move, devices=devices)
    chunks = range(len(SIZES))

    outgoing = call(
        functools.partial(front_kernel, devices),
        jax.ShapeDtypeStruct((ROWS, WIDTH + LANES), BF16), [ANY] * 2,
        [pltpu.VMEM((1, ROWS), jnp.int32), pltpu.VMEM((ROWS, WIDTH), BF16)]
        + [pltpu.VMEM((ROWS, WIDTH + LANES), BF16)] * 2 + [pltpu.SemaphoreType.DMA((5,))],
        1, (sorted_slot.reshape(1, ROWS), embeddings), 62, ANY,
    )
    arrived = lax.all_to_all(outgoing, AXES, split_axis=0, concat_axis=0, tiled=True)
    reach = position + 1 + jnp.arange(SHIFTS, dtype=jnp.int32)
    entries = jnp.pad(jnp.where(reach[None, :] < devices, block_list, 0), ((0, 0), (0, LANES - SHIFTS)))
    *own, land = call(
        split_kernel,
        [jax.ShapeDtypeStruct((size + TAIL, WIDTH), BF16) for size in SIZES] + [jax.ShapeDtypeStruct((1, ROWS), jnp.int32)],
        [VMEM] * 3, [], 0.3, (arrived, cluster_ids.reshape(1, ROWS), entries),
    )
    swap = lambda p: p ^ 1
    up, down = (lambda p: p + 2), (lambda p: p - 2)
    arrays = {("own", c): own[c] for c in chunks}
    for c in chunks:
        arrays["sw", c] = move_d(own[c], change=swap)
    for c in chunks:
        sent = own[c]
        if c > 0:
            sent = lax.optimization_barrier((sent, *(arrays["sw", d] for d in chunks)))[0]
        arrays["m", c] = move_d(sent, change=up)
        arrays["p", c] = move_d(sent, change=down)

    whole = lambda role: [(role, c) for c in chunks]
    tasks = [(None, ("own", a), ("own", b), None, 0) for a in chunks for b in chunks if a <= b]
    sums = run_stage(core, arrays, tasks, None)
    tasks = [(1, a, b, ("sw", 0), 1) for a in whole("own") for b in whole("sw")]
    sums = run_stage(core, arrays, tasks, sums)
    for c in chunks:
        m, p = ("m", c), ("p", c)
        relayed = lax.optimization_barrier((arrays[p], *sums))[0]
        arrays["x", c] = move_d(relayed, change=swap, only=0)
        tasks = [(None, m, b, m, 2) for b in whole("own")]
        tasks += [(None, m, ("p", d), m, 4) for d in range(c)]
        tasks += [(None, ("m", d), p, m, 4) for d in range(c + 1)]
        tasks += [(0, m, b, m, 3) for b in whole("sw")]
        tasks += [(0, p, b, ("sw", 0), 1) for b in whole("sw")]
        tasks += [(1, ("m", d), ("x", c - 1), m, 3) for d in range(c + 1) if c > 0]
        tasks += [(1, m, ("x", e), m, 3) for e in range(c - 1)]
        sums = run_stage(core, arrays, tasks, sums)
    last = chunks[-1]
    own_s, sw_s, m_s, p_s, x_s = sums
    sw_back, p_back = move_d(sw_s, change=swap), move_d(p_s, change=up)
    tasks = [(1, ("m", d), ("x", last), ("m", last), 3) for d in chunks]
    _, _, m_s, _, x_s = run_stage(core, arrays, tasks, sums)
    returned = [own_s, sw_back, p_back, move_d(m_s, change=down), move_d(x_s, change=lambda q: q + 1, only=1)]
    weights = call(end_kernel, vec(ROWS), [VMEM] * 6, [], 0.2, (land, *returned))
    return weights.reshape(ROWS)


def solution(mesh):
    in_specs = (
        P(("grp", "gr", "gc"), None),
        P(("grp", "gr", "gc")),
        P(("grp", "gr", "gc")),
        P(("grp", "gr", "gc"), None),
    )
    out_specs = P(("grp", "gr", "gc"))
    return jax.shard_map(local, mesh=mesh, in_specs=in_specs, out_specs=out_specs, check_vma=False)
```

```python
import functools
import math

import jax
import jax.numpy as jnp
from jax import lax
from jax.experimental import pallas as pl
from jax.experimental.pallas import tpu as pltpu
from jax.sharding import PartitionSpec as P

SHIFTS = 4
ROWS = 1024
WIDTH = 768
LANES = 128
HINT = 20
COPIES = 3
APART = 2
PER_PAIR = 16
PIECES = WIDTH // LANES
MESSAGE = (COPIES * PIECES + 1) * PER_PAIR
TAIL = 16
DIGITS = 32
AXES = ("gr", "gc")

sharpness = 20.0
threshold = 0.8

F32 = jnp.float32
BF16 = jnp.bfloat16
VMEM = pl.BlockSpec(memory_space=pltpu.VMEM)
ANY = pl.BlockSpec(memory_space=pl.ANY)
SMEM = pl.BlockSpec(memory_space=pltpu.SMEM)


def iota(shape, axis):
    return lax.broadcasted_iota(jnp.int32, shape, axis)


def one_hot(rows, first, wanted):
    hit = iota((rows, wanted.shape[1]), 0) + first == wanted
    return jnp.where(hit, 1.0, 0.0).astype(BF16)


def nt(a, b):
    return lax.dot_general(a, b, (((1,), (1,)), ((), ())), preferred_element_type=F32)


def as_column(row):
    return jnp.transpose(jnp.broadcast_to(row, (LANES, row.shape[1])))


def front_kernel(devices, slot_hbm, emb_ref, out_hbm, slot_ref, raw_ref, unit_ref, digit_ref, out_ref, sems):
    size = 256
    parts = [pl.ds(at, size) for at in range(0, ROWS, size)]
    slots = pltpu.make_async_copy(slot_hbm, slot_ref, sems.at[len(parts)])
    slots.start()
    copies = []
    for n, part in enumerate(parts):
        copies.append(pltpu.make_async_copy(emb_ref.at[part, :], raw_ref.at[part, :], sems.at[n]))
        copies[n].start()
    before = jnp.where(iota((ROWS, ROWS), 0) < iota((ROWS, ROWS), 1), 1.0, 0.0).astype(BF16)
    slots.wait()
    slot = slot_ref[...]
    target = slot // ROWS
    low = slot - target * ROWS
    goes = iota((devices, ROWS), 0) == target
    goes_b = jnp.where(goes, 1.0, 0.0).astype(BF16)
    count = jnp.dot(goes_b, before, preferred_element_type=F32)
    rank = jnp.sum(jnp.where(goes, count, 0.0), axis=0, keepdims=True)
    dest = target * PER_PAIR + rank.astype(jnp.int32)
    high = low // DIGITS
    even = iota((ROWS, LANES), 1) % 2 == 0
    digits = jnp.where(even, as_column(high.astype(F32)), as_column((low - high * DIGITS).astype(F32)))
    unit_ref[:, WIDTH:] = digits.astype(BF16)
    for n, part in enumerate(parts):
        copies[n].wait()
        values = raw_ref[part, :].astype(F32)
        mean = jnp.sum(values * values, axis=1, keepdims=True) * (1.0 / WIDTH)
        inverse = lax.rsqrt(mean + 1e-06) * (1.0 / math.sqrt(WIDTH))
        unit_ref[part, 0:WIDTH] = (values * inverse).astype(BF16)
    for n, part in enumerate(parts):
        place = one_hot(size, n * size, dest)
        placed = jnp.dot(place, unit_ref[...], preferred_element_type=F32).astype(BF16)
        digit_ref[part, :] = placed[:, WIDTH:]
        for i in range(size // PER_PAIR):
            block = n * (size // PER_PAIR) + i
            rows = placed[i * PER_PAIR:(i + 1) * PER_PAIR, :]
            for copy in range(COPIES):
                at = (block - APART * copy) % devices * MESSAGE + copy * PIECES * PER_PAIR
                for piece in range(PIECES):
                    out_ref[at + piece * PER_PAIR:at + (piece + 1) * PER_PAIR, :] = rows[:, piece * LANES:(piece + 1) * LANES]
    lane = iota((PER_PAIR, LANES), 1) // 2
    for device in range(devices):
        tile = digit_ref[device * PER_PAIR:(device + 1) * PER_PAIR, :]
        for copy in range(1, COPIES):
            at = (device + APART * copy) % devices * PER_PAIR
            tile = jnp.where(lane == copy, digit_ref[at:at + PER_PAIR, :], tile)
        out_ref[(device + 1) * MESSAGE - PER_PAIR:(device + 1) * MESSAGE, :] = tile
    back = []
    for n in range(len(parts)):
        rows = devices * MESSAGE // len(parts)
        back.append(pltpu.make_async_copy(out_ref.at[pl.ds(n * rows, rows), :], out_hbm.at[pl.ds(n * rows, rows), :], sems.at[n]))
        back[n].start()
    for copy in back:
        copy.wait()


def gather_block(got_ref, copy, write):
    for piece in range(PIECES):
        at = (copy * PIECES + piece) * PER_PAIR
        write(slice(piece * LANES, (piece + 1) * LANES), got_ref[:, at:at + PER_PAIR, :].reshape(ROWS, LANES))


def arrival_slots(got_ref):
    digits = got_ref[:, MESSAGE - PER_PAIR:MESSAGE, :].reshape(ROWS, LANES)
    digits = jnp.transpose(digits.astype(F32))[0:8, :]
    return [
        (digits[2 * c:2 * c + 1, :] * DIGITS + digits[2 * c + 1:2 * c + 2, :]).astype(jnp.int32) for c in range(COPIES)
    ]


def arrival_ids(ids, land):
    ids = jnp.broadcast_to(ids.astype(F32), (8, ROWS)).astype(BF16)
    arrived = jnp.zeros((8, ROWS), F32)
    for at in range(0, ROWS, 256):
        place = one_hot(256, at, land)
        arrived = arrived + jnp.dot(ids[:, at:at + 256], place, preferred_element_type=F32)
    return arrived[0:1, :]


def split_kernel(got_ref, ids_ref, list_ref, out_ref, land_ref):
    def write(lanes, rows):
        out_ref[0:ROWS, lanes] = rows

    gather_block(got_ref, 0, write)
    land = arrival_slots(got_ref)[0]
    land_ref[...] = land
    ids = arrival_ids(ids_ref[...], land)
    entries = list_ref[...].astype(F32)
    row = iota((TAIL, LANES), 0)
    for at in range(0, WIDTH, LANES):
        rest = ids[:, at + WIDTH:at + WIDTH + LANES] if at + WIDTH < ROWS else jnp.zeros((1, LANES), F32)
        tail = jnp.where(row == 0, ids[:, at:at + LANES], jnp.where(row == 1, rest, entries))
        out_ref[ROWS:ROWS + TAIL, at:at + LANES] = tail.astype(BF16)


def weight_of(ref, shift):
    entries = ref[ROWS:ROWS + TAIL, 0:LANES].astype(F32)[2:3, :]
    return jnp.sum(jnp.where(iota((1, LANES), 1) == shift - 1, entries, 0.0), axis=1, keepdims=True)


def ids_row(ref):
    tail = ref[ROWS:ROWS + TAIL, :].astype(F32)
    return jnp.concatenate([tail[0:1, :], tail[1:2, 0:ROWS - WIDTH]], axis=1)


def tile_terms(scores, id_col, id_row, masked):
    rows, cols = scores.shape
    over_cols, over_rows = None, []
    for lane in range(cols // LANES):
        cut = slice(lane * LANES, (lane + 1) * LANES)
        half = jnp.tanh(scores[:, cut] * (0.5 * sharpness) - 0.5 * sharpness * threshold)
        factor = jnp.where(id_col == id_row[:, cut], 0.5, 0.25)
        term = factor * (1.0 + half)
        if masked:
            term = jnp.where(iota(term.shape, 0) == iota(term.shape, 1) + lane * LANES, 0.0, term)
        over_cols = term if over_cols is None else over_cols + term
        over_rows.append(jnp.sum(term.reshape(rows // 8, 8, LANES), axis=0))
    return over_cols, jnp.concatenate(over_rows, axis=1)


SIZE = 256
CUTS = [slice(at, at + SIZE) for at in range(0, ROWS, SIZE)]


def pair(a_ref, a_col, b_of, b_row, weight, row_acc):
    over_rows = []
    for part in CUTS:
        b = b_of(part)
        down = None
        for at in CUTS:
            by_row, by_col = tile_terms(nt(a_ref[at, :], b), a_col[at, :], b_row[:, part], False)
            row_acc[at, :] = row_acc[at, :] + weight * by_row
            down = by_col if down is None else down + by_col
        over_rows.append(weight * down)
    return jnp.sum(jnp.concatenate(over_rows, axis=1), axis=0, keepdims=True)


def own_pair(ref, a_col, row, row_acc, col_acc):
    for i, at in enumerate(CUTS):
        a = ref[at, :]
        for j, part in enumerate(CUTS):
            if j < i:
                continue
            by_row, by_col = tile_terms(nt(a, ref[part, :]), a_col[at, :], row[:, part], i == j)
            row_acc[at, :] = row_acc[at, :] + by_row
            if j > i:
                col_acc[:, part] = col_acc[:, part] + by_col


def fold_rows(acc):
    return jnp.sum(jnp.transpose(acc[...]), axis=0, keepdims=True)


def first_kernel(got_ref, own_ref, *refs):
    ids_refs, (blocks_ref, ids_out, sums_ref, col, row_acc, col_acc) = refs[:COPIES - 1], refs[COPIES - 1:]
    blocks_ref[0] = own_ref[0:ROWS, :]
    row = ids_row(own_ref)
    ids_out[0] = row
    col[...] = as_column(row)
    row_acc[...] = jnp.zeros_like(row_acc)
    col_acc[...] = jnp.zeros_like(col_acc)
    own_pair(own_ref, col, row, row_acc, col_acc)
    lands = arrival_slots(got_ref)
    for c in range(1, COPIES):

        def write(lanes, rows, c=c):
            blocks_ref[c, :, lanes] = rows

        gather_block(got_ref, c, write)
        far = arrival_ids(ids_refs[c - 1][...], lands[c])
        ids_out[c] = far
        sums_ref[c] = pair(
            own_ref, col, lambda part, c=c: blocks_ref[c, part, :], far, weight_of(own_ref, APART * c), row_acc
        )
    sums_ref[0] = fold_rows(row_acc) + jnp.sum(col_acc[...], axis=0, keepdims=True)


def second_kernel(core_ref, blocks_ref, ids_ref, sums_ref, sw_ref, *refs):
    outs, (total, col, row_acc) = refs[:COPIES + 1], refs[COPIES + 1:]
    total[...] = sums_ref[...]
    col[...] = as_column(ids_row(sw_ref))
    row_acc[...] = jnp.zeros_like(row_acc)
    for n in range(2):
        which = 1 - core_ref[0] + n
        down = pair(
            sw_ref, col, lambda part: blocks_ref[which, part, :], ids_ref[which], weight_of(sw_ref, 1 + 2 * n), row_acc
        )
        total[which] = total[which] + down
    for c in range(COPIES):
        outs[c][...] = total[c]
    outs[COPIES][...] = fold_rows(row_acc)


def end_kernel(land_ref, *refs):
    out_ref = refs[-1]
    load = refs[0][...]
    for ref in refs[1:-1]:
        load = load + ref[...]
    result = 1.0 / (1.0 + load)
    high = result.astype(BF16).astype(F32)
    mid = (result - high).astype(BF16).astype(F32)
    low = result - high - mid
    which = iota((8, ROWS), 0)
    parts = jnp.where(which == 0, high, jnp.where(which == 1, mid, jnp.where(which == 2, low, 0.0))).astype(BF16)
    for step in range(4):
        placed = nt(parts, one_hot(256, step * 256, land_ref[...]))
        out_ref[:, step * 256:(step + 1) * 256] = placed[0:1, :] + placed[1:2, :] + placed[2:3, :]


def vec(n):
    return jax.ShapeDtypeStruct((1, n), F32)


def call(kernel, out_shape, in_specs, scratch, tasks, args, mib=40, out_spec=VMEM):
    single = not isinstance(out_shape, (list, tuple))
    return pl.pallas_call(
        kernel,
        out_shape=out_shape,
        in_specs=in_specs,
        out_specs=out_spec if single else [out_spec] * len(out_shape),
        scratch_shapes=scratch,
        compiler_params=pltpu.CompilerParams(vmem_limit_bytes=mib << 20),
        cost_estimate=pl.CostEstimate(
            flops=int(HINT * tasks * 2 * ROWS * ROWS * WIDTH),
            transcendentals=int(HINT * tasks * ROWS * ROWS),
            bytes_accessed=int(HINT * (1 + tasks) * 2 * ROWS * WIDTH),
        ),
    )(*args)


def move(value, devices, change, only=None):
    pairs = [
        (p, change(p))
        for p in range(devices)
        if 0 <= change(p) < devices and (only is None or p % 2 == only)
    ]
    return lax.ppermute(value, AXES, pairs)


def local(embeddings, sorted_slot, cluster_ids, block_list):
    devices = lax.axis_size(AXES)
    position = lax.axis_index(AXES)
    core = (position % 2).astype(jnp.int32).reshape(1)
    move_d = functools.partial(move, devices=devices)
    scratch = pltpu.VMEM

    outgoing = call(
        functools.partial(front_kernel, devices),
        jax.ShapeDtypeStruct((devices * MESSAGE, LANES), BF16), [ANY] * 2,
        [scratch((1, ROWS), jnp.int32), scratch((ROWS, WIDTH), BF16), scratch((ROWS, WIDTH + LANES), BF16)]
        + [scratch((ROWS, LANES), BF16), scratch((devices * MESSAGE, LANES), BF16), pltpu.SemaphoreType.DMA((5,))],
        1, (sorted_slot.reshape(1, ROWS), embeddings), 62, ANY,
    )
    arrived = lax.all_to_all(outgoing, AXES, split_axis=0, concat_axis=0, tiled=True)
    got = arrived.reshape(devices, MESSAGE, LANES)
    ids = cluster_ids.reshape(1, ROWS)
    far_ids = [move_d(ids, change=lambda p, c=c: p - APART * c) for c in range(1, COPIES)]
    reach = position + 1 + jnp.arange(SHIFTS, dtype=jnp.int32)
    entries = jnp.pad(jnp.where(reach[None, :] < devices, block_list, 0), ((0, 0), (0, LANES - SHIFTS)))
    own, land = call(
        split_kernel,
        [jax.ShapeDtypeStruct((ROWS + TAIL, WIDTH), BF16), jax.ShapeDtypeStruct((1, ROWS), jnp.int32)],
        [VMEM] * 3, [], 0.3, (got, ids, entries), 16,
    )
    sw = move_d(own, change=lambda p: p ^ 1)
    blocks, block_ids, sums = call(
        first_kernel,
        [jax.ShapeDtypeStruct((COPIES, ROWS, WIDTH), BF16)] + [jax.ShapeDtypeStruct((COPIES, 1, ROWS), F32)] * 2,
        [VMEM] * (COPIES + 1), [scratch((ROWS, LANES), F32)] * 2 + [scratch((8, ROWS), F32)],
        2.6, (got, own, *far_ids), 24,
    )
    sums = call(
        second_kernel, [vec(ROWS)] * (COPIES + 1), [SMEM] + [VMEM] * 4,
        [scratch((COPIES, 1, ROWS), F32)] + [scratch((ROWS, LANES), F32)] * 2,
        2, (core, blocks, block_ids, sums, sw), 24,
    )
    returned = [sums[0], move_d(sums[COPIES], change=lambda p: p ^ 1)]
    returned += [move_d(sums[c], change=lambda p, c=c: p + APART * c) for c in range(1, COPIES)]
    weights = call(end_kernel, vec(ROWS), [VMEM] * (COPIES + 2), [], 0.2, (land, *returned))
    return weights.reshape(ROWS)


def solution(mesh):
    in_specs = (
        P(("grp", "gr", "gc"), None),
        P(("grp", "gr", "gc")),
        P(("grp", "gr", "gc")),
        P(("grp", "gr", "gc"), None),
    )
    out_specs = P(("grp", "gr", "gc"))
    return jax.shard_map(local, mesh=mesh, in_specs=in_specs, out_specs=out_specs, check_vma=False)
```

```python
import functools
import math

import jax
import jax.numpy as jnp
from jax import lax
from jax.experimental import pallas as pl
from jax.experimental.pallas import tpu as pltpu
from jax.sharding import PartitionSpec as P

SHIFTS = 4
ROWS = 1024
WIDTH = 768
LANES = 128
HINT = 20
COPIES = 3
APART = 2
PER_PAIR = 16
PIECES = WIDTH // LANES
MESSAGE = (COPIES * PIECES + 1) * PER_PAIR
TAIL = 16
DIGITS = 32
AXES = ("gr", "gc")

sharpness = 20.0
threshold = 0.8

F32 = jnp.float32
BF16 = jnp.bfloat16
VMEM = pl.BlockSpec(memory_space=pltpu.VMEM)
ANY = pl.BlockSpec(memory_space=pl.ANY)
SMEM = pl.BlockSpec(memory_space=pltpu.SMEM)


def iota(shape, axis):
    return lax.broadcasted_iota(jnp.int32, shape, axis)


def one_hot(rows, first, wanted):
    hit = iota((rows, wanted.shape[1]), 0) + first == wanted
    return jnp.where(hit, 1.0, 0.0).astype(BF16)


def nt(a, b):
    return lax.dot_general(a, b, (((1,), (1,)), ((), ())), preferred_element_type=F32)


def as_column(row):
    return jnp.transpose(jnp.broadcast_to(row, (LANES, row.shape[1])))


def front_kernel(devices, slot_hbm, emb_ref, out_hbm, slot_ref, raw_ref, unit_ref, digit_ref, out_ref, sems):
    size = 256
    parts = [pl.ds(at, size) for at in range(0, ROWS, size)]
    slots = pltpu.make_async_copy(slot_hbm, slot_ref, sems.at[len(parts)])
    slots.start()
    copies = []
    for n, part in enumerate(parts):
        copies.append(pltpu.make_async_copy(emb_ref.at[part, :], raw_ref.at[part, :], sems.at[n]))
        copies[n].start()
    before = jnp.where(iota((ROWS, ROWS), 0) < iota((ROWS, ROWS), 1), 1.0, 0.0).astype(BF16)
    slots.wait()
    slot = slot_ref[...]
    target = slot // ROWS
    low = slot - target * ROWS
    goes = iota((devices, ROWS), 0) == target
    goes_b = jnp.where(goes, 1.0, 0.0).astype(BF16)
    count = jnp.dot(goes_b, before, preferred_element_type=F32)
    rank = jnp.sum(jnp.where(goes, count, 0.0), axis=0, keepdims=True)
    dest = target * PER_PAIR + rank.astype(jnp.int32)
    high = low // DIGITS
    even = iota((ROWS, LANES), 1) % 2 == 0
    digits = jnp.where(even, as_column(high.astype(F32)), as_column((low - high * DIGITS).astype(F32)))
    unit_ref[:, WIDTH:] = digits.astype(BF16)
    for n, part in enumerate(parts):
        copies[n].wait()
        values = raw_ref[part, :].astype(F32)
        mean = jnp.sum(values * values, axis=1, keepdims=True) * (1.0 / WIDTH)
        inverse = lax.rsqrt(mean + 1e-06) * (1.0 / math.sqrt(WIDTH))
        unit_ref[part, 0:WIDTH] = (values * inverse).astype(BF16)
    reach = APART * (COPIES - 1)
    per_part = size // PER_PAIR
    back = []

    def send(first, count):
        for device in range(first, first + count):
            tile = digit_ref[device * PER_PAIR:(device + 1) * PER_PAIR, :]
            for copy in range(1, COPIES):
                at = (device + APART * copy) % devices * PER_PAIR
                tile = jnp.where(lane == copy, digit_ref[at:at + PER_PAIR, :], tile)
            out_ref[(device + 1) * MESSAGE - PER_PAIR:(device + 1) * MESSAGE, :] = tile
        rows = pl.ds(first * MESSAGE, count * MESSAGE)
        back.append(pltpu.make_async_copy(out_ref.at[rows, :], out_hbm.at[rows, :], sems.at[len(back)]))
        back[-1].start()

    lane = iota((PER_PAIR, LANES), 1) // 2
    for n, part in enumerate(parts):
        place = one_hot(size, n * size, dest)
        placed = jnp.dot(place, unit_ref[...], preferred_element_type=F32).astype(BF16)
        digit_ref[part, :] = placed[:, WIDTH:]
        for i in range(per_part):
            block = n * per_part + i
            rows = placed[i * PER_PAIR:(i + 1) * PER_PAIR, :]
            for copy in range(COPIES):
                at = (block - APART * copy) % devices * MESSAGE + copy * PIECES * PER_PAIR
                for piece in range(PIECES):
                    out_ref[at + piece * PER_PAIR:at + (piece + 1) * PER_PAIR, :] = rows[:, piece * LANES:(piece + 1) * LANES]
        if n == 0:
            send(0, per_part - reach)
        else:
            send(n * per_part - reach, per_part)
    send(devices - reach, reach)
    for copy in back:
        copy.wait()


def tiles(got_hbm, copy, target, sem):
    started = []
    for piece in range(PIECES):
        at = (copy * PIECES + piece) * PER_PAIR
        lanes = pl.ds(piece * LANES, LANES)
        started.append(pltpu.make_async_copy(got_hbm.at[:, pl.ds(at, PER_PAIR), :], target.at[:, :, lanes], sem.at[piece]))
        started[-1].start()
    return started


def slot_tiles(got_hbm, target, sem):
    copy = pltpu.make_async_copy(got_hbm.at[:, pl.ds(MESSAGE - PER_PAIR, PER_PAIR), :], target, sem)
    copy.start()
    return copy


def arrival_slots(digits, copies):
    digits = jnp.transpose(digits.reshape(ROWS, LANES).astype(F32))[0:8, :]
    return [(digits[2 * c:2 * c + 1, :] * DIGITS + digits[2 * c + 1:2 * c + 2, :]).astype(jnp.int32) for c in copies]


def arrival_ids(ids, land):
    ids = jnp.broadcast_to(ids.astype(F32), (8, ROWS)).astype(BF16)
    arrived = jnp.zeros((8, ROWS), F32)
    for at in range(0, ROWS, 256):
        place = one_hot(256, at, land)
        arrived = arrived + jnp.dot(ids[:, at:at + 256], place, preferred_element_type=F32)
    return arrived[0:1, :]


def split_kernel(got_hbm, ids_ref, list_ref, out_ref, land_ref, digit_ref, row_ref, sems):
    slots = slot_tiles(got_hbm, digit_ref, sems.at[PIECES])
    rows = tiles(got_hbm, 0, row_ref, sems)
    slots.wait()
    land = arrival_slots(digit_ref[...], (0,))[0]
    land_ref[...] = land
    ids = arrival_ids(ids_ref[...], land)
    entries = list_ref[...].astype(F32)
    row = iota((TAIL, LANES), 0)
    for at in range(0, WIDTH, LANES):
        rest = ids[:, at + WIDTH:at + WIDTH + LANES] if at + WIDTH < ROWS else jnp.zeros((1, LANES), F32)
        tail = jnp.where(row == 0, ids[:, at:at + LANES], jnp.where(row == 1, rest, entries))
        out_ref[ROWS:ROWS + TAIL, at:at + LANES] = tail.astype(BF16)
    for copy in rows:
        copy.wait()
    out_ref[0:ROWS, :] = row_ref[...].reshape(ROWS, WIDTH)


def weight_of(ref, shift):
    entries = ref[ROWS:ROWS + TAIL, 0:LANES].astype(F32)[2:3, :]
    return jnp.sum(jnp.where(iota((1, LANES), 1) == shift - 1, entries, 0.0), axis=1, keepdims=True)


def ids_row(ref):
    tail = ref[ROWS:ROWS + TAIL, :].astype(F32)
    return jnp.concatenate([tail[0:1, :], tail[1:2, 0:ROWS - WIDTH]], axis=1)


def tile_terms(scores, id_col, id_row, masked):
    rows, cols = scores.shape
    over_cols, over_rows = None, []
    for lane in range(cols // LANES):
        cut = slice(lane * LANES, (lane + 1) * LANES)
        half = jnp.tanh(scores[:, cut] * (0.5 * sharpness) - 0.5 * sharpness * threshold)
        factor = jnp.where(id_col == id_row[:, cut], 0.5, 0.25)
        term = factor * (1.0 + half)
        if masked:
            term = jnp.where(iota(term.shape, 0) == iota(term.shape, 1) + lane * LANES, 0.0, term)
        over_cols = term if over_cols is None else over_cols + term
        over_rows.append(jnp.sum(term.reshape(rows // 8, 8, LANES), axis=0))
    return over_cols, jnp.concatenate(over_rows, axis=1)


SIZE = 256
CUTS = [slice(at, at + SIZE) for at in range(0, ROWS, SIZE)]


def pair(a_ref, a_col, b_of, b_row, weight, row_acc):
    over_rows = []
    for part in CUTS:
        b = b_of(part)
        down = None
        for at in CUTS:
            by_row, by_col = tile_terms(nt(a_ref[at, :], b), a_col[at, :], b_row[:, part], False)
            row_acc[at, :] = row_acc[at, :] + weight * by_row
            down = by_col if down is None else down + by_col
        over_rows.append(weight * down)
    return jnp.sum(jnp.concatenate(over_rows, axis=1), axis=0, keepdims=True)


def own_pair(ref, a_col, row, row_acc, col_acc):
    for i, at in enumerate(CUTS):
        a = ref[at, :]
        for j, part in enumerate(CUTS):
            if j < i:
                continue
            by_row, by_col = tile_terms(nt(a, ref[part, :]), a_col[at, :], row[:, part], i == j)
            row_acc[at, :] = row_acc[at, :] + by_row
            if j > i:
                col_acc[:, part] = col_acc[:, part] + by_col


def fold_rows(acc):
    return jnp.sum(jnp.transpose(acc[...]), axis=0, keepdims=True)


def first_kernel(devices, got_hbm, own_ref, *refs):
    ids_refs, (blocks_ref, ids_out, sums_ref, col, row_acc, col_acc, digit_ref, sems) = refs[:COPIES - 1], refs[COPIES - 1:]
    slots = slot_tiles(got_hbm, digit_ref, sems.at[0, PIECES])
    rows = [tiles(got_hbm, c, blocks_ref.at[c], sems.at[c]) for c in range(1, COPIES)]
    blocks_ref[0] = own_ref[0:ROWS, :].reshape(devices, PER_PAIR, WIDTH)
    row = ids_row(own_ref)
    ids_out[0] = row
    col[...] = as_column(row)
    row_acc[...] = jnp.zeros_like(row_acc)
    col_acc[...] = jnp.zeros_like(col_acc)
    own_pair(own_ref, col, row, row_acc, col_acc)
    slots.wait()
    lands = arrival_slots(digit_ref[...], range(1, COPIES))
    for c in range(1, COPIES):
        far = arrival_ids(ids_refs[c - 1][...], lands[c - 1])
        ids_out[c] = far
        for copy in rows[c - 1]:
            copy.wait()
        sums_ref[c] = pair(own_ref, col, block_part(blocks_ref, c), far, weight_of(own_ref, APART * c), row_acc)
    sums_ref[0] = fold_rows(row_acc) + jnp.sum(col_acc[...], axis=0, keepdims=True)


def block_part(blocks_ref, which):
    def part(rows):
        at = pl.ds(rows.start // PER_PAIR, SIZE // PER_PAIR)
        return blocks_ref[which, at, :, :].reshape(SIZE, WIDTH)

    return part


def second_kernel(core_ref, blocks_ref, ids_ref, sums_ref, sw_ref, *refs):
    outs, (total, col, row_acc) = refs[:COPIES + 1], refs[COPIES + 1:]
    total[...] = sums_ref[...]
    col[...] = as_column(ids_row(sw_ref))
    row_acc[...] = jnp.zeros_like(row_acc)
    for n in range(2):
        which = 1 - core_ref[0] + n
        down = pair(
            sw_ref, col, block_part(blocks_ref, which), ids_ref[which], weight_of(sw_ref, 1 + 2 * n), row_acc
        )
        total[which] = total[which] + down
    for c in range(COPIES):
        outs[c][...] = total[c]
    outs[COPIES][...] = fold_rows(row_acc)


def end_kernel(land_ref, *refs):
    out_ref = refs[-1]
    load = refs[0][...]
    for ref in refs[1:-1]:
        load = load + ref[...]
    result = 1.0 / (1.0 + load)
    high = result.astype(BF16).astype(F32)
    mid = (result - high).astype(BF16).astype(F32)
    low = result - high - mid
    which = iota((8, ROWS), 0)
    parts = jnp.where(which == 0, high, jnp.where(which == 1, mid, jnp.where(which == 2, low, 0.0))).astype(BF16)
    for step in range(4):
        placed = nt(parts, one_hot(256, step * 256, land_ref[...]))
        out_ref[:, step * 256:(step + 1) * 256] = placed[0:1, :] + placed[1:2, :] + placed[2:3, :]


def vec(n):
    return jax.ShapeDtypeStruct((1, n), F32)


def call(kernel, out_shape, in_specs, scratch, tasks, args, mib=40, out_spec=VMEM):
    single = not isinstance(out_shape, (list, tuple))
    return pl.pallas_call(
        kernel,
        out_shape=out_shape,
        in_specs=in_specs,
        out_specs=out_spec if single else [out_spec] * len(out_shape),
        scratch_shapes=scratch,
        compiler_params=pltpu.CompilerParams(vmem_limit_bytes=mib << 20),
        cost_estimate=pl.CostEstimate(
            flops=int(HINT * tasks * 2 * ROWS * ROWS * WIDTH),
            transcendentals=int(HINT * tasks * ROWS * ROWS),
            bytes_accessed=int(HINT * (1 + tasks) * 2 * ROWS * WIDTH),
        ),
    )(*args)


def move(value, devices, change, only=None):
    pairs = [
        (p, change(p))
        for p in range(devices)
        if 0 <= change(p) < devices and (only is None or p % 2 == only)
    ]
    return lax.ppermute(value, AXES, pairs)


def local(embeddings, sorted_slot, cluster_ids, block_list):
    devices = lax.axis_size(AXES)
    position = lax.axis_index(AXES)
    core = (position % 2).astype(jnp.int32).reshape(1)
    move_d = functools.partial(move, devices=devices)
    scratch = pltpu.VMEM

    outgoing = call(
        functools.partial(front_kernel, devices),
        jax.ShapeDtypeStruct((devices * MESSAGE, LANES), BF16), [ANY] * 2,
        [scratch((1, ROWS), jnp.int32), scratch((ROWS, WIDTH), BF16), scratch((ROWS, WIDTH + LANES), BF16)]
        + [scratch((ROWS, LANES), BF16), scratch((devices * MESSAGE, LANES), BF16), pltpu.SemaphoreType.DMA((5,))],
        1, (sorted_slot.reshape(1, ROWS), embeddings), 62, ANY,
    )
    arrived = lax.all_to_all(outgoing, AXES, split_axis=0, concat_axis=0, tiled=True)
    got = arrived.reshape(devices, MESSAGE, LANES)
    ids = cluster_ids.reshape(1, ROWS)
    far_ids = [move_d(ids, change=lambda p, c=c: p - APART * c) for c in range(1, COPIES)]
    reach = position + 1 + jnp.arange(SHIFTS, dtype=jnp.int32)
    entries = jnp.pad(jnp.where(reach[None, :] < devices, block_list, 0), ((0, 0), (0, LANES - SHIFTS)))
    tile_rows = lambda width: pltpu.VMEM((devices, PER_PAIR, width), BF16)
    sems = pltpu.SemaphoreType.DMA
    own, land = call(
        split_kernel,
        [jax.ShapeDtypeStruct((ROWS + TAIL, WIDTH), BF16), jax.ShapeDtypeStruct((1, ROWS), jnp.int32)],
        [ANY, VMEM, VMEM], [tile_rows(LANES), tile_rows(WIDTH), sems((PIECES + 1,))], 0.3, (got, ids, entries), 16,
    )
    sw = move_d(own, change=lambda p: p ^ 1)
    blocks, block_ids, sums = call(
        functools.partial(first_kernel, devices),
        [jax.ShapeDtypeStruct((COPIES, devices, PER_PAIR, WIDTH), BF16)]
        + [jax.ShapeDtypeStruct((COPIES, 1, ROWS), F32)] * 2,
        [ANY] + [VMEM] * COPIES,
        [scratch((ROWS, LANES), F32)] * 2 + [scratch((8, ROWS), F32), tile_rows(LANES), sems((COPIES, PIECES + 1))],
        2.6, (got, own, *far_ids), 16,
    )
    sums = call(
        second_kernel, [vec(ROWS)] * (COPIES + 1), [SMEM] + [VMEM] * 4,
        [scratch((COPIES, 1, ROWS), F32)] + [scratch((ROWS, LANES), F32)] * 2,
        2, (core, blocks, block_ids, sums, sw), 16,
    )
    returned = [sums[0], move_d(sums[COPIES], change=lambda p: p ^ 1)]
    returned += [move_d(sums[c], change=lambda p, c=c: p + APART * c) for c in range(1, COPIES)]
    weights = call(end_kernel, vec(ROWS), [VMEM] * (COPIES + 2), [], 0.2, (land, *returned))
    return weights.reshape(ROWS)


def solution(mesh):
    in_specs = (
        P(("grp", "gr", "gc"), None),
        P(("grp", "gr", "gc")),
        P(("grp", "gr", "gc")),
        P(("grp", "gr", "gc"), None),
    )
    out_specs = P(("grp", "gr", "gc"))
    return jax.shard_map(local, mesh=mesh, in_specs=in_specs, out_specs=out_specs, check_vma=False)
```

```python
import functools
import math

import jax
import jax.numpy as jnp
from jax import lax
from jax.experimental import pallas as pl
from jax.experimental.pallas import tpu as pltpu
from jax.sharding import PartitionSpec as P

SHIFTS = 4
ROWS = 1024
WIDTH = 768
LANES = 128
HINT = 20
COPIES = 3
APART = 2
PER_PAIR = 16
PIECES = WIDTH // LANES
MESSAGE = (COPIES * PIECES + 1) * PER_PAIR
TAIL = 16
DIGITS = 32
AXES = ("gr", "gc")

sharpness = 20.0
threshold = 0.8

F32 = jnp.float32
BF16 = jnp.bfloat16
VMEM = pl.BlockSpec(memory_space=pltpu.VMEM)
ANY = pl.BlockSpec(memory_space=pl.ANY)
SMEM = pl.BlockSpec(memory_space=pltpu.SMEM)


def iota(shape, axis):
    return lax.broadcasted_iota(jnp.int32, shape, axis)


def one_hot(rows, first, wanted):
    hit = iota((rows, wanted.shape[1]), 0) + first == wanted
    return jnp.where(hit, 1.0, 0.0).astype(BF16)


def nt(a, b):
    return lax.dot_general(a, b, (((1,), (1,)), ((), ())), preferred_element_type=F32)


def as_column(row):
    return jnp.transpose(jnp.broadcast_to(row, (LANES, row.shape[1])))


def front_kernel(devices, slot_hbm, emb_ref, out_hbm, slot_ref, raw_ref, unit_ref, digit_ref, out_ref, sems):
    size = 256
    parts = [pl.ds(at, size) for at in range(0, ROWS, size)]
    slots = pltpu.make_async_copy(slot_hbm, slot_ref, sems.at[len(parts)])
    slots.start()
    copies = []
    for n, part in enumerate(parts):
        copies.append(pltpu.make_async_copy(emb_ref.at[part, :], raw_ref.at[part, :], sems.at[n]))
        copies[n].start()
    before = jnp.where(iota((size, size), 0) < iota((size, size), 1), 1.0, 0.0).astype(BF16)
    slots.wait()
    slot = slot_ref[...]
    target = slot // ROWS
    low = slot - target * ROWS
    goes = iota((devices, ROWS), 0) == target
    goes_b = jnp.where(goes, 1.0, 0.0).astype(BF16)
    seen, ranks = jnp.zeros((devices, 1), F32), []
    for at in range(0, ROWS, size):
        here = goes[:, at:at + size]
        count = jnp.dot(goes_b[:, at:at + size], before, preferred_element_type=F32) + seen
        ranks.append(jnp.sum(jnp.where(here, count, 0.0), axis=0, keepdims=True))
        seen = seen + jnp.sum(jnp.where(here, 1.0, 0.0), axis=1, keepdims=True)
    rank = jnp.concatenate(ranks, axis=1)
    dest = target * PER_PAIR + rank.astype(jnp.int32)
    high = low // DIGITS
    even = iota((ROWS, LANES), 1) % 2 == 0
    digits = jnp.where(even, as_column(high.astype(F32)), as_column((low - high * DIGITS).astype(F32)))
    unit_ref[:, WIDTH:] = digits.astype(BF16)
    for n, part in enumerate(parts):
        copies[n].wait()
        values = raw_ref[part, :].astype(F32)
        mean = jnp.sum(values * values, axis=1, keepdims=True) * (1.0 / WIDTH)
        inverse = lax.rsqrt(mean + 1e-06) * (1.0 / math.sqrt(WIDTH))
        unit_ref[part, 0:WIDTH] = (values * inverse).astype(BF16)
    reach = APART * (COPIES - 1)
    per_part = size // PER_PAIR
    back = []

    def send(first, count):
        for device in range(first, first + count):
            tile = digit_ref[device * PER_PAIR:(device + 1) * PER_PAIR, :]
            for copy in range(1, COPIES):
                at = (device + APART * copy) % devices * PER_PAIR
                tile = jnp.where(lane == copy, digit_ref[at:at + PER_PAIR, :], tile)
            out_ref[(device + 1) * MESSAGE - PER_PAIR:(device + 1) * MESSAGE, :] = tile
        rows = pl.ds(first * MESSAGE, count * MESSAGE)
        back.append(pltpu.make_async_copy(out_ref.at[rows, :], out_hbm.at[rows, :], sems.at[len(back)]))
        back[-1].start()

    lane = iota((PER_PAIR, LANES), 1) // 2
    for n, part in enumerate(parts):
        place = one_hot(size, n * size, dest)
        placed = jnp.dot(place, unit_ref[...], preferred_element_type=F32).astype(BF16)
        digit_ref[part, :] = placed[:, WIDTH:]
        for i in range(per_part):
            block = n * per_part + i
            rows = placed[i * PER_PAIR:(i + 1) * PER_PAIR, :]
            for copy in range(COPIES):
                at = (block - APART * copy) % devices * MESSAGE + copy * PIECES * PER_PAIR
                for piece in range(PIECES):
                    out_ref[at + piece * PER_PAIR:at + (piece + 1) * PER_PAIR, :] = rows[:, piece * LANES:(piece + 1) * LANES]
        if n == 0:
            send(0, per_part - reach)
        else:
            send(n * per_part - reach, per_part)
    send(devices - reach, reach)
    for copy in back:
        copy.wait()


def tiles(got_hbm, copy, target, sem):
    started = []
    for piece in range(PIECES):
        at = (copy * PIECES + piece) * PER_PAIR
        lanes = pl.ds(piece * LANES, LANES)
        started.append(pltpu.make_async_copy(got_hbm.at[:, pl.ds(at, PER_PAIR), :], target.at[:, :, lanes], sem.at[piece]))
        started[-1].start()
    return started


def slot_tiles(got_hbm, target, sem):
    copy = pltpu.make_async_copy(got_hbm.at[:, pl.ds(MESSAGE - PER_PAIR, PER_PAIR), :], target, sem)
    copy.start()
    return copy


def arrival_slots(digits, copies):
    digits = jnp.transpose(digits.reshape(ROWS, LANES).astype(F32))[0:8, :]
    return [(digits[2 * c:2 * c + 1, :] * DIGITS + digits[2 * c + 1:2 * c + 2, :]).astype(jnp.int32) for c in copies]


def arrival_ids(ids, land):
    ids = jnp.broadcast_to(ids.astype(F32), (8, ROWS)).astype(BF16)
    arrived = jnp.zeros((8, ROWS), F32)
    for at in range(0, ROWS, 256):
        place = one_hot(256, at, land)
        arrived = arrived + jnp.dot(ids[:, at:at + 256], place, preferred_element_type=F32)
    return arrived[0:1, :]


def split_kernel(got_hbm, ids_ref, list_ref, out_ref, land_ref, digit_ref, row_ref, sems):
    slots = slot_tiles(got_hbm, digit_ref, sems.at[PIECES])
    rows = tiles(got_hbm, 0, row_ref, sems)
    slots.wait()
    land = arrival_slots(digit_ref[...], (0,))[0]
    land_ref[...] = land
    ids = arrival_ids(ids_ref[...], land)
    entries = list_ref[...].astype(F32)
    row = iota((TAIL, LANES), 0)
    for at in range(0, WIDTH, LANES):
        rest = ids[:, at + WIDTH:at + WIDTH + LANES] if at + WIDTH < ROWS else jnp.zeros((1, LANES), F32)
        tail = jnp.where(row == 0, ids[:, at:at + LANES], jnp.where(row == 1, rest, entries))
        out_ref[ROWS:ROWS + TAIL, at:at + LANES] = tail.astype(BF16)
    for copy in rows:
        copy.wait()
    out_ref[0:ROWS, :] = row_ref[...].reshape(ROWS, WIDTH)


def weight_of(ref, shift):
    entries = ref[ROWS:ROWS + TAIL, 0:LANES].astype(F32)[2:3, :]
    return jnp.sum(jnp.where(iota((1, LANES), 1) == shift - 1, entries, 0.0), axis=1, keepdims=True)


def ids_row(ref):
    tail = ref[ROWS:ROWS + TAIL, :].astype(F32)
    return jnp.concatenate([tail[0:1, :], tail[1:2, 0:ROWS - WIDTH]], axis=1)


def tile_terms(scores, id_col, id_row, masked):
    rows, cols = scores.shape
    over_cols, over_rows = None, []
    for lane in range(cols // LANES):
        cut = slice(lane * LANES, (lane + 1) * LANES)
        half = jnp.tanh(scores[:, cut] * (0.5 * sharpness) - 0.5 * sharpness * threshold)
        factor = jnp.where(id_col == id_row[:, cut], 0.5, 0.25)
        term = factor * (1.0 + half)
        if masked:
            term = jnp.where(iota(term.shape, 0) == iota(term.shape, 1) + lane * LANES, 0.0, term)
        over_cols = term if over_cols is None else over_cols + term
        over_rows.append(jnp.sum(term.reshape(rows // 8, 8, LANES), axis=0))
    return over_cols, jnp.concatenate(over_rows, axis=1)


SIZE = 256
CUTS = [slice(at, at + SIZE) for at in range(0, ROWS, SIZE)]


def pair(a_ref, a_col, b_of, b_row, weight, row_acc, total):
    @pl.when(jnp.sum(weight) > 0.0)
    def _():
        for part in CUTS:
            b = b_of(part)
            down = None
            for at in CUTS:
                by_row, by_col = tile_terms(nt(a_ref[at, :], b), a_col[at, :], b_row[:, part], False)
                row_acc[at, :] = row_acc[at, :] + weight * by_row
                down = by_col if down is None else down + by_col
            total[:, part] = total[:, part] + weight * jnp.sum(down, axis=0, keepdims=True)


def own_pair(ref, a_col, row, row_acc, col_acc):
    for i, at in enumerate(CUTS):
        a = ref[at, :]
        for j, part in enumerate(CUTS):
            if j < i:
                continue
            by_row, by_col = tile_terms(nt(a, ref[part, :]), a_col[at, :], row[:, part], i == j)
            row_acc[at, :] = row_acc[at, :] + by_row
            if j > i:
                col_acc[:, part] = col_acc[:, part] + by_col


def fold_rows(acc):
    return jnp.sum(jnp.transpose(acc[...]), axis=0, keepdims=True)


def first_kernel(devices, got_hbm, own_ref, *refs):
    ids_refs, (blocks_ref, ids_out, sums_ref, col, row_acc, digit_ref, sems) = refs[:COPIES - 1], refs[COPIES - 1:]
    slots = slot_tiles(got_hbm, digit_ref, sems.at[0, PIECES])
    rows = [tiles(got_hbm, c, blocks_ref.at[c], sems.at[c]) for c in range(1, COPIES)]
    blocks_ref[0] = own_ref[0:ROWS, :].reshape(devices, PER_PAIR, WIDTH)
    row = ids_row(own_ref)
    ids_out[0] = row
    col[...] = as_column(row)
    row_acc[...] = jnp.zeros_like(row_acc)
    sums_ref[...] = jnp.zeros_like(sums_ref)
    slots.wait()
    lands = arrival_slots(digit_ref[...], range(1, COPIES))
    for c in range(1, COPIES):
        ids_out[c] = arrival_ids(ids_refs[c - 1][...], lands[c - 1])
        for copy in rows[c - 1]:
            copy.wait()
        pair(
            own_ref, col, block_part(blocks_ref, c), ids_out[c], weight_of(own_ref, APART * c), row_acc, sums_ref.at[c]
        )
    sums_ref[0] = fold_rows(row_acc)


def self_kernel(own_ref, sum_ref, out_ref, col, row_acc, col_acc):
    row = ids_row(own_ref)
    col[...] = as_column(row)
    row_acc[...] = jnp.zeros_like(row_acc)
    col_acc[...] = jnp.zeros_like(col_acc)
    own_pair(own_ref, col, row, row_acc, col_acc)
    out_ref[...] = sum_ref[...] + fold_rows(row_acc) + jnp.sum(col_acc[...], axis=0, keepdims=True)


def block_part(blocks_ref, which):
    def part(rows):
        at = pl.ds(rows.start // PER_PAIR, SIZE // PER_PAIR)
        return blocks_ref[which, at, :, :].reshape(SIZE, WIDTH)

    return part


def second_kernel(core_ref, blocks_ref, ids_ref, sums_ref, sw_ref, *refs):
    outs, (total, col, row_acc) = refs[:COPIES + 1], refs[COPIES + 1:]
    total[...] = sums_ref[...]
    col[...] = as_column(ids_row(sw_ref))
    row_acc[...] = jnp.zeros_like(row_acc)
    for n in range(2):
        which = 1 - core_ref[0] + n
        pair(
            sw_ref, col, block_part(blocks_ref, which), ids_ref[which], weight_of(sw_ref, 1 + 2 * n), row_acc,
            total.at[which],
        )
    for c in range(COPIES):
        outs[c][...] = total[c]
    outs[COPIES][...] = fold_rows(row_acc)


def end_kernel(land_ref, *refs):
    out_ref = refs[-1]
    load = refs[0][...]
    for ref in refs[1:-1]:
        load = load + ref[...]
    result = 1.0 / (1.0 + load)
    high = result.astype(BF16).astype(F32)
    mid = (result - high).astype(BF16).astype(F32)
    low = result - high - mid
    which = iota((8, ROWS), 0)
    parts = jnp.where(which == 0, high, jnp.where(which == 1, mid, jnp.where(which == 2, low, 0.0))).astype(BF16)
    for step in range(4):
        placed = nt(parts, one_hot(256, step * 256, land_ref[...]))
        out_ref[:, step * 256:(step + 1) * 256] = placed[0:1, :] + placed[1:2, :] + placed[2:3, :]


def vec(n):
    return jax.ShapeDtypeStruct((1, n), F32)


def call(kernel, out_shape, in_specs, scratch, tasks, args, mib=40, out_spec=VMEM):
    single = not isinstance(out_shape, (list, tuple))
    return pl.pallas_call(
        kernel,
        out_shape=out_shape,
        in_specs=in_specs,
        out_specs=out_spec if single else [out_spec] * len(out_shape),
        scratch_shapes=scratch,
        compiler_params=pltpu.CompilerParams(vmem_limit_bytes=mib << 20),
        cost_estimate=pl.CostEstimate(
            flops=int(HINT * tasks * 2 * ROWS * ROWS * WIDTH),
            transcendentals=int(HINT * tasks * ROWS * ROWS),
            bytes_accessed=int(HINT * (1 + tasks) * 2 * ROWS * WIDTH),
        ),
    )(*args)


def move(value, devices, change, only=None):
    pairs = [
        (p, change(p))
        for p in range(devices)
        if 0 <= change(p) < devices and (only is None or p % 2 == only)
    ]
    return lax.ppermute(value, AXES, pairs)


def local(embeddings, sorted_slot, cluster_ids, block_list):
    devices = lax.axis_size(AXES)
    position = lax.axis_index(AXES)
    core = (position % 2).astype(jnp.int32).reshape(1)
    move_d = functools.partial(move, devices=devices)
    scratch = pltpu.VMEM

    outgoing = call(
        functools.partial(front_kernel, devices),
        jax.ShapeDtypeStruct((devices * MESSAGE, LANES), BF16), [ANY] * 2,
        [scratch((1, ROWS), jnp.int32), scratch((ROWS, WIDTH), BF16), scratch((ROWS, WIDTH + LANES), BF16)]
        + [scratch((ROWS, LANES), BF16), scratch((devices * MESSAGE, LANES), BF16), pltpu.SemaphoreType.DMA((5,))],
        1, (sorted_slot.reshape(1, ROWS), embeddings), 62, ANY,
    )
    arrived = lax.all_to_all(outgoing, AXES, split_axis=0, concat_axis=0, tiled=True)
    got = arrived.reshape(devices, MESSAGE, LANES)
    ids = cluster_ids.reshape(1, ROWS)
    far_ids = [move_d(ids, change=lambda p, c=c: p - APART * c) for c in range(1, COPIES)]
    reach = position + 1 + jnp.arange(SHIFTS, dtype=jnp.int32)
    entries = jnp.pad(jnp.where(reach[None, :] < devices, block_list, 0), ((0, 0), (0, LANES - SHIFTS)))
    tile_rows = lambda width: pltpu.VMEM((devices, PER_PAIR, width), BF16)
    sems = pltpu.SemaphoreType.DMA
    own, land = call(
        split_kernel,
        [jax.ShapeDtypeStruct((ROWS + TAIL, WIDTH), BF16), jax.ShapeDtypeStruct((1, ROWS), jnp.int32)],
        [ANY, VMEM, VMEM], [tile_rows(LANES), tile_rows(WIDTH), sems((PIECES + 1,))], 0.3, (got, ids, entries), 16,
    )
    sw = move_d(own, change=lambda p: p ^ 1)
    blocks, block_ids, sums = call(
        functools.partial(first_kernel, devices),
        [jax.ShapeDtypeStruct((COPIES, devices, PER_PAIR, WIDTH), BF16)]
        + [jax.ShapeDtypeStruct((COPIES, 1, ROWS), F32)] * 2,
        [ANY] + [VMEM] * COPIES,
        [scratch((ROWS, LANES), F32)] * 2 + [tile_rows(LANES), sems((COPIES, PIECES + 1))],
        2, (got, own, *far_ids), 16,
    )
    sums = call(
        second_kernel, [vec(ROWS)] * (COPIES + 1), [SMEM] + [VMEM] * 4,
        [scratch((COPIES, 1, ROWS), F32)] + [scratch((ROWS, LANES), F32)] * 2,
        2, (core, blocks, block_ids, sums, sw), 16,
    )
    own_sum = call(
        self_kernel, vec(ROWS), [VMEM] * 2, [scratch((ROWS, LANES), F32)] * 2 + [scratch((8, ROWS), F32)],
        0.6, (own, sums[0]), 16,
    )
    returned = [own_sum, move_d(sums[COPIES], change=lambda p: p ^ 1)]
    returned += [move_d(sums[c], change=lambda p, c=c: p + APART * c) for c in range(1, COPIES)]
    weights = call(end_kernel, vec(ROWS), [VMEM] * (COPIES + 2), [], 0.2, (land, *returned))
    return weights.reshape(ROWS)


def solution(mesh):
    in_specs = (
        P(("grp", "gr", "gc"), None),
        P(("grp", "gr", "gc")),
        P(("grp", "gr", "gc")),
        P(("grp", "gr", "gc"), None),
    )
    out_specs = P(("grp", "gr", "gc"))
    return jax.shard_map(local, mesh=mesh, in_specs=in_specs, out_specs=out_specs, check_vma=False)
```

```python
import functools
import math

import jax
import jax.numpy as jnp
from jax import lax
from jax.experimental import pallas as pl
from jax.experimental.pallas import tpu as pltpu
from jax.sharding import PartitionSpec as P

SHIFTS = 4
ROWS = 1024
WIDTH = 768
LANES = 128
HINT = 20
COPIES = 3
APART = 2
PER_PAIR = 16
PIECES = WIDTH // LANES
MESSAGE = (COPIES * PIECES + 1) * PER_PAIR
TAIL = 16
DIGITS = 32
AXES = ("gr", "gc")

sharpness = 20.0
threshold = 0.8

F32 = jnp.float32
BF16 = jnp.bfloat16
VMEM = pl.BlockSpec(memory_space=pltpu.VMEM)
ANY = pl.BlockSpec(memory_space=pl.ANY)
SMEM = pl.BlockSpec(memory_space=pltpu.SMEM)


def iota(shape, axis):
    return lax.broadcasted_iota(jnp.int32, shape, axis)


def one_hot(rows, first, wanted):
    hit = iota((rows, wanted.shape[1]), 0) + first == wanted
    return jnp.where(hit, 1.0, 0.0).astype(BF16)


def nt(a, b):
    return lax.dot_general(a, b, (((1,), (1,)), ((), ())), preferred_element_type=F32)


def as_column(row):
    return jnp.transpose(jnp.broadcast_to(row, (LANES, row.shape[1])))


def front_kernel(devices, slot_hbm, emb_ref, out_hbm, slot_ref, raw_ref, unit_ref, digit_ref, out_ref, sems):
    size = 256
    parts = [pl.ds(at, size) for at in range(0, ROWS, size)]
    slots = pltpu.make_async_copy(slot_hbm, slot_ref, sems.at[len(parts)])
    slots.start()
    copies = []
    for n, part in enumerate(parts):
        copies.append(pltpu.make_async_copy(emb_ref.at[part, :], raw_ref.at[part, :], sems.at[n]))
        copies[n].start()
    before = jnp.where(iota((size, size), 0) < iota((size, size), 1), 1.0, 0.0).astype(BF16)
    slots.wait()
    slot = slot_ref[...]
    target = slot // ROWS
    low = slot - target * ROWS
    goes = iota((devices, ROWS), 0) == target
    goes_b = jnp.where(goes, 1.0, 0.0).astype(BF16)
    seen, ranks = jnp.zeros((devices, 1), F32), []
    for at in range(0, ROWS, size):
        here = goes[:, at:at + size]
        count = jnp.dot(goes_b[:, at:at + size], before, preferred_element_type=F32) + seen
        ranks.append(jnp.sum(jnp.where(here, count, 0.0), axis=0, keepdims=True))
        seen = seen + jnp.sum(jnp.where(here, 1.0, 0.0), axis=1, keepdims=True)
    rank = jnp.concatenate(ranks, axis=1)
    dest = target * PER_PAIR + rank.astype(jnp.int32)
    high = low // DIGITS
    even = iota((ROWS, LANES), 1) % 2 == 0
    digits = jnp.where(even, as_column(high.astype(F32)), as_column((low - high * DIGITS).astype(F32)))
    unit_ref[:, WIDTH:] = digits.astype(BF16)
    for n, part in enumerate(parts):
        copies[n].wait()
        values = raw_ref[part, :].astype(F32)
        mean = jnp.sum(values * values, axis=1, keepdims=True) * (1.0 / WIDTH)
        inverse = lax.rsqrt(mean + 1e-06) * (1.0 / math.sqrt(WIDTH))
        unit_ref[part, 0:WIDTH] = (values * inverse).astype(BF16)
    reach = APART * (COPIES - 1)
    per_part = size // PER_PAIR
    back = []

    def send(first, count):
        for device in range(first, first + count):
            tile = digit_ref[device * PER_PAIR:(device + 1) * PER_PAIR, :]
            for copy in range(1, COPIES):
                at = (device + APART * copy) % devices * PER_PAIR
                tile = jnp.where(lane == copy, digit_ref[at:at + PER_PAIR, :], tile)
            out_ref[(device + 1) * MESSAGE - PER_PAIR:(device + 1) * MESSAGE, :] = tile
        rows = pl.ds(first * MESSAGE, count * MESSAGE)
        back.append(pltpu.make_async_copy(out_ref.at[rows, :], out_hbm.at[rows, :], sems.at[len(back)]))
        back[-1].start()

    lane = iota((PER_PAIR, LANES), 1) // 2
    for n, part in enumerate(parts):
        place = one_hot(size, n * size, dest)
        placed = jnp.dot(place, unit_ref[...], preferred_element_type=F32).astype(BF16)
        digit_ref[part, :] = placed[:, WIDTH:]
        for i in range(per_part):
            block = n * per_part + i
            rows = placed[i * PER_PAIR:(i + 1) * PER_PAIR, :]
            for copy in range(COPIES):
                at = (block - APART * copy) % devices * MESSAGE + copy * PIECES * PER_PAIR
                for piece in range(PIECES):
                    out_ref[at + piece * PER_PAIR:at + (piece + 1) * PER_PAIR, :] = rows[:, piece * LANES:(piece + 1) * LANES]
        if n == 0:
            send(0, per_part - reach)
        else:
            send(n * per_part - reach, per_part)
    send(devices - reach, reach)
    for copy in back:
        copy.wait()


def tiles(got_hbm, copy, target, sem):
    started = []
    for piece in range(PIECES):
        at = (copy * PIECES + piece) * PER_PAIR
        lanes = pl.ds(piece * LANES, LANES)
        started.append(pltpu.make_async_copy(got_hbm.at[:, pl.ds(at, PER_PAIR), :], target.at[:, :, lanes], sem.at[piece]))
        started[-1].start()
    return started


def slot_tiles(got_hbm, target, sem):
    copy = pltpu.make_async_copy(got_hbm.at[:, pl.ds(MESSAGE - PER_PAIR, PER_PAIR), :], target, sem)
    copy.start()
    return copy


def arrival_slots(digits, copies):
    digits = jnp.transpose(digits.reshape(ROWS, LANES).astype(F32))[0:8, :]
    return [(digits[2 * c:2 * c + 1, :] * DIGITS + digits[2 * c + 1:2 * c + 2, :]).astype(jnp.int32) for c in copies]


def arrival_ids(ids, land):
    ids = jnp.broadcast_to(ids.astype(F32), (8, ROWS)).astype(BF16)
    arrived = jnp.zeros((8, ROWS), F32)
    for at in range(0, ROWS, 256):
        place = one_hot(256, at, land)
        arrived = arrived + jnp.dot(ids[:, at:at + 256], place, preferred_element_type=F32)
    return arrived[0:1, :]


def split_kernel(got_hbm, list_ref, *refs):
    ids_refs, (out_ref, blocks_ref, far_ref, land_ref, digit_ref, sems) = refs[:COPIES], refs[COPIES:]
    slots = slot_tiles(got_hbm, digit_ref, sems.at[0, PIECES])
    rows = [tiles(got_hbm, c, blocks_ref.at[c], sems.at[c]) for c in range(COPIES)]
    slots.wait()
    lands = arrival_slots(digit_ref[...], range(COPIES))
    land_ref[...] = lands[0]
    for c in range(COPIES):
        far_ref[c] = arrival_ids(ids_refs[c][...], lands[c])
    ids = far_ref[0]
    entries = list_ref[...].astype(F32)
    row = iota((TAIL, LANES), 0)
    for at in range(0, WIDTH, LANES):
        rest = ids[:, at + WIDTH:at + WIDTH + LANES] if at + WIDTH < ROWS else jnp.zeros((1, LANES), F32)
        tail = jnp.where(row == 0, ids[:, at:at + LANES], jnp.where(row == 1, rest, entries))
        out_ref[ROWS:ROWS + TAIL, at:at + LANES] = tail.astype(BF16)
    for copy in rows[0]:
        copy.wait()
    out_ref[0:ROWS, :] = blocks_ref[0].reshape(ROWS, WIDTH)
    for copy in (*rows[1], *rows[2]):
        copy.wait()


def weight_of(ref, shift):
    entries = ref[ROWS:ROWS + TAIL, 0:LANES].astype(F32)[2:3, :]
    return jnp.sum(jnp.where(iota((1, LANES), 1) == shift - 1, entries, 0.0), axis=1, keepdims=True)


def ids_row(ref):
    tail = ref[ROWS:ROWS + TAIL, :].astype(F32)
    return jnp.concatenate([tail[0:1, :], tail[1:2, 0:ROWS - WIDTH]], axis=1)


def tile_terms(scores, id_col, id_row, masked):
    rows, cols = scores.shape
    over_cols, over_rows = None, []
    for lane in range(cols // LANES):
        cut = slice(lane * LANES, (lane + 1) * LANES)
        half = jnp.tanh(scores[:, cut] * (0.5 * sharpness) - 0.5 * sharpness * threshold)
        factor = jnp.where(id_col == id_row[:, cut], 0.5, 0.25)
        term = factor * (1.0 + half)
        if masked:
            term = jnp.where(iota(term.shape, 0) == iota(term.shape, 1) + lane * LANES, 0.0, term)
        over_cols = term if over_cols is None else over_cols + term
        over_rows.append(jnp.sum(term.reshape(rows // 8, 8, LANES), axis=0))
    return over_cols, jnp.concatenate(over_rows, axis=1)


SIZE = 256
CUTS = [slice(at, at + SIZE) for at in range(0, ROWS, SIZE)]


def pair(a_ref, a_col, b_of, b_row, listed, row_acc, col_acc, total):
    @pl.when(jnp.sum(listed) > 0.0)
    def _():
        for part in CUTS:
            b = b_of(part)
            down = None
            for at in CUTS:
                by_row, by_col = tile_terms(nt(a_ref[at, :], b), a_col[at, :], b_row[:, part], False)
                row_acc[at, :] = row_acc[at, :] + by_row
                down = by_col if down is None else down + by_col
            col_acc[:, part] = down
        total[...] = total[...] + jnp.sum(col_acc[...], axis=0, keepdims=True)


def own_pair(ref, a_col, row, row_acc, col_acc):
    for i, at in enumerate(CUTS):
        a = ref[at, :]
        for j, part in enumerate(CUTS):
            if j < i:
                continue
            by_row, by_col = tile_terms(nt(a, ref[part, :]), a_col[at, :], row[:, part], i == j)
            row_acc[at, :] = row_acc[at, :] + by_row
            if j > i:
                col_acc[:, part] = col_acc[:, part] + by_col


def fold_rows(acc):
    return jnp.sum(jnp.transpose(acc[...]), axis=0, keepdims=True)


def first_kernel(own_ref, blocks_ref, ids_ref, sums_ref, col, row_acc, col_acc):
    col[...] = as_column(ids_ref[0])
    row_acc[...] = jnp.zeros_like(row_acc)
    sums_ref[...] = jnp.zeros_like(sums_ref)
    for c in range(1, COPIES):
        pair(
            own_ref, col, block_part(blocks_ref, c), ids_ref[c], weight_of(own_ref, APART * c), row_acc, col_acc,
            sums_ref.at[c],
        )
    sums_ref[0] = fold_rows(row_acc)


def self_kernel(own_ref, sum_ref, out_ref, col, row_acc, col_acc):
    row = ids_row(own_ref)
    col[...] = as_column(row)
    row_acc[...] = jnp.zeros_like(row_acc)
    col_acc[...] = jnp.zeros_like(col_acc)
    own_pair(own_ref, col, row, row_acc, col_acc)
    out_ref[...] = sum_ref[...] + fold_rows(row_acc) + jnp.sum(col_acc[...], axis=0, keepdims=True)


def block_part(blocks_ref, which):
    def part(rows):
        at = pl.ds(rows.start // PER_PAIR, SIZE // PER_PAIR)
        return blocks_ref[which, at, :, :].reshape(SIZE, WIDTH)

    return part


def second_kernel(core_ref, blocks_ref, ids_ref, sums_ref, sw_ref, *refs):
    outs, (total, col, row_acc, col_acc) = refs[:COPIES + 1], refs[COPIES + 1:]
    total[...] = sums_ref[...]
    col[...] = as_column(ids_row(sw_ref))
    row_acc[...] = jnp.zeros_like(row_acc)
    for n in range(2):
        which = 1 - core_ref[0] + n
        pair(
            sw_ref, col, block_part(blocks_ref, which), ids_ref[which], weight_of(sw_ref, 1 + 2 * n), row_acc,
            col_acc, total.at[which],
        )
    for c in range(COPIES):
        outs[c][...] = total[c]
    outs[COPIES][...] = fold_rows(row_acc)


def end_kernel(land_ref, *refs):
    out_ref = refs[-1]
    load = refs[0][...]
    for ref in refs[1:-1]:
        load = load + ref[...]
    result = 1.0 / (1.0 + load)
    high = result.astype(BF16).astype(F32)
    mid = (result - high).astype(BF16).astype(F32)
    low = result - high - mid
    which = iota((8, ROWS), 0)
    parts = jnp.where(which == 0, high, jnp.where(which == 1, mid, jnp.where(which == 2, low, 0.0))).astype(BF16)
    for step in range(4):
        placed = nt(parts, one_hot(256, step * 256, land_ref[...]))
        out_ref[:, step * 256:(step + 1) * 256] = placed[0:1, :] + placed[1:2, :] + placed[2:3, :]


def vec(n):
    return jax.ShapeDtypeStruct((1, n), F32)


def call(kernel, out_shape, in_specs, scratch, tasks, args, mib=40, out_spec=VMEM):
    single = not isinstance(out_shape, (list, tuple))
    return pl.pallas_call(
        kernel,
        out_shape=out_shape,
        in_specs=in_specs,
        out_specs=out_spec if single else [out_spec] * len(out_shape),
        scratch_shapes=scratch,
        compiler_params=pltpu.CompilerParams(vmem_limit_bytes=mib << 20),
        cost_estimate=pl.CostEstimate(
            flops=int(HINT * tasks * 2 * ROWS * ROWS * WIDTH),
            transcendentals=int(HINT * tasks * ROWS * ROWS),
            bytes_accessed=int(HINT * (1 + tasks) * 2 * ROWS * WIDTH),
        ),
    )(*args)


def move(value, devices, change, only=None):
    pairs = [
        (p, change(p))
        for p in range(devices)
        if 0 <= change(p) < devices and (only is None or p % 2 == only)
    ]
    return lax.ppermute(value, AXES, pairs)


def local(embeddings, sorted_slot, cluster_ids, block_list):
    devices = lax.axis_size(AXES)
    position = lax.axis_index(AXES)
    core = (position % 2).astype(jnp.int32).reshape(1)
    move_d = functools.partial(move, devices=devices)
    scratch = pltpu.VMEM

    outgoing = call(
        functools.partial(front_kernel, devices),
        jax.ShapeDtypeStruct((devices * MESSAGE, LANES), BF16), [ANY] * 2,
        [scratch((1, ROWS), jnp.int32), scratch((ROWS, WIDTH), BF16), scratch((ROWS, WIDTH + LANES), BF16)]
        + [scratch((ROWS, LANES), BF16), scratch((devices * MESSAGE, LANES), BF16), pltpu.SemaphoreType.DMA((5,))],
        1, (sorted_slot.reshape(1, ROWS), embeddings), 62, ANY,
    )
    arrived = lax.all_to_all(outgoing, AXES, split_axis=0, concat_axis=0, tiled=True)
    got = arrived.reshape(devices, MESSAGE, LANES)
    ids = cluster_ids.reshape(1, ROWS)
    far_ids = [move_d(ids, change=lambda p, c=c: p - APART * c) for c in range(1, COPIES)]
    reach = position + 1 + jnp.arange(SHIFTS, dtype=jnp.int32)
    entries = jnp.pad(jnp.where(reach[None, :] < devices, block_list, 0), ((0, 0), (0, LANES - SHIFTS)))
    tile_rows = lambda width: pltpu.VMEM((devices, PER_PAIR, width), BF16)
    sems = pltpu.SemaphoreType.DMA
    own, blocks, block_ids, land = call(
        split_kernel,
        [
            jax.ShapeDtypeStruct((ROWS + TAIL, WIDTH), BF16),
            jax.ShapeDtypeStruct((COPIES, devices, PER_PAIR, WIDTH), BF16),
            jax.ShapeDtypeStruct((COPIES, 1, ROWS), F32),
            jax.ShapeDtypeStruct((1, ROWS), jnp.int32),
        ],
        [ANY] + [VMEM] * (1 + COPIES), [tile_rows(LANES), sems((COPIES, PIECES + 1))],
        0.5, (got, entries, ids, *far_ids), 16,
    )
    sw = move_d(own, change=lambda p: p ^ 1)
    sides = [scratch((ROWS, LANES), F32)] * 2 + [scratch((8, ROWS), F32)]
    sums = call(
        first_kernel, jax.ShapeDtypeStruct((COPIES, 1, ROWS), F32), [VMEM] * 3, sides, 2, (own, blocks, block_ids), 16
    )
    sums = call(
        second_kernel, [vec(ROWS)] * (COPIES + 1), [SMEM] + [VMEM] * 4,
        [scratch((COPIES, 1, ROWS), F32)] + sides,
        2, (core, blocks, block_ids, sums, sw), 16,
    )
    own_sum = call(
        self_kernel, vec(ROWS), [VMEM] * 2, sides,
        0.6, (own, sums[0]), 16,
    )
    returned = [own_sum, move_d(sums[COPIES], change=lambda p: p ^ 1)]
    returned += [move_d(sums[c], change=lambda p, c=c: p + APART * c) for c in range(1, COPIES)]
    weights = call(end_kernel, vec(ROWS), [VMEM] * (COPIES + 2), [], 0.2, (land, *returned))
    return weights.reshape(ROWS)


def solution(mesh):
    in_specs = (
        P(("grp", "gr", "gc"), None),
        P(("grp", "gr", "gc")),
        P(("grp", "gr", "gc")),
        P(("grp", "gr", "gc"), None),
    )
    out_specs = P(("grp", "gr", "gc"))
    return jax.shard_map(local, mesh=mesh, in_specs=in_specs, out_specs=out_specs, check_vma=False)
```

```python
import functools
import math

import jax
import jax.numpy as jnp
from jax import lax
from jax.experimental import pallas as pl
from jax.experimental.pallas import tpu as pltpu
from jax.sharding import PartitionSpec as P

SHIFTS = 4
ROWS = 1024
WIDTH = 768
LANES = 128
HINT = 20
COPIES = 3
APART = 2
PER_PAIR = 16
PIECES = WIDTH // LANES
BODY = PIECES * PER_PAIR
HALF = PER_PAIR // 2
MESSAGE = COPIES * BODY + HALF
TAIL = 16
DIGITS = 32
AXES = ("gr", "gc")

sharpness = 20.0
threshold = 0.8

F32 = jnp.float32
BF16 = jnp.bfloat16
VMEM = pl.BlockSpec(memory_space=pltpu.VMEM)
ANY = pl.BlockSpec(memory_space=pl.ANY)
SMEM = pl.BlockSpec(memory_space=pltpu.SMEM)


def iota(shape, axis):
    return lax.broadcasted_iota(jnp.int32, shape, axis)


def one_hot(rows, first, wanted):
    hit = iota((rows, wanted.shape[1]), 0) + first == wanted
    return jnp.where(hit, 1.0, 0.0).astype(BF16)


def nt(a, b):
    return lax.dot_general(a, b, (((1,), (1,)), ((), ())), preferred_element_type=F32)


def as_column(row):
    return jnp.transpose(jnp.broadcast_to(row, (LANES, row.shape[1])))


def front_kernel(devices, slot_hbm, emb_ref, out_hbm, slot_ref, raw_ref, unit_ref, digit_ref, info_ref, rows_ref, sems):
    size = 256
    parts = [pl.ds(at, size) for at in range(0, ROWS, size)]
    slots = pltpu.make_async_copy(slot_hbm, slot_ref, sems.at[len(parts)])
    slots.start()
    copies = []
    for n, part in enumerate(parts):
        copies.append(pltpu.make_async_copy(emb_ref.at[part, :], raw_ref.at[part, :], sems.at[n]))
        copies[n].start()
    before = jnp.where(iota((size, size), 0) < iota((size, size), 1), 1.0, 0.0).astype(BF16)
    slots.wait()
    slot = slot_ref[...]
    target = slot // ROWS
    low = slot - target * ROWS
    goes = iota((devices, ROWS), 0) == target
    goes_b = jnp.where(goes, 1.0, 0.0).astype(BF16)
    seen, ranks = jnp.zeros((devices, 1), F32), []
    for at in range(0, ROWS, size):
        here = goes[:, at:at + size]
        count = jnp.dot(goes_b[:, at:at + size], before, preferred_element_type=F32) + seen
        ranks.append(jnp.sum(jnp.where(here, count, 0.0), axis=0, keepdims=True))
        seen = seen + jnp.sum(jnp.where(here, 1.0, 0.0), axis=1, keepdims=True)
    rank = jnp.concatenate(ranks, axis=1)
    dest = target * PER_PAIR + rank.astype(jnp.int32)
    high = low // DIGITS
    even = iota((ROWS, LANES), 1) % 2 == 0
    digits = jnp.where(even, as_column(high.astype(F32)), as_column((low - high * DIGITS).astype(F32)))
    unit_ref[:, WIDTH:] = digits.astype(BF16)
    for n, part in enumerate(parts):
        copies[n].wait()
        values = raw_ref[part, :].astype(F32)
        mean = jnp.sum(values * values, axis=1, keepdims=True) * (1.0 / WIDTH)
        inverse = lax.rsqrt(mean + 1e-06) * (1.0 / math.sqrt(WIDTH))
        unit_ref[part, 0:WIDTH] = (values * inverse).astype(BF16)
    per_part = size // PER_PAIR
    back = []

    def send(source, target):
        back.append(pltpu.make_async_copy(source, target, sems.at[len(parts) + 1 + len(back)]))
        back[-1].start()

    lane = iota((per_part, HALF, LANES), 2)
    for n, part in enumerate(parts):
        place = one_hot(size, n * size, dest)
        placed = jnp.dot(place, unit_ref[...], preferred_element_type=F32)
        first = n * per_part
        sent = placed[:, WIDTH:].reshape(per_part, PER_PAIR, LANES)
        digit_ref[first:first + per_part] = jnp.where(lane < LANES // 2, sent[:, 0:HALF, :], sent[:, HALF:, :])
        for i in range(per_part):
            rows = placed[i * PER_PAIR:(i + 1) * PER_PAIR, :].astype(BF16)
            for piece in range(PIECES):
                rows_ref[first + i, piece * PER_PAIR:(piece + 1) * PER_PAIR, :] = rows[:, piece * LANES:(piece + 1) * LANES]
        for copy in range(COPIES):
            back_by = APART * copy
            body = pl.ds(copy * BODY, BODY)
            wrapped = max(0, back_by - first)
            if wrapped:
                send(rows_ref.at[pl.ds(first, wrapped)], out_hbm.at[pl.ds(devices - wrapped, wrapped), body, :])
            count = per_part - wrapped
            send(rows_ref.at[pl.ds(first + wrapped, count)], out_hbm.at[pl.ds(first + wrapped - back_by, count), body, :])
    which = iota((devices, HALF, LANES), 2) % (LANES // 2) // 2
    info = digit_ref[...]
    for copy in range(1, COPIES):
        ahead = APART * copy
        far = jnp.concatenate([digit_ref[ahead:], digit_ref[:ahead]], axis=0)
        info = jnp.where(which == copy, far, info)
    info_ref[...] = info.astype(BF16)
    send(info_ref, out_hbm.at[:, pl.ds(COPIES * BODY, HALF), :])
    for copy in back:
        copy.wait()


def tiles(got_hbm, copy, target, sem):
    started = []
    for piece in range(PIECES):
        at = (copy * PIECES + piece) * PER_PAIR
        lanes = pl.ds(piece * LANES, LANES)
        started.append(pltpu.make_async_copy(got_hbm.at[:, pl.ds(at, PER_PAIR), :], target.at[:, :, lanes], sem.at[piece]))
        started[-1].start()
    return started


def slot_tiles(got_hbm, target, sem):
    copy = pltpu.make_async_copy(got_hbm.at[:, pl.ds(COPIES * BODY, HALF), :], target, sem)
    copy.start()
    return copy


def arrival_slots(digits, copies):
    upper = digits.astype(F32)
    lower = jnp.concatenate([upper[:, :, LANES // 2:], upper[:, :, :LANES // 2]], axis=2)
    digits = jnp.concatenate([upper, lower], axis=1).reshape(ROWS, LANES)
    digits = jnp.transpose(digits)[0:8, :]
    return [(digits[2 * c:2 * c + 1, :] * DIGITS + digits[2 * c + 1:2 * c + 2, :]).astype(jnp.int32) for c in copies]


def arrival_ids(ids, land):
    ids = jnp.broadcast_to(ids.astype(F32), (8, ROWS)).astype(BF16)
    arrived = jnp.zeros((8, ROWS), F32)
    for at in range(0, ROWS, 256):
        place = one_hot(256, at, land)
        arrived = arrived + jnp.dot(ids[:, at:at + 256], place, preferred_element_type=F32)
    return arrived[0:1, :]


def split_kernel(got_hbm, list_ref, *refs):
    ids_refs, (out_ref, blocks_ref, far_ref, land_ref, digit_ref, sems) = refs[:COPIES], refs[COPIES:]
    slots = slot_tiles(got_hbm, digit_ref, sems.at[0, PIECES])
    rows = [tiles(got_hbm, c, blocks_ref.at[c], sems.at[c]) for c in range(COPIES)]
    slots.wait()
    lands = arrival_slots(digit_ref[...], range(COPIES))
    land_ref[...] = lands[0]
    for c in range(COPIES):
        far_ref[c] = arrival_ids(ids_refs[c][...], lands[c])
    ids = far_ref[0]
    entries = list_ref[...].astype(F32)
    row = iota((TAIL, LANES), 0)
    for at in range(0, WIDTH, LANES):
        rest = ids[:, at + WIDTH:at + WIDTH + LANES] if at + WIDTH < ROWS else jnp.zeros((1, LANES), F32)
        tail = jnp.where(row == 0, ids[:, at:at + LANES], jnp.where(row == 1, rest, entries))
        out_ref[ROWS:ROWS + TAIL, at:at + LANES] = tail.astype(BF16)
    for copy in rows[0]:
        copy.wait()
    out_ref[0:ROWS, :] = blocks_ref[0].reshape(ROWS, WIDTH)
    for copy in (*rows[1], *rows[2]):
        copy.wait()


def weight_of(ref, shift):
    entries = ref[ROWS:ROWS + TAIL, 0:LANES].astype(F32)[2:3, :]
    return jnp.sum(jnp.where(iota((1, LANES), 1) == shift - 1, entries, 0.0), axis=1, keepdims=True)


def ids_row(ref):
    tail = ref[ROWS:ROWS + TAIL, :].astype(F32)
    return jnp.concatenate([tail[0:1, :], tail[1:2, 0:ROWS - WIDTH]], axis=1)


def tile_terms(scores, id_col, id_row, masked):
    rows, cols = scores.shape
    over_cols, over_rows = None, []
    for lane in range(cols // LANES):
        cut = slice(lane * LANES, (lane + 1) * LANES)
        half = jnp.tanh(scores[:, cut] * (0.5 * sharpness) - 0.5 * sharpness * threshold)
        factor = jnp.where(id_col == id_row[:, cut], 0.5, 0.25)
        term = factor * (1.0 + half)
        if masked:
            term = jnp.where(iota(term.shape, 0) == iota(term.shape, 1) + lane * LANES, 0.0, term)
        over_cols = term if over_cols is None else over_cols + term
        over_rows.append(jnp.sum(term.reshape(rows // 8, 8, LANES), axis=0))
    return over_cols, jnp.concatenate(over_rows, axis=1)


SIZE = 256
CUTS = [slice(at, at + SIZE) for at in range(0, ROWS, SIZE)]


def pair(a_ref, a_col, b_of, b_row, listed, row_acc, col_acc, total):
    @pl.when(jnp.sum(listed) > 0.0)
    def _():
        for part in CUTS:
            b = b_of(part)
            down = None
            for at in CUTS:
                by_row, by_col = tile_terms(nt(a_ref[at, :], b), a_col[at, :], b_row[:, part], False)
                row_acc[at, :] = row_acc[at, :] + by_row
                down = by_col if down is None else down + by_col
            col_acc[:, part] = down
        total[...] = total[...] + jnp.sum(col_acc[...], axis=0, keepdims=True)


def own_pair(ref, a_col, row, row_acc, col_acc):
    for i, at in enumerate(CUTS):
        a = ref[at, :]
        for j, part in enumerate(CUTS):
            if j < i:
                continue
            by_row, by_col = tile_terms(nt(a, ref[part, :]), a_col[at, :], row[:, part], i == j)
            row_acc[at, :] = row_acc[at, :] + by_row
            if j > i:
                col_acc[:, part] = col_acc[:, part] + by_col


def fold_rows(acc):
    return jnp.sum(jnp.transpose(acc[...]), axis=0, keepdims=True)


def first_kernel(own_ref, blocks_ref, ids_ref, sums_ref, col, row_acc, col_acc):
    col[...] = as_column(ids_ref[0])
    row_acc[...] = jnp.zeros_like(row_acc)
    sums_ref[...] = jnp.zeros_like(sums_ref)
    for c in range(1, COPIES):
        pair(
            own_ref, col, block_part(blocks_ref, c), ids_ref[c], weight_of(own_ref, APART * c), row_acc, col_acc,
            sums_ref.at[c],
        )
    sums_ref[0] = fold_rows(row_acc)


def self_kernel(own_ref, sum_ref, out_ref, col, row_acc, col_acc):
    row = ids_row(own_ref)
    col[...] = as_column(row)
    row_acc[...] = jnp.zeros_like(row_acc)
    col_acc[...] = jnp.zeros_like(col_acc)
    own_pair(own_ref, col, row, row_acc, col_acc)
    out_ref[...] = sum_ref[...] + fold_rows(row_acc) + jnp.sum(col_acc[...], axis=0, keepdims=True)


def block_part(blocks_ref, which):
    def part(rows):
        at = pl.ds(rows.start // PER_PAIR, SIZE // PER_PAIR)
        return blocks_ref[which, at, :, :].reshape(SIZE, WIDTH)

    return part


def second_kernel(core_ref, blocks_ref, ids_ref, sums_ref, sw_ref, *refs):
    outs, (total, col, row_acc, col_acc) = refs[:COPIES + 1], refs[COPIES + 1:]
    total[...] = sums_ref[...]
    col[...] = as_column(ids_row(sw_ref))
    row_acc[...] = jnp.zeros_like(row_acc)
    for n in range(2):
        which = 1 - core_ref[0] + n
        pair(
            sw_ref, col, block_part(blocks_ref, which), ids_ref[which], weight_of(sw_ref, 1 + 2 * n), row_acc,
            col_acc, total.at[which],
        )
    for c in range(COPIES):
        outs[c][...] = total[c]
    outs[COPIES][...] = fold_rows(row_acc)


def end_kernel(land_ref, *refs):
    out_ref = refs[-1]
    load = refs[0][...]
    for ref in refs[1:-1]:
        load = load + ref[...]
    result = 1.0 / (1.0 + load)
    high = result.astype(BF16).astype(F32)
    mid = (result - high).astype(BF16).astype(F32)
    low = result - high - mid
    which = iota((8, ROWS), 0)
    parts = jnp.where(which == 0, high, jnp.where(which == 1, mid, jnp.where(which == 2, low, 0.0))).astype(BF16)
    for step in range(4):
        placed = nt(parts, one_hot(256, step * 256, land_ref[...]))
        out_ref[:, step * 256:(step + 1) * 256] = placed[0:1, :] + placed[1:2, :] + placed[2:3, :]


def vec(n):
    return jax.ShapeDtypeStruct((1, n), F32)


def call(kernel, out_shape, in_specs, scratch, tasks, args, mib=40, out_spec=VMEM):
    single = not isinstance(out_shape, (list, tuple))
    return pl.pallas_call(
        kernel,
        out_shape=out_shape,
        in_specs=in_specs,
        out_specs=out_spec if single else [out_spec] * len(out_shape),
        scratch_shapes=scratch,
        compiler_params=pltpu.CompilerParams(vmem_limit_bytes=mib << 20),
        cost_estimate=pl.CostEstimate(
            flops=int(HINT * tasks * 2 * ROWS * ROWS * WIDTH),
            transcendentals=int(HINT * tasks * ROWS * ROWS),
            bytes_accessed=int(HINT * (1 + tasks) * 2 * ROWS * WIDTH),
        ),
    )(*args)


def move(value, devices, change, only=None):
    pairs = [
        (p, change(p))
        for p in range(devices)
        if 0 <= change(p) < devices and (only is None or p % 2 == only)
    ]
    return lax.ppermute(value, AXES, pairs)


def local(embeddings, sorted_slot, cluster_ids, block_list):
    devices = lax.axis_size(AXES)
    position = lax.axis_index(AXES)
    core = (position % 2).astype(jnp.int32).reshape(1)
    move_d = functools.partial(move, devices=devices)
    scratch = pltpu.VMEM

    outgoing = call(
        functools.partial(front_kernel, devices),
        jax.ShapeDtypeStruct((devices, MESSAGE, LANES), BF16), [ANY] * 2,
        [scratch((1, ROWS), jnp.int32), scratch((ROWS, WIDTH), BF16), scratch((ROWS, WIDTH + LANES), BF16)]
        + [scratch((devices, HALF, LANES), F32), scratch((devices, HALF, LANES), BF16)]
        + [scratch((devices, BODY, LANES), BF16), pltpu.SemaphoreType.DMA((24,))],
        1, (sorted_slot.reshape(1, ROWS), embeddings), 62, ANY,
    )
    got = lax.all_to_all(outgoing, AXES, split_axis=0, concat_axis=0, tiled=True)
    ids = cluster_ids.reshape(1, ROWS)
    far_ids = [move_d(ids, change=lambda p, c=c: p - APART * c) for c in range(1, COPIES)]
    reach = position + 1 + jnp.arange(SHIFTS, dtype=jnp.int32)
    entries = jnp.pad(jnp.where(reach[None, :] < devices, block_list, 0), ((0, 0), (0, LANES - SHIFTS)))
    sems = pltpu.SemaphoreType.DMA
    own, blocks, block_ids, land = call(
        split_kernel,
        [
            jax.ShapeDtypeStruct((ROWS + TAIL, WIDTH), BF16),
            jax.ShapeDtypeStruct((COPIES, devices, PER_PAIR, WIDTH), BF16),
            jax.ShapeDtypeStruct((COPIES, 1, ROWS), F32),
            jax.ShapeDtypeStruct((1, ROWS), jnp.int32),
        ],
        [ANY] + [VMEM] * (1 + COPIES), [scratch((devices, HALF, LANES), BF16), sems((COPIES, PIECES + 1))],
        0.5, (got, entries, ids, *far_ids), 16,
    )
    sw = move_d(own, change=lambda p: p ^ 1)
    sides = [scratch((ROWS, LANES), F32)] * 2 + [scratch((8, ROWS), F32)]
    sums = call(
        first_kernel, jax.ShapeDtypeStruct((COPIES, 1, ROWS), F32), [VMEM] * 3, sides, 2, (own, blocks, block_ids), 16
    )
    sums = call(
        second_kernel, [vec(ROWS)] * (COPIES + 1), [SMEM] + [VMEM] * 4,
        [scratch((COPIES, 1, ROWS), F32)] + sides,
        2, (core, blocks, block_ids, sums, sw), 16,
    )
    own_sum = call(
        self_kernel, vec(ROWS), [VMEM] * 2, sides,
        0.6, (own, sums[0]), 16,
    )
    returned = [own_sum, move_d(sums[COPIES], change=lambda p: p ^ 1)]
    returned += [move_d(sums[c], change=lambda p, c=c: p + APART * c) for c in range(1, COPIES)]
    weights = call(end_kernel, vec(ROWS), [VMEM] * (COPIES + 2), [], 0.2, (land, *returned))
    return weights.reshape(ROWS)


def solution(mesh):
    in_specs = (
        P(("grp", "gr", "gc"), None),
        P(("grp", "gr", "gc")),
        P(("grp", "gr", "gc")),
        P(("grp", "gr", "gc"), None),
    )
    out_specs = P(("grp", "gr", "gc"))
    return jax.shard_map(local, mesh=mesh, in_specs=in_specs, out_specs=out_specs, check_vma=False)
```

```python
import functools
import math

import jax
import jax.numpy as jnp
from jax import lax
from jax.experimental import pallas as pl
from jax.experimental.pallas import tpu as pltpu
from jax.sharding import PartitionSpec as P

SHIFTS = 4
ROWS = 1024
WIDTH = 768
LANES = 128
HINT = 20
COPIES = 3
APART = 2
PER_PAIR = 16
PIECES = WIDTH // LANES
BODY = PIECES * PER_PAIR
HALF = PER_PAIR // 2
MESSAGE = COPIES * BODY + HALF
TAIL = 16
DIGITS = 32
CLUSTERS = 32
STARTS_AT = 8
AXES = ("gr", "gc")

sharpness = 20.0
threshold = 0.8

F32 = jnp.float32
BF16 = jnp.bfloat16
VMEM = pl.BlockSpec(memory_space=pltpu.VMEM)
ANY = pl.BlockSpec(memory_space=pl.ANY)
SMEM = pl.BlockSpec(memory_space=pltpu.SMEM)


def iota(shape, axis):
    return lax.broadcasted_iota(jnp.int32, shape, axis)


def one_hot(rows, first, wanted):
    hit = iota((rows, wanted.shape[1]), 0) + first == wanted
    return jnp.where(hit, 1.0, 0.0).astype(BF16)


def nt(a, b):
    return lax.dot_general(a, b, (((1,), (1,)), ((), ())), preferred_element_type=F32)


def as_column(row):
    return jnp.transpose(jnp.broadcast_to(row, (LANES, row.shape[1])))


def front_kernel(devices, slot_hbm, ids_hbm, emb_ref, out_hbm, slot_ref, ids_ref, raw_ref, unit_ref, digit_ref, info_ref, rows_ref, sems):
    size = 256
    parts = [pl.ds(at, size) for at in range(0, ROWS, size)]
    slots = pltpu.make_async_copy(slot_hbm, slot_ref, sems.at[len(parts)])
    slots.start()
    ids = pltpu.make_async_copy(ids_hbm, ids_ref, sems.at[len(parts) + 1])
    ids.start()
    copies = []
    for n, part in enumerate(parts):
        copies.append(pltpu.make_async_copy(emb_ref.at[part, :], raw_ref.at[part, :], sems.at[n]))
        copies[n].start()
    before = jnp.where(iota((size, size), 0) < iota((size, size), 1), 1.0, 0.0).astype(BF16)
    slots.wait()
    slot = slot_ref[...]
    target = slot // ROWS
    low = slot - target * ROWS
    goes = iota((devices, ROWS), 0) == target
    goes_b = jnp.where(goes, 1.0, 0.0).astype(BF16)
    seen, ranks = jnp.zeros((devices, 1), F32), []
    for at in range(0, ROWS, size):
        here = goes[:, at:at + size]
        count = jnp.dot(goes_b[:, at:at + size], before, preferred_element_type=F32) + seen
        ranks.append(jnp.sum(jnp.where(here, count, 0.0), axis=0, keepdims=True))
        seen = seen + jnp.sum(jnp.where(here, 1.0, 0.0), axis=1, keepdims=True)
    rank = jnp.concatenate(ranks, axis=1)
    dest = target * PER_PAIR + rank.astype(jnp.int32)
    high = low // DIGITS
    even = iota((ROWS, LANES), 1) % 2 == 0
    digits = jnp.where(even, as_column(high.astype(F32)), as_column((low - high * DIGITS).astype(F32)))
    unit_ref[:, WIDTH:] = digits.astype(BF16)
    ids.wait()
    below = jnp.where(ids_ref[...] < iota((CLUSTERS, ROWS), 0), 1.0, 0.0)
    starts = jnp.sum(below, axis=1, keepdims=True).astype(jnp.int32)
    for n, part in enumerate(parts):
        copies[n].wait()
        values = raw_ref[part, :].astype(F32)
        mean = jnp.sum(values * values, axis=1, keepdims=True) * (1.0 / WIDTH)
        inverse = lax.rsqrt(mean + 1e-06) * (1.0 / math.sqrt(WIDTH))
        unit_ref[part, 0:WIDTH] = (values * inverse).astype(BF16)
    per_part = size // PER_PAIR
    back = []

    def send(source, target):
        back.append(pltpu.make_async_copy(source, target, sems.at[len(parts) + 2 + len(back)]))
        back[-1].start()

    lane = iota((per_part, HALF, LANES), 2)
    for n, part in enumerate(parts):
        place = one_hot(size, n * size, dest)
        placed = jnp.dot(place, unit_ref[...], preferred_element_type=F32)
        first = n * per_part
        sent = placed[:, WIDTH:].reshape(per_part, PER_PAIR, LANES)
        digit_ref[first:first + per_part] = jnp.where(lane < LANES // 2, sent[:, 0:HALF, :], sent[:, HALF:, :])
        for i in range(per_part):
            rows = placed[i * PER_PAIR:(i + 1) * PER_PAIR, :].astype(BF16)
            for piece in range(PIECES):
                rows_ref[first + i, piece * PER_PAIR:(piece + 1) * PER_PAIR, :] = rows[:, piece * LANES:(piece + 1) * LANES]
        for copy in range(COPIES):
            back_by = APART * copy
            body = pl.ds(copy * BODY, BODY)
            wrapped = max(0, back_by - first)
            if wrapped:
                send(rows_ref.at[pl.ds(first, wrapped)], out_hbm.at[pl.ds(devices - wrapped, wrapped), body, :])
            count = per_part - wrapped
            send(rows_ref.at[pl.ds(first + wrapped, count)], out_hbm.at[pl.ds(first + wrapped - back_by, count), body, :])
    which = iota((devices, HALF, LANES), 2) % (LANES // 2) // 2
    info = digit_ref[...]
    for copy in range(1, COPIES):
        ahead = APART * copy
        far = jnp.concatenate([digit_ref[ahead:], digit_ref[:ahead]], axis=0)
        info = jnp.where(which == copy, far, info)
    own_lane = iota((HALF, LANES), 1)
    ahead = own_lane < 0
    mine = jnp.zeros((HALF, LANES), jnp.int32)
    for group in range(CLUSTERS // HALF):
        value = starts[group * HALF:(group + 1) * HALF, :]
        at = STARTS_AT + 2 * group
        mine = jnp.where(own_lane == at, value // DIGITS, jnp.where(own_lane == at + 1, value % DIGITS, mine))
        ahead = ahead | (own_lane == at) | (own_lane == at + 1)
    info = jnp.where(ahead[None], mine.astype(F32)[None], info)
    info_ref[...] = info.astype(BF16)
    send(info_ref, out_hbm.at[:, pl.ds(COPIES * BODY, HALF), :])
    for copy in back:
        copy.wait()


def tiles(got_hbm, copy, target, sem):
    started = []
    for piece in range(PIECES):
        at = (copy * PIECES + piece) * PER_PAIR
        lanes = pl.ds(piece * LANES, LANES)
        started.append(pltpu.make_async_copy(got_hbm.at[:, pl.ds(at, PER_PAIR), :], target.at[:, :, lanes], sem.at[piece]))
        started[-1].start()
    return started


def slot_tiles(got_hbm, target, sem):
    copy = pltpu.make_async_copy(got_hbm.at[:, pl.ds(COPIES * BODY, HALF), :], target, sem)
    copy.start()
    return copy


def arrival_slots(digits, copies):
    upper = digits.astype(F32)
    lower = jnp.concatenate([upper[:, :, LANES // 2:], upper[:, :, :LANES // 2]], axis=2)
    digits = jnp.concatenate([upper, lower], axis=1).reshape(ROWS, LANES)
    digits = jnp.transpose(digits)[0:8, :]
    return [(digits[2 * c:2 * c + 1, :] * DIGITS + digits[2 * c + 1:2 * c + 2, :]).astype(jnp.int32) for c in copies]


def arrival_ids(tile, land):
    tile = tile.astype(F32)
    lane = iota((HALF, LANES), 1)
    count = jnp.zeros((HALF, ROWS), F32)
    for group in range(CLUSTERS // HALF):
        at = STARTS_AT + 2 * group
        digits = jnp.where(lane == at, tile * DIGITS, jnp.where(lane == at + 1, tile, 0.0))
        starts = jnp.sum(digits, axis=1, keepdims=True).astype(jnp.int32)
        count = count + jnp.where(starts <= land, 1.0, 0.0)
    return jnp.sum(count, axis=0, keepdims=True) - 1.0


def split_kernel(devices, position_ref, list_ref, got_hbm, out_ref, blocks_ref, ids_ref, land_ref, digit_ref, sems):
    slots = slot_tiles(got_hbm, digit_ref, sems.at[0, PIECES])
    rows = [tiles(got_hbm, c, blocks_ref.at[c], sems.at[c]) for c in range(COPIES)]
    position = position_ref[0]
    lane = iota((TAIL, LANES), 1)
    entries = jnp.zeros((TAIL, LANES), F32)
    for shift in range(1, SHIFTS + 1):
        entry = jnp.where(position + shift < devices, list_ref[0, shift - 1], 0).astype(F32)
        entries = jnp.where(lane == shift - 1, entry, entries)
    slots.wait()
    lands = arrival_slots(digit_ref[...], range(COPIES))
    land_ref[...] = lands[0]
    for c in range(COPIES):
        source = jnp.minimum(position + APART * c, devices - 1)
        ids_ref[c] = arrival_ids(digit_ref[source], lands[c])
    ids = ids_ref[0]
    row = iota((TAIL, LANES), 0)
    for at in range(0, WIDTH, LANES):
        rest = ids[:, at + WIDTH:at + WIDTH + LANES] if at + WIDTH < ROWS else jnp.zeros((1, LANES), F32)
        tail = jnp.where(row == 0, ids[:, at:at + LANES], jnp.where(row == 1, rest, entries))
        out_ref[ROWS:ROWS + TAIL, at:at + LANES] = tail.astype(BF16)
    for copy in rows[0]:
        copy.wait()
    out_ref[0:ROWS, :] = blocks_ref[0].reshape(ROWS, WIDTH)
    for copy in (*rows[1], *rows[2]):
        copy.wait()


def weight_of(ref, shift):
    entries = ref[ROWS:ROWS + TAIL, 0:LANES].astype(F32)[2:3, :]
    return jnp.sum(jnp.where(iota((1, LANES), 1) == shift - 1, entries, 0.0), axis=1, keepdims=True)


def ids_row(ref):
    tail = ref[ROWS:ROWS + TAIL, :].astype(F32)
    return jnp.concatenate([tail[0:1, :], tail[1:2, 0:ROWS - WIDTH]], axis=1)


def tile_terms(scores, id_col, id_row, masked):
    rows, cols = scores.shape
    over_cols, over_rows = None, []
    for lane in range(cols // LANES):
        cut = slice(lane * LANES, (lane + 1) * LANES)
        half = jnp.tanh(scores[:, cut] * (0.5 * sharpness) - 0.5 * sharpness * threshold)
        factor = jnp.where(id_col == id_row[:, cut], 0.5, 0.25)
        term = factor * (1.0 + half)
        if masked:
            term = jnp.where(iota(term.shape, 0) == iota(term.shape, 1) + lane * LANES, 0.0, term)
        over_cols = term if over_cols is None else over_cols + term
        over_rows.append(jnp.sum(term.reshape(rows // 8, 8, LANES), axis=0))
    return over_cols, jnp.concatenate(over_rows, axis=1)


SIZE = 256
CUTS = [slice(at, at + SIZE) for at in range(0, ROWS, SIZE)]


def pair(a_ref, a_col, b_of, b_row, listed, row_acc, col_acc, total):
    @pl.when(jnp.sum(listed) > 0.0)
    def _():
        for part in CUTS:
            b = b_of(part)
            down = None
            for at in CUTS:
                by_row, by_col = tile_terms(nt(a_ref[at, :], b), a_col[at, :], b_row[:, part], False)
                row_acc[at, :] = row_acc[at, :] + by_row
                down = by_col if down is None else down + by_col
            col_acc[:, part] = down
        total[...] = total[...] + jnp.sum(col_acc[...], axis=0, keepdims=True)


def own_pair(ref, a_col, row, row_acc, col_acc):
    for i, at in enumerate(CUTS):
        a = ref[at, :]
        for j, part in enumerate(CUTS):
            if j < i:
                continue
            by_row, by_col = tile_terms(nt(a, ref[part, :]), a_col[at, :], row[:, part], i == j)
            row_acc[at, :] = row_acc[at, :] + by_row
            if j > i:
                col_acc[:, part] = col_acc[:, part] + by_col


def fold_rows(acc):
    return jnp.sum(jnp.transpose(acc[...]), axis=0, keepdims=True)


def first_kernel(own_ref, blocks_ref, ids_ref, sums_ref, col, row_acc, col_acc):
    col[...] = as_column(ids_ref[0])
    row_acc[...] = jnp.zeros_like(row_acc)
    sums_ref[...] = jnp.zeros_like(sums_ref)
    for c in range(1, COPIES):
        pair(
            own_ref, col, block_part(blocks_ref, c), ids_ref[c], weight_of(own_ref, APART * c), row_acc, col_acc,
            sums_ref.at[c],
        )
    sums_ref[0] = fold_rows(row_acc)


def self_kernel(own_ref, sum_ref, out_ref, col, row_acc, col_acc):
    row = ids_row(own_ref)
    col[...] = as_column(row)
    row_acc[...] = jnp.zeros_like(row_acc)
    col_acc[...] = jnp.zeros_like(col_acc)
    own_pair(own_ref, col, row, row_acc, col_acc)
    out_ref[...] = sum_ref[...] + fold_rows(row_acc) + jnp.sum(col_acc[...], axis=0, keepdims=True)


def block_part(blocks_ref, which):
    def part(rows):
        at = pl.ds(rows.start // PER_PAIR, SIZE // PER_PAIR)
        return blocks_ref[which, at, :, :].reshape(SIZE, WIDTH)

    return part


def second_kernel(position_ref, blocks_ref, ids_ref, sums_ref, sw_ref, *refs):
    outs, (total, col, row_acc, col_acc) = refs[:COPIES + 1], refs[COPIES + 1:]
    total[...] = sums_ref[...]
    col[...] = as_column(ids_row(sw_ref))
    row_acc[...] = jnp.zeros_like(row_acc)
    for n in range(2):
        which = 1 - position_ref[0] % 2 + n
        pair(
            sw_ref, col, block_part(blocks_ref, which), ids_ref[which], weight_of(sw_ref, 1 + 2 * n), row_acc,
            col_acc, total.at[which],
        )
    for c in range(COPIES):
        outs[c][...] = total[c]
    outs[COPIES][...] = fold_rows(row_acc)


def end_kernel(land_ref, *refs):
    out_ref = refs[-1]
    load = refs[0][...]
    for ref in refs[1:-1]:
        load = load + ref[...]
    result = 1.0 / (1.0 + load)
    high = result.astype(BF16).astype(F32)
    mid = (result - high).astype(BF16).astype(F32)
    low = result - high - mid
    which = iota((8, ROWS), 0)
    parts = jnp.where(which == 0, high, jnp.where(which == 1, mid, jnp.where(which == 2, low, 0.0))).astype(BF16)
    for step in range(4):
        placed = nt(parts, one_hot(256, step * 256, land_ref[...]))
        out_ref[:, step * 256:(step + 1) * 256] = placed[0:1, :] + placed[1:2, :] + placed[2:3, :]


def vec(n):
    return jax.ShapeDtypeStruct((1, n), F32)


def call(kernel, out_shape, in_specs, scratch, tasks, args, mib=40, out_spec=VMEM):
    single = not isinstance(out_shape, (list, tuple))
    return pl.pallas_call(
        kernel,
        out_shape=out_shape,
        in_specs=in_specs,
        out_specs=out_spec if single else [out_spec] * len(out_shape),
        scratch_shapes=scratch,
        compiler_params=pltpu.CompilerParams(vmem_limit_bytes=mib << 20),
        cost_estimate=pl.CostEstimate(
            flops=int(HINT * tasks * 2 * ROWS * ROWS * WIDTH),
            transcendentals=int(HINT * tasks * ROWS * ROWS),
            bytes_accessed=int(HINT * (1 + tasks) * 2 * ROWS * WIDTH),
        ),
    )(*args)


def move(value, devices, change, only=None):
    pairs = [
        (p, change(p))
        for p in range(devices)
        if 0 <= change(p) < devices and (only is None or p % 2 == only)
    ]
    return lax.ppermute(value, AXES, pairs)


def local(embeddings, sorted_slot, cluster_ids, block_list):
    devices = lax.axis_size(AXES)
    position = lax.axis_index(AXES).astype(jnp.int32).reshape(1)
    move_d = functools.partial(move, devices=devices)
    scratch = pltpu.VMEM

    outgoing = call(
        functools.partial(front_kernel, devices),
        jax.ShapeDtypeStruct((devices, MESSAGE, LANES), BF16), [ANY] * 3,
        [scratch((1, ROWS), jnp.int32)] * 2 + [scratch((ROWS, WIDTH), BF16), scratch((ROWS, WIDTH + LANES), BF16)]
        + [scratch((devices, HALF, LANES), F32), scratch((devices, HALF, LANES), BF16)]
        + [scratch((devices, BODY, LANES), BF16), pltpu.SemaphoreType.DMA((24,))],
        1, (sorted_slot.reshape(1, ROWS), cluster_ids.reshape(1, ROWS), embeddings), 62, ANY,
    )
    got = lax.all_to_all(outgoing, AXES, split_axis=0, concat_axis=0, tiled=True)
    sems = pltpu.SemaphoreType.DMA
    own, blocks, block_ids, land = call(
        functools.partial(split_kernel, devices),
        [
            jax.ShapeDtypeStruct((ROWS + TAIL, WIDTH), BF16),
            jax.ShapeDtypeStruct((COPIES, devices, PER_PAIR, WIDTH), BF16),
            jax.ShapeDtypeStruct((COPIES, 1, ROWS), F32),
            jax.ShapeDtypeStruct((1, ROWS), jnp.int32),
        ],
        [SMEM, SMEM, ANY], [scratch((devices, HALF, LANES), BF16), sems((COPIES, PIECES + 1))],
        0.5, (position, block_list, got), 16,
    )
    sw = move_d(own, change=lambda p: p ^ 1)
    sides = [scratch((ROWS, LANES), F32)] * 2 + [scratch((8, ROWS), F32)]
    sums = call(
        first_kernel, jax.ShapeDtypeStruct((COPIES, 1, ROWS), F32), [VMEM] * 3, sides, 2, (own, blocks, block_ids), 16
    )
    sums = call(
        second_kernel, [vec(ROWS)] * (COPIES + 1), [SMEM] + [VMEM] * 4,
        [scratch((COPIES, 1, ROWS), F32)] + sides,
        2, (position, blocks, block_ids, sums, sw), 16,
    )
    own_sum = call(
        self_kernel, vec(ROWS), [VMEM] * 2, sides,
        0.6, (own, sums[0]), 16,
    )
    returned = [own_sum, move_d(sums[COPIES], change=lambda p: p ^ 1)]
    returned += [move_d(sums[c], change=lambda p, c=c: p + APART * c) for c in range(1, COPIES)]
    weights = call(end_kernel, vec(ROWS), [VMEM] * (COPIES + 2), [], 0.2, (land, *returned))
    return weights.reshape(ROWS)


def solution(mesh):
    in_specs = (
        P(("grp", "gr", "gc"), None),
        P(("grp", "gr", "gc")),
        P(("grp", "gr", "gc")),
        P(("grp", "gr", "gc"), None),
    )
    out_specs = P(("grp", "gr", "gc"))
    return jax.shard_map(local, mesh=mesh, in_specs=in_specs, out_specs=out_specs, check_vma=False)
```

```python
import functools
import math

import jax
import jax.numpy as jnp
from jax import lax
from jax.experimental import pallas as pl
from jax.experimental.pallas import tpu as pltpu
from jax.sharding import PartitionSpec as P

SHIFTS = 4
ROWS = 1024
WIDTH = 768
LANES = 128
HINT = 20
COPIES = 3
APART = 2
PER_PAIR = 16
PIECES = WIDTH // LANES
BODY = PIECES * PER_PAIR
HALF = PER_PAIR // 2
MESSAGE = COPIES * BODY + HALF
TAIL = 16
DIGITS = 32
AXES = ("gr", "gc")

sharpness = 20.0
threshold = 0.8

F32 = jnp.float32
BF16 = jnp.bfloat16
VMEM = pl.BlockSpec(memory_space=pltpu.VMEM)
ANY = pl.BlockSpec(memory_space=pl.ANY)
SMEM = pl.BlockSpec(memory_space=pltpu.SMEM)


def iota(shape, axis):
    return lax.broadcasted_iota(jnp.int32, shape, axis)


def one_hot(rows, first, wanted):
    hit = iota((rows, wanted.shape[1]), 0) + first == wanted
    return jnp.where(hit, 1.0, 0.0).astype(BF16)


def nt(a, b):
    return lax.dot_general(a, b, (((1,), (1,)), ((), ())), preferred_element_type=F32)


def as_column(row):
    return jnp.transpose(jnp.broadcast_to(row, (LANES, row.shape[1])))


def front_kernel(devices, slot_hbm, emb_ref, out_hbm, slot_ref, raw_ref, unit_ref, digit_ref, info_ref, rows_ref, sems):
    size = 256
    parts = [pl.ds(at, size) for at in range(0, ROWS, size)]
    slots = pltpu.make_async_copy(slot_hbm, slot_ref, sems.at[len(parts)])
    slots.start()
    copies = []
    for n, part in enumerate(parts):
        copies.append(pltpu.make_async_copy(emb_ref.at[part, :], raw_ref.at[part, :], sems.at[n]))
        copies[n].start()
    before = jnp.where(iota((size, size), 0) < iota((size, size), 1), 1.0, 0.0).astype(BF16)
    slots.wait()
    slot = slot_ref[...]
    target = slot // ROWS
    low = slot - target * ROWS
    goes = iota((devices, ROWS), 0) == target
    goes_b = jnp.where(goes, 1.0, 0.0).astype(BF16)
    seen, ranks = jnp.zeros((devices, 1), F32), []
    for at in range(0, ROWS, size):
        here = goes[:, at:at + size]
        count = jnp.dot(goes_b[:, at:at + size], before, preferred_element_type=F32) + seen
        ranks.append(jnp.sum(jnp.where(here, count, 0.0), axis=0, keepdims=True))
        seen = seen + jnp.sum(jnp.where(here, 1.0, 0.0), axis=1, keepdims=True)
    rank = jnp.concatenate(ranks, axis=1)
    dest = target * PER_PAIR + rank.astype(jnp.int32)
    high = low // DIGITS
    even = iota((ROWS, LANES), 1) % 2 == 0
    digits = jnp.where(even, as_column(high.astype(F32)), as_column((low - high * DIGITS).astype(F32)))
    unit_ref[:, WIDTH:] = digits.astype(BF16)
    for n, part in enumerate(parts):
        copies[n].wait()
        values = raw_ref[part, :].astype(F32)
        mean = jnp.sum(values * values, axis=1, keepdims=True) * (1.0 / WIDTH)
        inverse = lax.rsqrt(mean + 1e-06) * (1.0 / math.sqrt(WIDTH))
        unit_ref[part, 0:WIDTH] = (values * inverse).astype(BF16)
    per_part = size // PER_PAIR
    back = []

    def send(source, target):
        back.append(pltpu.make_async_copy(source, target, sems.at[len(parts) + 1 + len(back)]))
        back[-1].start()

    lane = iota((per_part, HALF, LANES), 2)
    for n, part in enumerate(parts):
        place = one_hot(size, n * size, dest)
        placed = jnp.dot(place, unit_ref[...], preferred_element_type=F32)
        first = n * per_part
        sent = placed[:, WIDTH:].reshape(per_part, PER_PAIR, LANES)
        digit_ref[first:first + per_part] = jnp.where(lane < LANES // 2, sent[:, 0:HALF, :], sent[:, HALF:, :])
        for i in range(per_part):
            rows = placed[i * PER_PAIR:(i + 1) * PER_PAIR, :].astype(BF16)
            for piece in range(PIECES):
                rows_ref[first + i, piece * PER_PAIR:(piece + 1) * PER_PAIR, :] = rows[:, piece * LANES:(piece + 1) * LANES]
        for copy in range(COPIES):
            back_by = APART * copy
            body = pl.ds(copy * BODY, BODY)
            wrapped = max(0, back_by - first)
            if wrapped:
                send(rows_ref.at[pl.ds(first, wrapped)], out_hbm.at[pl.ds(devices - wrapped, wrapped), body, :])
            count = per_part - wrapped
            send(rows_ref.at[pl.ds(first + wrapped, count)], out_hbm.at[pl.ds(first + wrapped - back_by, count), body, :])
    which = iota((devices, HALF, LANES), 2) % (LANES // 2) // 2
    info = digit_ref[...]
    for copy in range(1, COPIES):
        ahead = APART * copy
        far = jnp.concatenate([digit_ref[ahead:], digit_ref[:ahead]], axis=0)
        info = jnp.where(which == copy, far, info)
    info_ref[...] = info.astype(BF16)
    send(info_ref, out_hbm.at[:, pl.ds(COPIES * BODY, HALF), :])
    for copy in back:
        copy.wait()


def tiles(got_hbm, copy, target, sem):
    started = []
    for piece in range(PIECES):
        at = (copy * PIECES + piece) * PER_PAIR
        lanes = pl.ds(piece * LANES, LANES)
        started.append(pltpu.make_async_copy(got_hbm.at[:, pl.ds(at, PER_PAIR), :], target.at[:, :, lanes], sem.at[piece]))
        started[-1].start()
    return started


def slot_tiles(got_hbm, target, sem):
    copy = pltpu.make_async_copy(got_hbm.at[:, pl.ds(COPIES * BODY, HALF), :], target, sem)
    copy.start()
    return copy


def arrival_slots(digits, copies):
    upper = digits.astype(F32)
    lower = jnp.concatenate([upper[:, :, LANES // 2:], upper[:, :, :LANES // 2]], axis=2)
    digits = jnp.concatenate([upper, lower], axis=1).reshape(ROWS, LANES)
    digits = jnp.transpose(digits)[0:8, :]
    return [(digits[2 * c:2 * c + 1, :] * DIGITS + digits[2 * c + 1:2 * c + 2, :]).astype(jnp.int32) for c in copies]


def arrival_ids(ids, land):
    ids = jnp.broadcast_to(ids.astype(F32), (8, ROWS)).astype(BF16)
    arrived = jnp.zeros((8, ROWS), F32)
    for at in range(0, ROWS, 256):
        place = one_hot(256, at, land)
        arrived = arrived + jnp.dot(ids[:, at:at + 256], place, preferred_element_type=F32)
    return arrived[0:1, :]


def split_kernel(got_hbm, list_ref, *refs):
    ids_refs, (out_ref, blocks_ref, far_ref, land_ref, digit_ref, sems) = refs[:COPIES], refs[COPIES:]
    slots = slot_tiles(got_hbm, digit_ref, sems.at[0, PIECES])
    rows = [tiles(got_hbm, c, blocks_ref.at[c], sems.at[c]) for c in range(COPIES - 1)]
    slots.wait()
    lands = arrival_slots(digit_ref[...], range(COPIES))
    land_ref[...] = lands[0]
    for c in range(COPIES):
        far_ref[c] = arrival_ids(ids_refs[c][...], lands[c])
    ids = far_ref[0]
    entries = list_ref[...].astype(F32)
    row = iota((TAIL, LANES), 0)
    for at in range(0, WIDTH, LANES):
        rest = ids[:, at + WIDTH:at + WIDTH + LANES] if at + WIDTH < ROWS else jnp.zeros((1, LANES), F32)
        tail = jnp.where(row == 0, ids[:, at:at + LANES], jnp.where(row == 1, rest, entries))
        out_ref[ROWS:ROWS + TAIL, at:at + LANES] = tail.astype(BF16)
    for copy in rows[0]:
        copy.wait()
    out_ref[0:ROWS, :] = blocks_ref[0].reshape(ROWS, WIDTH)
    for copy in rows[1]:
        copy.wait()


def weight_of(ref, shift):
    entries = ref[ROWS:ROWS + TAIL, 0:LANES].astype(F32)[2:3, :]
    return jnp.sum(jnp.where(iota((1, LANES), 1) == shift - 1, entries, 0.0), axis=1, keepdims=True)


def ids_row(ref):
    tail = ref[ROWS:ROWS + TAIL, :].astype(F32)
    return jnp.concatenate([tail[0:1, :], tail[1:2, 0:ROWS - WIDTH]], axis=1)


def tile_terms(scores, id_col, id_row, masked):
    rows, cols = scores.shape
    over_cols, over_rows = None, []
    for lane in range(cols // LANES):
        cut = slice(lane * LANES, (lane + 1) * LANES)
        half = jnp.tanh(scores[:, cut] * (0.5 * sharpness) - 0.5 * sharpness * threshold)
        factor = jnp.where(id_col == id_row[:, cut], 0.5, 0.25)
        term = factor * (1.0 + half)
        if masked:
            term = jnp.where(iota(term.shape, 0) == iota(term.shape, 1) + lane * LANES, 0.0, term)
        over_cols = term if over_cols is None else over_cols + term
        over_rows.append(jnp.sum(term.reshape(rows // 8, 8, LANES), axis=0))
    return over_cols, jnp.concatenate(over_rows, axis=1)


SIZE = 256
CUTS = [slice(at, at + SIZE) for at in range(0, ROWS, SIZE)]


def pair(a_ref, a_col, b_of, b_row, listed, row_acc, col_acc, total):
    @pl.when(jnp.sum(listed) > 0.0)
    def _():
        for part in CUTS:
            b = b_of(part)
            down = None
            for at in CUTS:
                by_row, by_col = tile_terms(nt(a_ref[at, :], b), a_col[at, :], b_row[:, part], False)
                row_acc[at, :] = row_acc[at, :] + by_row
                down = by_col if down is None else down + by_col
            col_acc[:, part] = down
        total[...] = total[...] + jnp.sum(col_acc[...], axis=0, keepdims=True)


def own_pair(ref, a_col, row, row_acc, col_acc):
    for i, at in enumerate(CUTS):
        a = ref[at, :]
        for j, part in enumerate(CUTS):
            if j < i:
                continue
            by_row, by_col = tile_terms(nt(a, ref[part, :]), a_col[at, :], row[:, part], i == j)
            row_acc[at, :] = row_acc[at, :] + by_row
            if j > i:
                col_acc[:, part] = col_acc[:, part] + by_col


def fold_rows(acc):
    return jnp.sum(jnp.transpose(acc[...]), axis=0, keepdims=True)


def first_kernel(got_hbm, own_ref, near_ref, ids_ref, sums_ref, far_ref, col, row_acc, col_acc, sems):
    rows = [tiles(got_hbm, c, far_ref.at[c - 1], sems.at[c]) for c in range(COPIES - 1, 0, -1)]
    col[...] = as_column(ids_ref[0])
    row_acc[...] = jnp.zeros_like(row_acc)
    sums_ref[...] = jnp.zeros_like(sums_ref)
    for c in range(1, COPIES):
        block = block_part(near_ref, 1) if c == 1 else block_part(far_ref, 1)
        pair(own_ref, col, block, ids_ref[c], weight_of(own_ref, APART * c), row_acc, col_acc, sums_ref.at[c])
        for copy in rows.pop(0):
            copy.wait()
    sums_ref[0] = fold_rows(row_acc)


def self_kernel(own_ref, land_ref, sum_ref, out_ref, place_ref, col, row_acc, col_acc):
    for at in range(0, ROWS, 256):
        place_ref[at:at + 256, :] = one_hot(256, at, land_ref[...])
    row = ids_row(own_ref)
    col[...] = as_column(row)
    row_acc[...] = jnp.zeros_like(row_acc)
    col_acc[...] = jnp.zeros_like(col_acc)
    own_pair(own_ref, col, row, row_acc, col_acc)
    out_ref[...] = sum_ref[...] + fold_rows(row_acc) + jnp.sum(col_acc[...], axis=0, keepdims=True)


def block_part(blocks_ref, which):
    def part(rows):
        at = pl.ds(rows.start // PER_PAIR, SIZE // PER_PAIR)
        return blocks_ref[which, at, :, :].reshape(SIZE, WIDTH)

    return part


def second_kernel(core_ref, near_ref, far_ref, ids_ref, sums_ref, sw_ref, *refs):
    outs, (total, col, row_acc, col_acc) = refs[:COPIES + 1], refs[COPIES + 1:]
    total[...] = sums_ref[...]
    col[...] = as_column(ids_row(sw_ref))
    row_acc[...] = jnp.zeros_like(row_acc)
    for n in range(2):
        which = 1 - core_ref[0] + n
        pair(
            sw_ref, col, block_part(far_ref if n else near_ref, 1 - core_ref[0]), ids_ref[which], weight_of(sw_ref, 1 + 2 * n), row_acc,
            col_acc, total.at[which],
        )
    for c in range(COPIES):
        outs[c][...] = total[c]
    outs[COPIES][...] = fold_rows(row_acc)


def end_kernel(place_ref, *refs):
    out_ref = refs[-1]
    load = refs[0][...]
    for ref in refs[1:-1]:
        load = load + ref[...]
    result = 1.0 / (1.0 + load)
    high = result.astype(BF16).astype(F32)
    mid = (result - high).astype(BF16).astype(F32)
    low = result - high - mid
    which = iota((8, ROWS), 0)
    parts = jnp.where(which == 0, high, jnp.where(which == 1, mid, jnp.where(which == 2, low, 0.0))).astype(BF16)
    for step in range(4):
        placed = nt(parts, place_ref[step * 256:(step + 1) * 256, :])
        out_ref[:, step * 256:(step + 1) * 256] = placed[0:1, :] + placed[1:2, :] + placed[2:3, :]


def vec(n):
    return jax.ShapeDtypeStruct((1, n), F32)


def call(kernel, out_shape, in_specs, scratch, tasks, args, mib=40, out_spec=VMEM):
    single = not isinstance(out_shape, (list, tuple))
    return pl.pallas_call(
        kernel,
        out_shape=out_shape,
        in_specs=in_specs,
        out_specs=out_spec if single else [out_spec] * len(out_shape),
        scratch_shapes=scratch,
        compiler_params=pltpu.CompilerParams(vmem_limit_bytes=mib << 20),
        cost_estimate=pl.CostEstimate(
            flops=int(HINT * tasks * 2 * ROWS * ROWS * WIDTH),
            transcendentals=int(HINT * tasks * ROWS * ROWS),
            bytes_accessed=int(HINT * (1 + tasks) * 2 * ROWS * WIDTH),
        ),
    )(*args)


def move(value, devices, change, only=None):
    pairs = [
        (p, change(p))
        for p in range(devices)
        if 0 <= change(p) < devices and (only is None or p % 2 == only)
    ]
    return lax.ppermute(value, AXES, pairs)


def local(embeddings, sorted_slot, cluster_ids, block_list):
    devices = lax.axis_size(AXES)
    position = lax.axis_index(AXES)
    core = (position % 2).astype(jnp.int32).reshape(1)
    move_d = functools.partial(move, devices=devices)
    scratch = pltpu.VMEM

    outgoing = call(
        functools.partial(front_kernel, devices),
        jax.ShapeDtypeStruct((devices, MESSAGE, LANES), BF16), [ANY] * 2,
        [scratch((1, ROWS), jnp.int32), scratch((ROWS, WIDTH), BF16), scratch((ROWS, WIDTH + LANES), BF16)]
        + [scratch((devices, HALF, LANES), F32), scratch((devices, HALF, LANES), BF16)]
        + [scratch((devices, BODY, LANES), BF16), pltpu.SemaphoreType.DMA((24,))],
        1, (sorted_slot.reshape(1, ROWS), embeddings), 62, ANY,
    )
    got = lax.all_to_all(outgoing, AXES, split_axis=0, concat_axis=0, tiled=True)
    ids = cluster_ids.reshape(1, ROWS)
    far_ids = [move_d(ids, change=lambda p, c=c: p - APART * c) for c in range(1, COPIES)]
    reach = position + 1 + jnp.arange(SHIFTS, dtype=jnp.int32)
    entries = jnp.pad(jnp.where(reach[None, :] < devices, block_list, 0), ((0, 0), (0, LANES - SHIFTS)))
    sems = pltpu.SemaphoreType.DMA
    two_blocks = jax.ShapeDtypeStruct((2, devices, PER_PAIR, WIDTH), BF16)
    own, near, block_ids, land = call(
        split_kernel,
        [
            jax.ShapeDtypeStruct((ROWS + TAIL, WIDTH), BF16),
            two_blocks,
            jax.ShapeDtypeStruct((COPIES, 1, ROWS), F32),
            jax.ShapeDtypeStruct((1, ROWS), jnp.int32),
        ],
        [ANY] + [VMEM] * (1 + COPIES), [scratch((devices, HALF, LANES), BF16), sems((COPIES, PIECES + 1))],
        0.5, (got, entries, ids, *far_ids), 16,
    )
    sw = move_d(own, change=lambda p: p ^ 1)
    sides = [scratch((ROWS, LANES), F32)] * 2 + [scratch((8, ROWS), F32)]
    sums, far = call(
        first_kernel, [jax.ShapeDtypeStruct((COPIES, 1, ROWS), F32), two_blocks], [ANY] + [VMEM] * 3,
        sides + [sems((COPIES, PIECES))], 2, (got, own, near, block_ids), 16,
    )
    sums = call(
        second_kernel, [vec(ROWS)] * (COPIES + 1), [SMEM] + [VMEM] * 5,
        [scratch((COPIES, 1, ROWS), F32)] + sides,
        2, (core, near, far, block_ids, sums, sw), 16,
    )
    own_sum, place = call(
        self_kernel, [vec(ROWS), jax.ShapeDtypeStruct((ROWS, ROWS), BF16)], [VMEM] * 3, sides,
        0.6, (own, land, sums[0]), 16,
    )
    returned = [own_sum, move_d(sums[COPIES], change=lambda p: p ^ 1)]
    returned += [move_d(sums[c], change=lambda p, c=c: p + APART * c) for c in range(1, COPIES)]
    weights = call(end_kernel, vec(ROWS), [VMEM] * (COPIES + 2), [], 0.2, (place, *returned))
    return weights.reshape(ROWS)


def solution(mesh):
    in_specs = (
        P(("grp", "gr", "gc"), None),
        P(("grp", "gr", "gc")),
        P(("grp", "gr", "gc")),
        P(("grp", "gr", "gc"), None),
    )
    out_specs = P(("grp", "gr", "gc"))
    return jax.shard_map(local, mesh=mesh, in_specs=in_specs, out_specs=out_specs, check_vma=False)
```

```python
import functools
import math

import jax
import jax.numpy as jnp
from jax import lax
from jax.experimental import pallas as pl
from jax.experimental.pallas import tpu as pltpu
from jax.sharding import PartitionSpec as P

SHIFTS = 4
ROWS = 1024
WIDTH = 768
LANES = 128
HINT = 20
COPIES = 3
APART = 2
PER_PAIR = 16
PIECES = WIDTH // LANES
BODY = PIECES * PER_PAIR
HALF = PER_PAIR // 2
MESSAGE = COPIES * BODY + HALF
TAIL = 16
DIGITS = 32
AXES = ("gr", "gc")

sharpness = 20.0
threshold = 0.8

F32 = jnp.float32
BF16 = jnp.bfloat16
VMEM = pl.BlockSpec(memory_space=pltpu.VMEM)
ANY = pl.BlockSpec(memory_space=pl.ANY)
SMEM = pl.BlockSpec(memory_space=pltpu.SMEM)


def iota(shape, axis):
    return lax.broadcasted_iota(jnp.int32, shape, axis)


def one_hot(rows, first, wanted):
    hit = iota((rows, wanted.shape[1]), 0) + first == wanted
    return jnp.where(hit, 1.0, 0.0).astype(BF16)


def nt(a, b):
    return lax.dot_general(a, b, (((1,), (1,)), ((), ())), preferred_element_type=F32)


def as_column(row):
    return jnp.transpose(jnp.broadcast_to(row, (LANES, row.shape[1])))


def front_kernel(devices, slot_hbm, emb_ref, out_hbm, slot_ref, raw_ref, unit_ref, digit_ref, info_ref, rows_ref, sems):
    size = 256
    parts = [pl.ds(at, size) for at in range(0, ROWS, size)]
    slots = pltpu.make_async_copy(slot_hbm, slot_ref, sems.at[len(parts)])
    slots.start()
    copies = []
    for n, part in enumerate(parts):
        copies.append(pltpu.make_async_copy(emb_ref.at[part, :], raw_ref.at[part, :], sems.at[n]))
        copies[n].start()
    before = jnp.where(iota((size, size), 0) < iota((size, size), 1), 1.0, 0.0).astype(BF16)
    slots.wait()
    slot = slot_ref[...]
    target = slot // ROWS
    low = slot - target * ROWS
    goes = iota((devices, ROWS), 0) == target
    goes_b = jnp.where(goes, 1.0, 0.0).astype(BF16)
    seen, ranks = jnp.zeros((devices, 1), F32), []
    for at in range(0, ROWS, size):
        here = goes[:, at:at + size]
        count = jnp.dot(goes_b[:, at:at + size], before, preferred_element_type=F32) + seen
        ranks.append(jnp.sum(jnp.where(here, count, 0.0), axis=0, keepdims=True))
        seen = seen + jnp.sum(jnp.where(here, 1.0, 0.0), axis=1, keepdims=True)
    rank = jnp.concatenate(ranks, axis=1)
    dest = target * PER_PAIR + rank.astype(jnp.int32)
    high = low // DIGITS
    even = iota((ROWS, LANES), 1) % 2 == 0
    digits = jnp.where(even, as_column(high.astype(F32)), as_column((low - high * DIGITS).astype(F32)))
    unit_ref[:, WIDTH:] = digits.astype(BF16)
    for n, part in enumerate(parts):
        copies[n].wait()
        values = raw_ref[part, :].astype(F32)
        mean = jnp.sum(values * values, axis=1, keepdims=True) * (1.0 / WIDTH)
        inverse = lax.rsqrt(mean + 1e-06) * (1.0 / math.sqrt(WIDTH))
        unit_ref[part, 0:WIDTH] = (values * inverse).astype(BF16)
    per_part = size // PER_PAIR
    back = []

    def send(source, target):
        back.append(pltpu.make_async_copy(source, target, sems.at[len(parts) + 1 + len(back)]))
        back[-1].start()

    lane = iota((per_part, HALF, LANES), 2)
    for n, part in enumerate(parts):
        place = one_hot(size, n * size, dest)
        placed = jnp.dot(place, unit_ref[...], preferred_element_type=F32)
        first = n * per_part
        sent = placed[:, WIDTH:].reshape(per_part, PER_PAIR, LANES)
        digit_ref[first:first + per_part] = jnp.where(lane < LANES // 2, sent[:, 0:HALF, :], sent[:, HALF:, :])
        for i in range(per_part):
            rows = placed[i * PER_PAIR:(i + 1) * PER_PAIR, :].astype(BF16)
            for piece in range(PIECES):
                rows_ref[first + i, piece * PER_PAIR:(piece + 1) * PER_PAIR, :] = rows[:, piece * LANES:(piece + 1) * LANES]
        for copy in range(COPIES):
            back_by = APART * copy
            body = pl.ds(copy * BODY, BODY)
            wrapped = max(0, back_by - first)
            if wrapped:
                send(rows_ref.at[pl.ds(first, wrapped)], out_hbm.at[pl.ds(devices - wrapped, wrapped), body, :])
            count = per_part - wrapped
            send(rows_ref.at[pl.ds(first + wrapped, count)], out_hbm.at[pl.ds(first + wrapped - back_by, count), body, :])
    which = iota((devices, HALF, LANES), 2) % (LANES // 2) // 2
    info = digit_ref[...]
    for copy in range(1, COPIES):
        ahead = APART * copy
        far = jnp.concatenate([digit_ref[ahead:], digit_ref[:ahead]], axis=0)
        info = jnp.where(which == copy, far, info)
    info_ref[...] = info.astype(BF16)
    send(info_ref, out_hbm.at[:, pl.ds(COPIES * BODY, HALF), :])
    for copy in back:
        copy.wait()


def tiles(got_hbm, copy, target, sem):
    started = []
    for piece in range(PIECES):
        at = (copy * PIECES + piece) * PER_PAIR
        lanes = pl.ds(piece * LANES, LANES)
        started.append(pltpu.make_async_copy(got_hbm.at[:, pl.ds(at, PER_PAIR), :], target.at[:, :, lanes], sem.at[piece]))
        started[-1].start()
    return started


def slot_tiles(got_hbm, target, sem):
    copy = pltpu.make_async_copy(got_hbm.at[:, pl.ds(COPIES * BODY, HALF), :], target, sem)
    copy.start()
    return copy


def arrival_slots(digits, copies):
    upper = digits.astype(F32)
    lower = jnp.concatenate([upper[:, :, LANES // 2:], upper[:, :, :LANES // 2]], axis=2)
    digits = jnp.concatenate([upper, lower], axis=1).reshape(ROWS, LANES)
    digits = jnp.transpose(digits)[0:8, :]
    return [(digits[2 * c:2 * c + 1, :] * DIGITS + digits[2 * c + 1:2 * c + 2, :]).astype(jnp.int32) for c in copies]


def arrival_ids(ids, land):
    ids = jnp.broadcast_to(ids.astype(F32), (8, ROWS)).astype(BF16)
    arrived = jnp.zeros((8, ROWS), F32)
    for at in range(0, ROWS, 256):
        place = one_hot(256, at, land)
        arrived = arrived + jnp.dot(ids[:, at:at + 256], place, preferred_element_type=F32)
    return arrived[0:1, :]


def split_kernel(got_hbm, list_ref, *refs):
    ids_refs, (out_ref, blocks_ref, far_ref, land_ref, digit_ref, sems) = refs[:COPIES], refs[COPIES:]
    slots = slot_tiles(got_hbm, digit_ref, sems.at[0, PIECES])
    rows = [tiles(got_hbm, c, blocks_ref.at[c], sems.at[c]) for c in range(COPIES - 1)]
    slots.wait()
    lands = arrival_slots(digit_ref[...], range(COPIES))
    land_ref[...] = lands[0]
    for c in range(COPIES):
        far_ref[c] = arrival_ids(ids_refs[c][...], lands[c])
    ids = far_ref[0]
    entries = list_ref[...].astype(F32)
    row = iota((TAIL, LANES), 0)
    for at in range(0, WIDTH, LANES):
        rest = ids[:, at + WIDTH:at + WIDTH + LANES] if at + WIDTH < ROWS else jnp.zeros((1, LANES), F32)
        tail = jnp.where(row == 0, ids[:, at:at + LANES], jnp.where(row == 1, rest, entries))
        out_ref[ROWS:ROWS + TAIL, at:at + LANES] = tail.astype(BF16)
    for copy in rows[0]:
        copy.wait()
    out_ref[0:ROWS, :] = blocks_ref[0].reshape(ROWS, WIDTH)
    for copy in rows[1]:
        copy.wait()


def weight_of(ref, shift):
    entries = ref[ROWS:ROWS + TAIL, 0:LANES].astype(F32)[2:3, :]
    return jnp.sum(jnp.where(iota((1, LANES), 1) == shift - 1, entries, 0.0), axis=1, keepdims=True)


def ids_row(ref):
    tail = ref[ROWS:ROWS + TAIL, :].astype(F32)
    return jnp.concatenate([tail[0:1, :], tail[1:2, 0:ROWS - WIDTH]], axis=1)


def tile_terms(scores, id_col, id_row, masked):
    rows, cols = scores.shape
    over_cols, over_rows = None, []
    for lane in range(cols // LANES):
        cut = slice(lane * LANES, (lane + 1) * LANES)
        half = jnp.tanh(scores[:, cut] * (0.5 * sharpness) - 0.5 * sharpness * threshold)
        factor = jnp.where(id_col == id_row[:, cut], 0.5, 0.25)
        term = factor * (1.0 + half)
        if masked:
            term = jnp.where(iota(term.shape, 0) == iota(term.shape, 1) + lane * LANES, 0.0, term)
        over_cols = term if over_cols is None else over_cols + term
        over_rows.append(jnp.sum(term.reshape(rows // 8, 8, LANES), axis=0))
    return over_cols, jnp.concatenate(over_rows, axis=1)


SIZE = 256
CUTS = [slice(at, at + SIZE) for at in range(0, ROWS, SIZE)]


def pair(a_ref, a_col, b_of, b_row, row_acc, total):
    over_rows = []
    for part in CUTS:
        b = b_of(part)
        down = None
        for at in CUTS:
            by_row, by_col = tile_terms(nt(a_ref[at, :], b), a_col[at, :], b_row[:, part], False)
            row_acc[at, :] = row_acc[at, :] + by_row
            down = by_col if down is None else down + by_col
        over_rows.append(down)
    total[...] = total[...] + jnp.sum(jnp.concatenate(over_rows, axis=1), axis=0, keepdims=True)


def listed_pairs(listed, first, second, between):
    one, two = [jnp.sum(entry) > 0.0 for entry in listed]

    @pl.when(one & two)
    def _():
        first()
        between()
        second()

    @pl.when(jnp.logical_not(one & two))
    def _():
        pl.when(one)(first)
        between()
        pl.when(two)(second)


def own_pair(ref, a_col, row, row_acc, col_acc):
    for i, at in enumerate(CUTS):
        a = ref[at, :]
        for j, part in enumerate(CUTS):
            if j < i:
                continue
            by_row, by_col = tile_terms(nt(a, ref[part, :]), a_col[at, :], row[:, part], i == j)
            row_acc[at, :] = row_acc[at, :] + by_row
            if j > i:
                col_acc[:, part] = col_acc[:, part] + by_col


def fold_rows(acc):
    return jnp.sum(jnp.transpose(acc[...]), axis=0, keepdims=True)


def first_kernel(got_hbm, own_ref, near_ref, ids_ref, sums_ref, far_ref, col, row_acc, sems):
    rows = [tiles(got_hbm, c, far_ref.at[c - 1], sems.at[c]) for c in range(COPIES - 1, 0, -1)]
    col[...] = as_column(ids_ref[0])
    row_acc[...] = jnp.zeros_like(row_acc)
    sums_ref[...] = jnp.zeros_like(sums_ref)

    def against(c, block):
        return lambda: pair(own_ref, col, block, ids_ref[c], row_acc, sums_ref.at[c])

    def arrived(copies):
        for copy in copies:
            copy.wait()

    listed = [weight_of(own_ref, APART * c) for c in range(1, COPIES)]
    listed_pairs(
        listed, against(1, block_part(near_ref, 1)), against(2, block_part(far_ref, 1)), lambda: arrived(rows[0])
    )
    arrived(rows[1])
    sums_ref[0] = fold_rows(row_acc)


def self_kernel(own_ref, land_ref, sum_ref, out_ref, place_ref, col, row_acc, col_acc):
    for at in range(0, ROWS, 256):
        place_ref[at:at + 256, :] = one_hot(256, at, land_ref[...])
    row = ids_row(own_ref)
    col[...] = as_column(row)
    row_acc[...] = jnp.zeros_like(row_acc)
    col_acc[...] = jnp.zeros_like(col_acc)
    own_pair(own_ref, col, row, row_acc, col_acc)
    out_ref[...] = sum_ref[...] + fold_rows(row_acc) + jnp.sum(col_acc[...], axis=0, keepdims=True)


def block_part(blocks_ref, which):
    def part(rows):
        at = pl.ds(rows.start // PER_PAIR, SIZE // PER_PAIR)
        return blocks_ref[which, at, :, :].reshape(SIZE, WIDTH)

    return part


def second_kernel(core_ref, near_ref, far_ref, ids_ref, sums_ref, sw_ref, *refs):
    outs, (total, col, row_acc) = refs[:COPIES + 1], refs[COPIES + 1:]
    total[...] = sums_ref[...]
    col[...] = as_column(ids_row(sw_ref))
    row_acc[...] = jnp.zeros_like(row_acc)

    def against(n, blocks_ref):
        def run():
            which = 1 - core_ref[0] + n
            pair(sw_ref, col, block_part(blocks_ref, 1 - core_ref[0]), ids_ref[which], row_acc, total.at[which])

        return run

    listed = [weight_of(sw_ref, 1), weight_of(sw_ref, 3)]
    listed_pairs(listed, against(0, near_ref), against(1, far_ref), lambda: None)
    for c in range(COPIES):
        outs[c][...] = total[c]
    outs[COPIES][...] = fold_rows(row_acc)


def end_kernel(place_ref, *refs):
    out_ref = refs[-1]
    load = refs[0][...]
    for ref in refs[1:-1]:
        load = load + ref[...]
    result = 1.0 / (1.0 + load)
    high = result.astype(BF16).astype(F32)
    mid = (result - high).astype(BF16).astype(F32)
    low = result - high - mid
    which = iota((8, ROWS), 0)
    parts = jnp.where(which == 0, high, jnp.where(which == 1, mid, jnp.where(which == 2, low, 0.0))).astype(BF16)
    for step in range(4):
        placed = nt(parts, place_ref[step * 256:(step + 1) * 256, :])
        out_ref[:, step * 256:(step + 1) * 256] = placed[0:1, :] + placed[1:2, :] + placed[2:3, :]


def vec(n):
    return jax.ShapeDtypeStruct((1, n), F32)


def call(kernel, out_shape, in_specs, scratch, tasks, args, mib=40, out_spec=VMEM):
    single = not isinstance(out_shape, (list, tuple))
    return pl.pallas_call(
        kernel,
        out_shape=out_shape,
        in_specs=in_specs,
        out_specs=out_spec if single else [out_spec] * len(out_shape),
        scratch_shapes=scratch,
        compiler_params=pltpu.CompilerParams(vmem_limit_bytes=mib << 20),
        cost_estimate=pl.CostEstimate(
            flops=int(HINT * tasks * 2 * ROWS * ROWS * WIDTH),
            transcendentals=int(HINT * tasks * ROWS * ROWS),
            bytes_accessed=int(HINT * (1 + tasks) * 2 * ROWS * WIDTH),
        ),
    )(*args)


def move(value, devices, change, only=None):
    pairs = [
        (p, change(p))
        for p in range(devices)
        if 0 <= change(p) < devices and (only is None or p % 2 == only)
    ]
    return lax.ppermute(value, AXES, pairs)


def local(embeddings, sorted_slot, cluster_ids, block_list):
    devices = lax.axis_size(AXES)
    position = lax.axis_index(AXES)
    core = (position % 2).astype(jnp.int32).reshape(1)
    move_d = functools.partial(move, devices=devices)
    scratch = pltpu.VMEM

    outgoing = call(
        functools.partial(front_kernel, devices),
        jax.ShapeDtypeStruct((devices, MESSAGE, LANES), BF16), [ANY] * 2,
        [scratch((1, ROWS), jnp.int32), scratch((ROWS, WIDTH), BF16), scratch((ROWS, WIDTH + LANES), BF16)]
        + [scratch((devices, HALF, LANES), F32), scratch((devices, HALF, LANES), BF16)]
        + [scratch((devices, BODY, LANES), BF16), pltpu.SemaphoreType.DMA((24,))],
        1, (sorted_slot.reshape(1, ROWS), embeddings), 62, ANY,
    )
    got = lax.all_to_all(outgoing, AXES, split_axis=0, concat_axis=0, tiled=True)
    ids = cluster_ids.reshape(1, ROWS)
    far_ids = [move_d(ids, change=lambda p, c=c: p - APART * c) for c in range(1, COPIES)]
    reach = position + 1 + jnp.arange(SHIFTS, dtype=jnp.int32)
    entries = jnp.pad(jnp.where(reach[None, :] < devices, block_list, 0), ((0, 0), (0, LANES - SHIFTS)))
    sems = pltpu.SemaphoreType.DMA
    two_blocks = jax.ShapeDtypeStruct((2, devices, PER_PAIR, WIDTH), BF16)
    own, near, block_ids, land = call(
        split_kernel,
        [
            jax.ShapeDtypeStruct((ROWS + TAIL, WIDTH), BF16),
            two_blocks,
            jax.ShapeDtypeStruct((COPIES, 1, ROWS), F32),
            jax.ShapeDtypeStruct((1, ROWS), jnp.int32),
        ],
        [ANY] + [VMEM] * (1 + COPIES), [scratch((devices, HALF, LANES), BF16), sems((COPIES, PIECES + 1))],
        0.5, (got, entries, ids, *far_ids), 16,
    )
    sw = move_d(own, change=lambda p: p ^ 1)
    sides = [scratch((ROWS, LANES), F32)] * 2 + [scratch((8, ROWS), F32)]
    sums, far = call(
        first_kernel, [jax.ShapeDtypeStruct((COPIES, 1, ROWS), F32), two_blocks], [ANY] + [VMEM] * 3,
        sides[:2] + [sems((COPIES, PIECES))], 2, (got, own, near, block_ids), 16,
    )
    sums = call(
        second_kernel, [vec(ROWS)] * (COPIES + 1), [SMEM] + [VMEM] * 5,
        [scratch((COPIES, 1, ROWS), F32)] + sides[:2],
        2, (core, near, far, block_ids, sums, sw), 16,
    )
    own_sum, place = call(
        self_kernel, [vec(ROWS), jax.ShapeDtypeStruct((ROWS, ROWS), BF16)], [VMEM] * 3, sides,
        0.6, (own, land, sums[0]), 16,
    )
    returned = [own_sum, move_d(sums[COPIES], change=lambda p: p ^ 1)]
    returned += [move_d(sums[c], change=lambda p, c=c: p + APART * c) for c in range(1, COPIES)]
    weights = call(end_kernel, vec(ROWS), [VMEM] * (COPIES + 2), [], 0.2, (place, *returned))
    return weights.reshape(ROWS)


def solution(mesh):
    in_specs = (
        P(("grp", "gr", "gc"), None),
        P(("grp", "gr", "gc")),
        P(("grp", "gr", "gc")),
        P(("grp", "gr", "gc"), None),
    )
    out_specs = P(("grp", "gr", "gc"))
    return jax.shard_map(local, mesh=mesh, in_specs=in_specs, out_specs=out_specs, check_vma=False)
```

```python
import functools
import math

import jax
import jax.numpy as jnp
from jax import lax
from jax.experimental import pallas as pl
from jax.experimental.pallas import tpu as pltpu
from jax.sharding import PartitionSpec as P

SHIFTS = 4
ROWS = 1024
WIDTH = 768
LANES = 128
HINT = 20
COPIES = 3
APART = 2
PER_PAIR = 16
PIECES = WIDTH // LANES
BODY = PIECES * PER_PAIR
HALF = PER_PAIR // 2
MESSAGE = COPIES * BODY + HALF
TAIL = 16
DIGITS = 32
AXES = ("gr", "gc")

sharpness = 20.0
threshold = 0.8

F32 = jnp.float32
BF16 = jnp.bfloat16
VMEM = pl.BlockSpec(memory_space=pltpu.VMEM)
ANY = pl.BlockSpec(memory_space=pl.ANY)
SMEM = pl.BlockSpec(memory_space=pltpu.SMEM)


def iota(shape, axis):
    return lax.broadcasted_iota(jnp.int32, shape, axis)


def one_hot(rows, first, wanted):
    hit = iota((rows, wanted.shape[1]), 0) + first == wanted
    return jnp.where(hit, 1.0, 0.0).astype(BF16)


def nt(a, b):
    return lax.dot_general(a, b, (((1,), (1,)), ((), ())), preferred_element_type=F32)


def as_column(row):
    return jnp.transpose(jnp.broadcast_to(row, (LANES, row.shape[1])))


def front_kernel(devices, slot_hbm, emb_ref, out_hbm, slot_ref, raw_ref, unit_ref, digit_ref, info_ref, rows_ref, sems):
    size = 256
    parts = [pl.ds(at, size) for at in range(0, ROWS, size)]
    slots = pltpu.make_async_copy(slot_hbm, slot_ref, sems.at[len(parts)])
    slots.start()
    copies = []
    for n, part in enumerate(parts):
        copies.append(pltpu.make_async_copy(emb_ref.at[part, :], raw_ref.at[part, :], sems.at[n]))
        copies[n].start()
    before = jnp.where(iota((size, size), 0) < iota((size, size), 1), 1.0, 0.0).astype(BF16)
    slots.wait()
    slot = slot_ref[...]
    target = slot // ROWS
    low = slot - target * ROWS
    goes = iota((devices, ROWS), 0) == target
    goes_b = jnp.where(goes, 1.0, 0.0).astype(BF16)
    seen, ranks = jnp.zeros((devices, 1), F32), []
    for at in range(0, ROWS, size):
        here = goes[:, at:at + size]
        count = jnp.dot(goes_b[:, at:at + size], before, preferred_element_type=F32) + seen
        ranks.append(jnp.sum(jnp.where(here, count, 0.0), axis=0, keepdims=True))
        seen = seen + jnp.sum(jnp.where(here, 1.0, 0.0), axis=1, keepdims=True)
    rank = jnp.concatenate(ranks, axis=1)
    dest = target * PER_PAIR + rank.astype(jnp.int32)
    high = low // DIGITS
    even = iota((ROWS, LANES), 1) % 2 == 0
    digits = jnp.where(even, as_column(high.astype(F32)), as_column((low - high * DIGITS).astype(F32)))
    unit_ref[:, WIDTH:] = digits.astype(BF16)
    for n, part in enumerate(parts):
        copies[n].wait()
        values = raw_ref[part, :].astype(F32)
        mean = jnp.sum(values * values, axis=1, keepdims=True) * (1.0 / WIDTH)
        inverse = lax.rsqrt(mean + 1e-06) * (1.0 / math.sqrt(WIDTH))
        unit_ref[part, 0:WIDTH] = (values * inverse).astype(BF16)
    per_part = size // PER_PAIR
    back = []

    def send(source, target):
        back.append(pltpu.make_async_copy(source, target, sems.at[len(parts) + 1 + len(back)]))
        back[-1].start()

    lane = iota((per_part, HALF, LANES), 2)
    for n, part in enumerate(parts):
        place = one_hot(size, n * size, dest)
        placed = jnp.dot(place, unit_ref[...], preferred_element_type=F32)
        first = n * per_part
        sent = placed[:, WIDTH:].reshape(per_part, PER_PAIR, LANES)
        digit_ref[first:first + per_part] = jnp.where(lane < LANES // 2, sent[:, 0:HALF, :], sent[:, HALF:, :])
        for i in range(per_part):
            rows = placed[i * PER_PAIR:(i + 1) * PER_PAIR, :].astype(BF16)
            for piece in range(PIECES):
                rows_ref[first + i, piece * PER_PAIR:(piece + 1) * PER_PAIR, :] = rows[:, piece * LANES:(piece + 1) * LANES]
        for copy in range(COPIES):
            back_by = APART * copy
            body = pl.ds(copy * BODY, BODY)
            wrapped = max(0, back_by - first)
            if wrapped:
                send(rows_ref.at[pl.ds(first, wrapped)], out_hbm.at[pl.ds(devices - wrapped, wrapped), body, :])
            count = per_part - wrapped
            send(rows_ref.at[pl.ds(first + wrapped, count)], out_hbm.at[pl.ds(first + wrapped - back_by, count), body, :])
    which = iota((devices, HALF, LANES), 2) % (LANES // 2) // 2
    info = digit_ref[...]
    for copy in range(1, COPIES):
        ahead = APART * copy
        far = jnp.concatenate([digit_ref[ahead:], digit_ref[:ahead]], axis=0)
        info = jnp.where(which == copy, far, info)
    info_ref[...] = info.astype(BF16)
    send(info_ref, out_hbm.at[:, pl.ds(COPIES * BODY, HALF), :])
    for copy in back:
        copy.wait()


def tiles(got_hbm, copy, target, sem):
    started = []
    for piece in range(PIECES):
        at = (copy * PIECES + piece) * PER_PAIR
        lanes = pl.ds(piece * LANES, LANES)
        started.append(pltpu.make_async_copy(got_hbm.at[:, pl.ds(at, PER_PAIR), :], target.at[:, :, lanes], sem.at[piece]))
        started[-1].start()
    return started


def slot_tiles(got_hbm, target, sem):
    copy = pltpu.make_async_copy(got_hbm.at[:, pl.ds(COPIES * BODY, HALF), :], target, sem)
    copy.start()
    return copy


def arrival_slots(digits, copies):
    upper = digits.astype(F32)
    lower = jnp.concatenate([upper[:, :, LANES // 2:], upper[:, :, :LANES // 2]], axis=2)
    digits = jnp.concatenate([upper, lower], axis=1).reshape(ROWS, LANES)
    digits = jnp.transpose(digits)[0:8, :]
    return [(digits[2 * c:2 * c + 1, :] * DIGITS + digits[2 * c + 1:2 * c + 2, :]).astype(jnp.int32) for c in copies]


def arrival_ids(ids, land):
    ids = jnp.broadcast_to(ids.astype(F32), (8, ROWS)).astype(BF16)
    arrived = jnp.zeros((8, ROWS), F32)
    for at in range(0, ROWS, 256):
        place = one_hot(256, at, land)
        arrived = arrived + jnp.dot(ids[:, at:at + 256], place, preferred_element_type=F32)
    return arrived[0:1, :]


def split_kernel(got_hbm, list_ref, *refs):
    ids_refs, (out_ref, blocks_ref, far_ref, land_ref, digit_ref, sems) = refs[:COPIES], refs[COPIES:]
    slots = slot_tiles(got_hbm, digit_ref, sems.at[0, PIECES])
    rows = [tiles(got_hbm, c, blocks_ref.at[c], sems.at[c]) for c in range(COPIES)]
    slots.wait()
    lands = arrival_slots(digit_ref[...], range(COPIES))
    land_ref[...] = lands[0]
    for c in range(COPIES):
        far_ref[c] = arrival_ids(ids_refs[c][...], lands[c])
    ids = far_ref[0]
    entries = list_ref[...].astype(F32)
    row = iota((TAIL, LANES), 0)
    for at in range(0, WIDTH, LANES):
        rest = ids[:, at + WIDTH:at + WIDTH + LANES] if at + WIDTH < ROWS else jnp.zeros((1, LANES), F32)
        tail = jnp.where(row == 0, ids[:, at:at + LANES], jnp.where(row == 1, rest, entries))
        out_ref[ROWS:ROWS + TAIL, at:at + LANES] = tail.astype(BF16)
    for copy in rows[0]:
        copy.wait()
    out_ref[0:ROWS, :] = blocks_ref[0].reshape(ROWS, WIDTH)
    for copy in (*rows[1], *rows[2]):
        copy.wait()


def weight_of(ref, shift):
    entries = ref[ROWS:ROWS + TAIL, 0:LANES].astype(F32)[2:3, :]
    return jnp.sum(jnp.where(iota((1, LANES), 1) == shift - 1, entries, 0.0), axis=1, keepdims=True)


def ids_row(ref):
    tail = ref[ROWS:ROWS + TAIL, :].astype(F32)
    return jnp.concatenate([tail[0:1, :], tail[1:2, 0:ROWS - WIDTH]], axis=1)


def tile_terms(scores, id_col, id_row, masked):
    rows, cols = scores.shape
    over_cols, over_rows = None, []
    for lane in range(cols // LANES):
        cut = slice(lane * LANES, (lane + 1) * LANES)
        half = jnp.tanh(scores[:, cut] * (0.5 * sharpness) - 0.5 * sharpness * threshold)
        factor = jnp.where(id_col == id_row[:, cut], 0.5, 0.25)
        term = factor * (1.0 + half)
        if masked:
            term = jnp.where(iota(term.shape, 0) == iota(term.shape, 1) + lane * LANES, 0.0, term)
        over_cols = term if over_cols is None else over_cols + term
        over_rows.append(jnp.sum(term.reshape(rows // 8, 8, LANES), axis=0))
    return over_cols, jnp.concatenate(over_rows, axis=1)


SIZE = 256
CUTS = [slice(at, at + SIZE) for at in range(0, ROWS, SIZE)]


def pair(a_ref, a_col, b_of, b_row, row_acc, total):
    over_rows = []
    for part in CUTS:
        b = b_of(part)
        down = None
        for at in CUTS:
            by_row, by_col = tile_terms(nt(a_ref[at, :], b), a_col[at, :], b_row[:, part], False)
            row_acc[at, :] = row_acc[at, :] + by_row
            down = by_col if down is None else down + by_col
        over_rows.append(down)
    total[...] = total[...] + jnp.sum(jnp.concatenate(over_rows, axis=1), axis=0, keepdims=True)


def listed_pairs(listed, first, second):
    one, two = [jnp.sum(entry) > 0.0 for entry in listed]

    @pl.when(one & two)
    def _():
        first()
        second()

    @pl.when(jnp.logical_not(one & two))
    def _():
        pl.when(one)(first)
        pl.when(two)(second)


def own_pair(ref, a_col, row, row_acc, col_acc):
    for i, at in enumerate(CUTS):
        a = ref[at, :]
        for j, part in enumerate(CUTS):
            if j < i:
                continue
            by_row, by_col = tile_terms(nt(a, ref[part, :]), a_col[at, :], row[:, part], i == j)
            row_acc[at, :] = row_acc[at, :] + by_row
            if j > i:
                col_acc[:, part] = col_acc[:, part] + by_col


def fold_rows(acc):
    return jnp.sum(jnp.transpose(acc[...]), axis=0, keepdims=True)


def first_kernel(own_ref, blocks_ref, ids_ref, sums_ref, col, row_acc):
    col[...] = as_column(ids_ref[0])
    row_acc[...] = jnp.zeros_like(row_acc)
    sums_ref[...] = jnp.zeros_like(sums_ref)

    def against(c):
        return lambda: pair(own_ref, col, block_part(blocks_ref, c), ids_ref[c], row_acc, sums_ref.at[c])

    listed_pairs([weight_of(own_ref, APART * c) for c in range(1, COPIES)], against(1), against(2))
    sums_ref[0] = fold_rows(row_acc)


def self_kernel(own_ref, sum_ref, out_ref, col, row_acc, col_acc):
    row = ids_row(own_ref)
    col[...] = as_column(row)
    row_acc[...] = jnp.zeros_like(row_acc)
    col_acc[...] = jnp.zeros_like(col_acc)
    own_pair(own_ref, col, row, row_acc, col_acc)
    out_ref[...] = sum_ref[...] + fold_rows(row_acc) + jnp.sum(col_acc[...], axis=0, keepdims=True)


def block_part(blocks_ref, which):
    def part(rows):
        at = pl.ds(rows.start // PER_PAIR, SIZE // PER_PAIR)
        return blocks_ref[which, at, :, :].reshape(SIZE, WIDTH)

    return part


def second_kernel(core_ref, blocks_ref, ids_ref, sums_ref, sw_ref, *refs):
    outs, (total, col, row_acc) = refs[:COPIES + 1], refs[COPIES + 1:]
    total[...] = sums_ref[...]
    col[...] = as_column(ids_row(sw_ref))
    row_acc[...] = jnp.zeros_like(row_acc)

    def against(n):
        def run():
            which = 1 - core_ref[0] + n
            pair(sw_ref, col, block_part(blocks_ref, which), ids_ref[which], row_acc, total.at[which])

        return run

    listed_pairs([weight_of(sw_ref, 1), weight_of(sw_ref, 3)], against(0), against(1))
    for c in range(COPIES):
        outs[c][...] = total[c]
    outs[COPIES][...] = fold_rows(row_acc)


def end_kernel(land_ref, *refs):
    out_ref = refs[-1]
    load = refs[0][...]
    for ref in refs[1:-1]:
        load = load + ref[...]
    result = 1.0 / (1.0 + load)
    high = result.astype(BF16).astype(F32)
    mid = (result - high).astype(BF16).astype(F32)
    low = result - high - mid
    which = iota((8, ROWS), 0)
    parts = jnp.where(which == 0, high, jnp.where(which == 1, mid, jnp.where(which == 2, low, 0.0))).astype(BF16)
    for step in range(4):
        placed = nt(parts, one_hot(256, step * 256, land_ref[...]))
        out_ref[:, step * 256:(step + 1) * 256] = placed[0:1, :] + placed[1:2, :] + placed[2:3, :]


def vec(n):
    return jax.ShapeDtypeStruct((1, n), F32)


def call(kernel, out_shape, in_specs, scratch, tasks, args, mib=40, out_spec=VMEM):
    single = not isinstance(out_shape, (list, tuple))
    return pl.pallas_call(
        kernel,
        out_shape=out_shape,
        in_specs=in_specs,
        out_specs=out_spec if single else [out_spec] * len(out_shape),
        scratch_shapes=scratch,
        compiler_params=pltpu.CompilerParams(vmem_limit_bytes=mib << 20),
        cost_estimate=pl.CostEstimate(
            flops=int(HINT * tasks * 2 * ROWS * ROWS * WIDTH),
            transcendentals=int(HINT * tasks * ROWS * ROWS),
            bytes_accessed=int(HINT * (1 + tasks) * 2 * ROWS * WIDTH),
        ),
    )(*args)


def move(value, devices, change, only=None):
    pairs = [
        (p, change(p))
        for p in range(devices)
        if 0 <= change(p) < devices and (only is None or p % 2 == only)
    ]
    return lax.ppermute(value, AXES, pairs)


def local(embeddings, sorted_slot, cluster_ids, block_list):
    devices = lax.axis_size(AXES)
    position = lax.axis_index(AXES)
    core = (position % 2).astype(jnp.int32).reshape(1)
    move_d = functools.partial(move, devices=devices)
    scratch = pltpu.VMEM

    outgoing = call(
        functools.partial(front_kernel, devices),
        jax.ShapeDtypeStruct((devices, MESSAGE, LANES), BF16), [ANY] * 2,
        [scratch((1, ROWS), jnp.int32), scratch((ROWS, WIDTH), BF16), scratch((ROWS, WIDTH + LANES), BF16)]
        + [scratch((devices, HALF, LANES), F32), scratch((devices, HALF, LANES), BF16)]
        + [scratch((devices, BODY, LANES), BF16), pltpu.SemaphoreType.DMA((24,))],
        1, (sorted_slot.reshape(1, ROWS), embeddings), 62, ANY,
    )
    got = lax.all_to_all(outgoing, AXES, split_axis=0, concat_axis=0, tiled=True)
    ids = cluster_ids.reshape(1, ROWS)
    far_ids = [move_d(ids, change=lambda p, c=c: p - APART * c) for c in range(1, COPIES)]
    reach = position + 1 + jnp.arange(SHIFTS, dtype=jnp.int32)
    entries = jnp.pad(jnp.where(reach[None, :] < devices, block_list, 0), ((0, 0), (0, LANES - SHIFTS)))
    sems = pltpu.SemaphoreType.DMA
    own, blocks, block_ids, land = call(
        split_kernel,
        [
            jax.ShapeDtypeStruct((ROWS + TAIL, WIDTH), BF16),
            jax.ShapeDtypeStruct((COPIES, devices, PER_PAIR, WIDTH), BF16),
            jax.ShapeDtypeStruct((COPIES, 1, ROWS), F32),
            jax.ShapeDtypeStruct((1, ROWS), jnp.int32),
        ],
        [ANY] + [VMEM] * (1 + COPIES), [scratch((devices, HALF, LANES), BF16), sems((COPIES, PIECES + 1))],
        0.5, (got, entries, ids, *far_ids), 16,
    )
    sw = move_d(own, change=lambda p: p ^ 1)
    sides = [scratch((ROWS, LANES), F32)] * 2 + [scratch((8, ROWS), F32)]
    sums = call(
        first_kernel, jax.ShapeDtypeStruct((COPIES, 1, ROWS), F32), [VMEM] * 3, sides[:2], 2, (own, blocks, block_ids), 16
    )
    sums = call(
        second_kernel, [vec(ROWS)] * (COPIES + 1), [SMEM] + [VMEM] * 4,
        [scratch((COPIES, 1, ROWS), F32)] + sides[:2],
        2, (core, blocks, block_ids, sums, sw), 16,
    )
    own_sum = call(self_kernel, vec(ROWS), [VMEM] * 2, sides, 0.6, (own, sums[0]), 16)
    returned = [own_sum, move_d(sums[COPIES], change=lambda p: p ^ 1)]
    returned += [move_d(sums[c], change=lambda p, c=c: p + APART * c) for c in range(1, COPIES)]
    weights = call(end_kernel, vec(ROWS), [VMEM] * (COPIES + 2), [], 0.2, (land, *returned))
    return weights.reshape(ROWS)


def solution(mesh):
    in_specs = (
        P(("grp", "gr", "gc"), None),
        P(("grp", "gr", "gc")),
        P(("grp", "gr", "gc")),
        P(("grp", "gr", "gc"), None),
    )
    out_specs = P(("grp", "gr", "gc"))
    return jax.shard_map(local, mesh=mesh, in_specs=in_specs, out_specs=out_specs, check_vma=False)
```

```python
import functools
import math

import jax
import jax.numpy as jnp
from jax import lax
from jax.experimental import pallas as pl
from jax.experimental.pallas import tpu as pltpu
from jax.sharding import PartitionSpec as P

SHIFTS = 4
ROWS = 1024
WIDTH = 768
LANES = 128
HINT = 20
COPIES = 3
APART = 2
PER_PAIR = 16
PIECES = WIDTH // LANES
BODY = PIECES * PER_PAIR
HALF = PER_PAIR // 2
MESSAGE = COPIES * BODY + HALF
TAIL = 16
DIGITS = 32
AXES = ("gr", "gc")

sharpness = 20.0
threshold = 0.8

F32 = jnp.float32
BF16 = jnp.bfloat16
VMEM = pl.BlockSpec(memory_space=pltpu.VMEM)
ANY = pl.BlockSpec(memory_space=pl.ANY)
SMEM = pl.BlockSpec(memory_space=pltpu.SMEM)


def iota(shape, axis):
    return lax.broadcasted_iota(jnp.int32, shape, axis)


def one_hot(rows, first, wanted):
    hit = iota((rows, wanted.shape[1]), 0) + first == wanted
    return jnp.where(hit, 1.0, 0.0).astype(BF16)


def nt(a, b):
    return lax.dot_general(a, b, (((1,), (1,)), ((), ())), preferred_element_type=F32)


def as_column(row):
    return jnp.transpose(jnp.broadcast_to(row, (LANES, row.shape[1])))


def front_kernel(devices, slot_hbm, emb_ref, out_hbm, slot_ref, raw_ref, unit_ref, digit_ref, info_ref, rows_ref, sems):
    size = 256
    parts = [pl.ds(at, size) for at in range(0, ROWS, size)]
    slots = pltpu.make_async_copy(slot_hbm, slot_ref, sems.at[len(parts)])
    slots.start()
    copies = []
    for n, part in enumerate(parts):
        copies.append(pltpu.make_async_copy(emb_ref.at[part, :], raw_ref.at[part, :], sems.at[n]))
        copies[n].start()
    before = jnp.where(iota((size, size), 0) < iota((size, size), 1), 1.0, 0.0).astype(BF16)
    slots.wait()
    slot = slot_ref[...]
    target = slot // ROWS
    low = slot - target * ROWS
    goes = iota((devices, ROWS), 0) == target
    goes_b = jnp.where(goes, 1.0, 0.0).astype(BF16)
    seen, ranks = jnp.zeros((devices, 1), F32), []
    for at in range(0, ROWS, size):
        here = goes[:, at:at + size]
        count = jnp.dot(goes_b[:, at:at + size], before, preferred_element_type=F32) + seen
        ranks.append(jnp.sum(jnp.where(here, count, 0.0), axis=0, keepdims=True))
        seen = seen + jnp.sum(jnp.where(here, 1.0, 0.0), axis=1, keepdims=True)
    rank = jnp.concatenate(ranks, axis=1)
    dest = target * PER_PAIR + rank.astype(jnp.int32)
    high = low // DIGITS
    even = iota((ROWS, LANES), 1) % 2 == 0
    digits = jnp.where(even, as_column(high.astype(F32)), as_column((low - high * DIGITS).astype(F32)))
    unit_ref[:, WIDTH:] = digits.astype(BF16)
    for n, part in enumerate(parts):
        copies[n].wait()
        values = raw_ref[part, :].astype(F32)
        mean = jnp.sum(values * values, axis=1, keepdims=True) * (1.0 / WIDTH)
        inverse = lax.rsqrt(mean + 1e-06) * (1.0 / math.sqrt(WIDTH))
        unit_ref[part, 0:WIDTH] = (values * inverse).astype(BF16)
    per_part = size // PER_PAIR
    back = []

    def send(source, target):
        back.append(pltpu.make_async_copy(source, target, sems.at[len(parts) + 1 + len(back)]))
        back[-1].start()

    lane = iota((per_part, HALF, LANES), 2)
    for n, part in enumerate(parts):
        place = one_hot(size, n * size, dest)
        placed = jnp.dot(place, unit_ref[...], preferred_element_type=F32)
        first = n * per_part
        sent = placed[:, WIDTH:].reshape(per_part, PER_PAIR, LANES)
        digit_ref[first:first + per_part] = jnp.where(lane < LANES // 2, sent[:, 0:HALF, :], sent[:, HALF:, :])
        for i in range(per_part):
            rows = placed[i * PER_PAIR:(i + 1) * PER_PAIR, :].astype(BF16)
            for piece in range(PIECES):
                rows_ref[first + i, piece * PER_PAIR:(piece + 1) * PER_PAIR, :] = rows[:, piece * LANES:(piece + 1) * LANES]
        for copy in range(COPIES):
            back_by = APART * copy
            body = pl.ds(copy * BODY, BODY)
            wrapped = max(0, back_by - first)
            if wrapped:
                send(rows_ref.at[pl.ds(first, wrapped)], out_hbm.at[pl.ds(devices - wrapped, wrapped), body, :])
            count = per_part - wrapped
            send(rows_ref.at[pl.ds(first + wrapped, count)], out_hbm.at[pl.ds(first + wrapped - back_by, count), body, :])
    which = iota((devices, HALF, LANES), 2) % (LANES // 2) // 2
    info = digit_ref[...]
    for copy in range(1, COPIES):
        ahead = APART * copy
        far = jnp.concatenate([digit_ref[ahead:], digit_ref[:ahead]], axis=0)
        info = jnp.where(which == copy, far, info)
    info_ref[...] = info.astype(BF16)
    send(info_ref, out_hbm.at[:, pl.ds(COPIES * BODY, HALF), :])
    for copy in back:
        copy.wait()


def tiles(got_hbm, copy, target, sem):
    started = []
    for piece in range(PIECES):
        at = (copy * PIECES + piece) * PER_PAIR
        lanes = pl.ds(piece * LANES, LANES)
        started.append(pltpu.make_async_copy(got_hbm.at[:, pl.ds(at, PER_PAIR), :], target.at[:, :, lanes], sem.at[piece]))
        started[-1].start()
    return started


def slot_tiles(got_hbm, target, sem):
    copy = pltpu.make_async_copy(got_hbm.at[:, pl.ds(COPIES * BODY, HALF), :], target, sem)
    copy.start()
    return copy


def arrival_slots(digits, copies):
    upper = digits.astype(F32)
    lower = jnp.concatenate([upper[:, :, LANES // 2:], upper[:, :, :LANES // 2]], axis=2)
    digits = jnp.concatenate([upper, lower], axis=1).reshape(ROWS, LANES)
    digits = jnp.transpose(digits)[0:8, :]
    return [(digits[2 * c:2 * c + 1, :] * DIGITS + digits[2 * c + 1:2 * c + 2, :]).astype(jnp.int32) for c in copies]


def arrival_ids(ids, land):
    ids = jnp.broadcast_to(ids.astype(F32), (8, ROWS)).astype(BF16)
    arrived = jnp.zeros((8, ROWS), F32)
    for at in range(0, ROWS, 256):
        place = one_hot(256, at, land)
        arrived = arrived + jnp.dot(ids[:, at:at + 256], place, preferred_element_type=F32)
    return arrived[0:1, :]


def split_kernel(got_hbm, list_ref, *refs):
    ids_refs, (out_ref, blocks_ref, far_ref, land_ref, digit_ref, sems) = refs[:COPIES], refs[COPIES:]
    slots = slot_tiles(got_hbm, digit_ref, sems.at[0, PIECES])
    rows = [tiles(got_hbm, c, blocks_ref.at[c], sems.at[c]) for c in range(COPIES)]
    slots.wait()
    lands = arrival_slots(digit_ref[...], range(COPIES))
    land_ref[...] = lands[0]
    for c in range(COPIES):
        far_ref[c] = arrival_ids(ids_refs[c][...], lands[c])
    ids = far_ref[0]
    entries = list_ref[...].astype(F32)
    row = iota((TAIL, LANES), 0)
    for at in range(0, WIDTH, LANES):
        rest = ids[:, at + WIDTH:at + WIDTH + LANES] if at + WIDTH < ROWS else jnp.zeros((1, LANES), F32)
        tail = jnp.where(row == 0, ids[:, at:at + LANES], jnp.where(row == 1, rest, entries))
        out_ref[ROWS:ROWS + TAIL, at:at + LANES] = tail.astype(BF16)
    for copy in rows[0]:
        copy.wait()
    out_ref[0:ROWS, :] = blocks_ref[0].reshape(ROWS, WIDTH)
    for copy in (*rows[1], *rows[2]):
        copy.wait()


def weight_of(ref, shift):
    entries = ref[ROWS:ROWS + TAIL, 0:LANES].astype(F32)[2:3, :]
    return jnp.sum(jnp.where(iota((1, LANES), 1) == shift - 1, entries, 0.0), axis=1, keepdims=True)


def ids_row(ref):
    tail = ref[ROWS:ROWS + TAIL, :].astype(F32)
    return jnp.concatenate([tail[0:1, :], tail[1:2, 0:ROWS - WIDTH]], axis=1)


def tile_terms(scores, id_col, id_row, masked):
    rows, cols = scores.shape
    over_cols, over_rows = None, []
    for lane in range(cols // LANES):
        cut = slice(lane * LANES, (lane + 1) * LANES)
        half = jnp.tanh(scores[:, cut] * (0.5 * sharpness) - 0.5 * sharpness * threshold)
        factor = jnp.where(id_col == id_row[:, cut], 0.5, 0.25)
        term = factor + factor * half
        if masked:
            term = jnp.where(iota(term.shape, 0) == iota(term.shape, 1) + lane * LANES, 0.0, term)
        over_cols = term if over_cols is None else over_cols + term
        over_rows.append(jnp.sum(term.reshape(rows // 8, 8, LANES), axis=0))
    return over_cols, jnp.concatenate(over_rows, axis=1)


SIZE = 256
CUTS = [slice(at, at + SIZE) for at in range(0, ROWS, SIZE)]


def pair(a_ref, a_col, b_of, b_row, row_acc, total):
    over_rows = []
    for part in CUTS:
        b = b_of(part)
        down = None
        for at in CUTS:
            by_row, by_col = tile_terms(nt(a_ref[at, :], b), a_col[at, :], b_row[:, part], False)
            row_acc[at, :] = row_acc[at, :] + by_row
            down = by_col if down is None else down + by_col
        over_rows.append(down)
    total[...] = total[...] + jnp.sum(jnp.concatenate(over_rows, axis=1), axis=0, keepdims=True)


def listed_pairs(listed, first, second):
    one, two = [jnp.sum(entry) > 0.0 for entry in listed]

    @pl.when(one & two)
    def _():
        first()
        second()

    @pl.when(jnp.logical_not(one & two))
    def _():
        pl.when(one)(first)
        pl.when(two)(second)


def own_pair(ref, a_col, row, row_acc, col_acc):
    for i, at in enumerate(CUTS):
        a = ref[at, :]
        for j, part in enumerate(CUTS):
            if j < i:
                continue
            by_row, by_col = tile_terms(nt(a, ref[part, :]), a_col[at, :], row[:, part], i == j)
            row_acc[at, :] = row_acc[at, :] + by_row
            if j > i:
                col_acc[:, part] = col_acc[:, part] + by_col


def fold_rows(acc):
    return jnp.sum(jnp.transpose(acc[...]), axis=0, keepdims=True)


def first_kernel(own_ref, blocks_ref, ids_ref, sums_ref, col, row_acc):
    col[...] = as_column(ids_ref[0])
    row_acc[...] = jnp.zeros_like(row_acc)
    sums_ref[...] = jnp.zeros_like(sums_ref)

    def against(c):
        return lambda: pair(own_ref, col, block_part(blocks_ref, c), ids_ref[c], row_acc, sums_ref.at[c])

    listed_pairs([weight_of(own_ref, APART * c) for c in range(1, COPIES)], against(1), against(2))
    sums_ref[0] = fold_rows(row_acc)


def self_kernel(own_ref, sum_ref, out_ref, col, row_acc, col_acc):
    row = ids_row(own_ref)
    col[...] = as_column(row)
    row_acc[...] = jnp.zeros_like(row_acc)
    col_acc[...] = jnp.zeros_like(col_acc)
    own_pair(own_ref, col, row, row_acc, col_acc)
    out_ref[...] = sum_ref[...] + fold_rows(row_acc) + jnp.sum(col_acc[...], axis=0, keepdims=True)


def block_part(blocks_ref, which):
    def part(rows):
        at = pl.ds(rows.start // PER_PAIR, SIZE // PER_PAIR)
        return blocks_ref[which, at, :, :].reshape(SIZE, WIDTH)

    return part


def second_kernel(core_ref, blocks_ref, ids_ref, sums_ref, sw_ref, *refs):
    outs, (total, col, row_acc) = refs[:COPIES + 1], refs[COPIES + 1:]
    total[...] = sums_ref[...]
    col[...] = as_column(ids_row(sw_ref))
    row_acc[...] = jnp.zeros_like(row_acc)

    def against(n):
        def run():
            which = 1 - core_ref[0] + n
            pair(sw_ref, col, block_part(blocks_ref, which), ids_ref[which], row_acc, total.at[which])

        return run

    listed_pairs([weight_of(sw_ref, 1), weight_of(sw_ref, 3)], against(0), against(1))
    for c in range(COPIES):
        outs[c][...] = total[c]
    outs[COPIES][...] = fold_rows(row_acc)


def end_kernel(land_ref, *refs):
    out_ref = refs[-1]
    load = refs[0][...]
    for ref in refs[1:-1]:
        load = load + ref[...]
    result = 1.0 / (1.0 + load)
    high = result.astype(BF16).astype(F32)
    mid = (result - high).astype(BF16).astype(F32)
    low = result - high - mid
    which = iota((8, ROWS), 0)
    parts = jnp.where(which == 0, high, jnp.where(which == 1, mid, jnp.where(which == 2, low, 0.0))).astype(BF16)
    for step in range(4):
        placed = nt(parts, one_hot(256, step * 256, land_ref[...]))
        out_ref[:, step * 256:(step + 1) * 256] = placed[0:1, :] + placed[1:2, :] + placed[2:3, :]


def vec(n):
    return jax.ShapeDtypeStruct((1, n), F32)


def call(kernel, out_shape, in_specs, scratch, tasks, args, mib=40, out_spec=VMEM):
    single = not isinstance(out_shape, (list, tuple))
    return pl.pallas_call(
        kernel,
        out_shape=out_shape,
        in_specs=in_specs,
        out_specs=out_spec if single else [out_spec] * len(out_shape),
        scratch_shapes=scratch,
        compiler_params=pltpu.CompilerParams(vmem_limit_bytes=mib << 20),
        cost_estimate=pl.CostEstimate(
            flops=int(HINT * tasks * 2 * ROWS * ROWS * WIDTH),
            transcendentals=int(HINT * tasks * ROWS * ROWS),
            bytes_accessed=int(HINT * (1 + tasks) * 2 * ROWS * WIDTH),
        ),
    )(*args)


def move(value, devices, change, only=None):
    pairs = [
        (p, change(p))
        for p in range(devices)
        if 0 <= change(p) < devices and (only is None or p % 2 == only)
    ]
    return lax.ppermute(value, AXES, pairs)


def local(embeddings, sorted_slot, cluster_ids, block_list):
    devices = lax.axis_size(AXES)
    position = lax.axis_index(AXES)
    core = (position % 2).astype(jnp.int32).reshape(1)
    move_d = functools.partial(move, devices=devices)
    scratch = pltpu.VMEM

    outgoing = call(
        functools.partial(front_kernel, devices),
        jax.ShapeDtypeStruct((devices, MESSAGE, LANES), BF16), [ANY] * 2,
        [scratch((1, ROWS), jnp.int32), scratch((ROWS, WIDTH), BF16), scratch((ROWS, WIDTH + LANES), BF16)]
        + [scratch((devices, HALF, LANES), F32), scratch((devices, HALF, LANES), BF16)]
        + [scratch((devices, BODY, LANES), BF16), pltpu.SemaphoreType.DMA((24,))],
        1, (sorted_slot.reshape(1, ROWS), embeddings), 62, ANY,
    )
    got = lax.all_to_all(outgoing, AXES, split_axis=0, concat_axis=0, tiled=True)
    ids = cluster_ids.reshape(1, ROWS)
    far_ids = [move_d(ids, change=lambda p, c=c: p - APART * c) for c in range(1, COPIES)]
    reach = position + 1 + jnp.arange(SHIFTS, dtype=jnp.int32)
    entries = jnp.pad(jnp.where(reach[None, :] < devices, block_list, 0), ((0, 0), (0, LANES - SHIFTS)))
    sems = pltpu.SemaphoreType.DMA
    own, blocks, block_ids, land = call(
        split_kernel,
        [
            jax.ShapeDtypeStruct((ROWS + TAIL, WIDTH), BF16),
            jax.ShapeDtypeStruct((COPIES, devices, PER_PAIR, WIDTH), BF16),
            jax.ShapeDtypeStruct((COPIES, 1, ROWS), F32),
            jax.ShapeDtypeStruct((1, ROWS), jnp.int32),
        ],
        [ANY] + [VMEM] * (1 + COPIES), [scratch((devices, HALF, LANES), BF16), sems((COPIES, PIECES + 1))],
        0.5, (got, entries, ids, *far_ids), 16,
    )
    sw = move_d(own, change=lambda p: p ^ 1)
    sides = [scratch((ROWS, LANES), F32)] * 2 + [scratch((8, ROWS), F32)]
    sums = call(
        first_kernel, jax.ShapeDtypeStruct((COPIES, 1, ROWS), F32), [VMEM] * 3, sides[:2], 2, (own, blocks, block_ids), 16
    )
    sums = call(
        second_kernel, [vec(ROWS)] * (COPIES + 1), [SMEM] + [VMEM] * 4,
        [scratch((COPIES, 1, ROWS), F32)] + sides[:2],
        2, (core, blocks, block_ids, sums, sw), 16,
    )
    own_sum = call(self_kernel, vec(ROWS), [VMEM] * 2, sides, 0.6, (own, sums[0]), 16)
    returned = [own_sum, move_d(sums[COPIES], change=lambda p: p ^ 1)]
    returned += [move_d(sums[c], change=lambda p, c=c: p + APART * c) for c in range(1, COPIES)]
    weights = call(end_kernel, vec(ROWS), [VMEM] * (COPIES + 2), [], 0.2, (land, *returned))
    return weights.reshape(ROWS)


def solution(mesh):
    in_specs = (
        P(("grp", "gr", "gc"), None),
        P(("grp", "gr", "gc")),
        P(("grp", "gr", "gc")),
        P(("grp", "gr", "gc"), None),
    )
    out_specs = P(("grp", "gr", "gc"))
    return jax.shard_map(local, mesh=mesh, in_specs=in_specs, out_specs=out_specs, check_vma=False)
```

```python
import functools
import math

import jax
import jax.numpy as jnp
from jax import lax
from jax.experimental import pallas as pl
from jax.experimental.pallas import tpu as pltpu
from jax.sharding import PartitionSpec as P

SHIFTS = 4
ROWS = 1024
WIDTH = 768
LANES = 128
HINT = 20
COPIES = 3
APART = 2
PER_PAIR = 16
PIECES = WIDTH // LANES
BODY = PIECES * PER_PAIR
HALF = PER_PAIR // 2
MESSAGE = COPIES * BODY + HALF
TAIL = 16
DIGITS = 32
AXES = ("gr", "gc")

sharpness = 20.0
threshold = 0.8

F32 = jnp.float32
BF16 = jnp.bfloat16
VMEM = pl.BlockSpec(memory_space=pltpu.VMEM)
ANY = pl.BlockSpec(memory_space=pl.ANY)
SMEM = pl.BlockSpec(memory_space=pltpu.SMEM)


def iota(shape, axis):
    return lax.broadcasted_iota(jnp.int32, shape, axis)


def one_hot(rows, first, wanted):
    hit = iota((rows, wanted.shape[1]), 0).astype(jnp.int16) == (wanted - first).astype(jnp.int16)
    return jnp.where(hit, jnp.ones((), BF16), jnp.zeros((), BF16))


def nt(a, b):
    return lax.dot_general(a, b, (((1,), (1,)), ((), ())), preferred_element_type=F32)


def as_column(row):
    return jnp.transpose(jnp.broadcast_to(row, (LANES, row.shape[1])))


def front_kernel(devices, slot_hbm, emb_ref, out_hbm, slot_ref, raw_ref, unit_ref, digit_ref, info_ref, rows_ref, sems):
    size = 256
    parts = [pl.ds(at, size) for at in range(0, ROWS, size)]
    slots = pltpu.make_async_copy(slot_hbm, slot_ref, sems.at[len(parts)])
    slots.start()
    copies = []
    for n, part in enumerate(parts):
        copies.append(pltpu.make_async_copy(emb_ref.at[part, :], raw_ref.at[part, :], sems.at[n]))
        copies[n].start()
    before = jnp.where(iota((size, size), 0) < iota((size, size), 1), 1.0, 0.0).astype(BF16)
    slots.wait()
    slot = slot_ref[...]
    target = slot // ROWS
    low = slot - target * ROWS
    goes = iota((devices, ROWS), 0) == target
    goes_b = jnp.where(goes, 1.0, 0.0).astype(BF16)
    seen, ranks = jnp.zeros((devices, 1), F32), []
    for at in range(0, ROWS, size):
        here = goes[:, at:at + size]
        count = jnp.dot(goes_b[:, at:at + size], before, preferred_element_type=F32) + seen
        ranks.append(jnp.sum(jnp.where(here, count, 0.0), axis=0, keepdims=True))
        seen = seen + jnp.sum(jnp.where(here, 1.0, 0.0), axis=1, keepdims=True)
    rank = jnp.concatenate(ranks, axis=1)
    dest = target * PER_PAIR + rank.astype(jnp.int32)
    high = low // DIGITS
    even = iota((ROWS, LANES), 1) % 2 == 0
    digits = jnp.where(even, as_column(high.astype(F32)), as_column((low - high * DIGITS).astype(F32)))
    unit_ref[:, WIDTH:] = digits.astype(BF16)
    for n, part in enumerate(parts):
        copies[n].wait()
        values = raw_ref[part, :].astype(F32)
        mean = jnp.sum(values * values, axis=1, keepdims=True) * (1.0 / WIDTH)
        inverse = lax.rsqrt(mean + 1e-06) * (1.0 / math.sqrt(WIDTH))
        unit_ref[part, 0:WIDTH] = (values * inverse).astype(BF16)
    per_part = size // PER_PAIR
    back = []

    def send(source, target):
        back.append(pltpu.make_async_copy(source, target, sems.at[len(parts) + 1 + len(back)]))
        back[-1].start()

    lane = iota((per_part, HALF, LANES), 2)
    for n, part in enumerate(parts):
        place = one_hot(size, n * size, dest)
        placed = jnp.dot(place, unit_ref[...], preferred_element_type=F32)
        first = n * per_part
        sent = placed[:, WIDTH:].reshape(per_part, PER_PAIR, LANES)
        digit_ref[first:first + per_part] = jnp.where(lane < LANES // 2, sent[:, 0:HALF, :], sent[:, HALF:, :])
        for i in range(per_part):
            rows = placed[i * PER_PAIR:(i + 1) * PER_PAIR, :].astype(BF16)
            for piece in range(PIECES):
                rows_ref[first + i, piece * PER_PAIR:(piece + 1) * PER_PAIR, :] = rows[:, piece * LANES:(piece + 1) * LANES]
        for copy in range(COPIES):
            back_by = APART * copy
            body = pl.ds(copy * BODY, BODY)
            wrapped = max(0, back_by - first)
            if wrapped:
                send(rows_ref.at[pl.ds(first, wrapped)], out_hbm.at[pl.ds(devices - wrapped, wrapped), body, :])
            count = per_part - wrapped
            send(rows_ref.at[pl.ds(first + wrapped, count)], out_hbm.at[pl.ds(first + wrapped - back_by, count), body, :])
    which = iota((devices, HALF, LANES), 2) % (LANES // 2) // 2
    info = digit_ref[...]
    for copy in range(1, COPIES):
        ahead = APART * copy
        far = jnp.concatenate([digit_ref[ahead:], digit_ref[:ahead]], axis=0)
        info = jnp.where(which == copy, far, info)
    info_ref[...] = info.astype(BF16)
    send(info_ref, out_hbm.at[:, pl.ds(COPIES * BODY, HALF), :])
    for copy in back:
        copy.wait()


def tiles(got_hbm, copy, target, sem):
    started = []
    for piece in range(PIECES):
        at = (copy * PIECES + piece) * PER_PAIR
        lanes = pl.ds(piece * LANES, LANES)
        started.append(pltpu.make_async_copy(got_hbm.at[:, pl.ds(at, PER_PAIR), :], target.at[:, :, lanes], sem.at[piece]))
        started[-1].start()
    return started


def slot_tiles(got_hbm, target, sem):
    copy = pltpu.make_async_copy(got_hbm.at[:, pl.ds(COPIES * BODY, HALF), :], target, sem)
    copy.start()
    return copy


def arrival_slots(digits, copies):
    upper = digits.astype(F32)
    lower = jnp.concatenate([upper[:, :, LANES // 2:], upper[:, :, :LANES // 2]], axis=2)
    digits = jnp.concatenate([upper, lower], axis=1).reshape(ROWS, LANES)
    digits = jnp.transpose(digits)[0:8, :]
    return [(digits[2 * c:2 * c + 1, :] * DIGITS + digits[2 * c + 1:2 * c + 2, :]).astype(jnp.int32) for c in copies]


def arrival_ids(ids, land):
    ids = jnp.broadcast_to(ids.astype(F32), (8, ROWS)).astype(BF16)
    arrived = jnp.zeros((8, ROWS), F32)
    for at in range(0, ROWS, 256):
        place = one_hot(256, at, land)
        arrived = arrived + jnp.dot(ids[:, at:at + 256], place, preferred_element_type=F32)
    return arrived[0:1, :]


def split_kernel(got_hbm, list_ref, *refs):
    ids_refs, (out_ref, blocks_ref, far_ref, land_ref, digit_ref, sems) = refs[:COPIES], refs[COPIES:]
    slots = slot_tiles(got_hbm, digit_ref, sems.at[0, PIECES])
    rows = [tiles(got_hbm, c, blocks_ref.at[c], sems.at[c]) for c in range(COPIES)]
    slots.wait()
    lands = arrival_slots(digit_ref[...], range(COPIES))
    land_ref[...] = lands[0]
    for c in range(COPIES):
        far_ref[c] = arrival_ids(ids_refs[c][...], lands[c])
    ids = far_ref[0]
    entries = list_ref[...].astype(F32)
    row = iota((TAIL, LANES), 0)
    for at in range(0, WIDTH, LANES):
        rest = ids[:, at + WIDTH:at + WIDTH + LANES] if at + WIDTH < ROWS else jnp.zeros((1, LANES), F32)
        tail = jnp.where(row == 0, ids[:, at:at + LANES], jnp.where(row == 1, rest, entries))
        out_ref[ROWS:ROWS + TAIL, at:at + LANES] = tail.astype(BF16)
    for copy in rows[0]:
        copy.wait()
    out_ref[0:ROWS, :] = blocks_ref[0].reshape(ROWS, WIDTH)
    for copy in (*rows[1], *rows[2]):
        copy.wait()


def weight_of(ref, shift):
    entries = ref[ROWS:ROWS + TAIL, 0:LANES].astype(F32)[2:3, :]
    return jnp.sum(jnp.where(iota((1, LANES), 1) == shift - 1, entries, 0.0), axis=1, keepdims=True)


def ids_row(ref):
    tail = ref[ROWS:ROWS + TAIL, :].astype(F32)
    return jnp.concatenate([tail[0:1, :], tail[1:2, 0:ROWS - WIDTH]], axis=1)


def tile_terms(scores, id_col, id_row, masked):
    rows, cols = scores.shape
    over_cols, over_rows = None, []
    for lane in range(cols // LANES):
        cut = slice(lane * LANES, (lane + 1) * LANES)
        half = jnp.tanh(scores[:, cut] * (0.5 * sharpness) - 0.5 * sharpness * threshold)
        factor = jnp.where(id_col == id_row[:, cut], 0.5, 0.25)
        term = factor + factor * half
        if masked:
            term = jnp.where(iota(term.shape, 0) == iota(term.shape, 1) + lane * LANES, 0.0, term)
        over_cols = term if over_cols is None else over_cols + term
        over_rows.append(jnp.sum(term.reshape(rows // 8, 8, LANES), axis=0))
    return over_cols, jnp.concatenate(over_rows, axis=1)


SIZE = 256
CUTS = [slice(at, at + SIZE) for at in range(0, ROWS, SIZE)]


def pair(a_ref, a_col, b_of, b_row, row_acc, total):
    over_rows = []
    for part in CUTS:
        b = b_of(part)
        down = None
        for at in CUTS:
            by_row, by_col = tile_terms(nt(a_ref[at, :], b), a_col[at, :], b_row[:, part], False)
            row_acc[at, :] = row_acc[at, :] + by_row
            down = by_col if down is None else down + by_col
        over_rows.append(down)
    total[...] = total[...] + jnp.sum(jnp.concatenate(over_rows, axis=1), axis=0, keepdims=True)


def listed_pairs(listed, first, second):
    one, two = [jnp.sum(entry) > 0.0 for entry in listed]

    @pl.when(one & two)
    def _():
        first()
        second()

    @pl.when(jnp.logical_not(one & two))
    def _():
        pl.when(one)(first)
        pl.when(two)(second)


def own_pair(ref, a_col, row, row_acc, col_acc):
    for i, at in enumerate(CUTS):
        a = ref[at, :]
        for j, part in enumerate(CUTS):
            if j < i:
                continue
            by_row, by_col = tile_terms(nt(a, ref[part, :]), a_col[at, :], row[:, part], i == j)
            row_acc[at, :] = row_acc[at, :] + by_row
            if j > i:
                col_acc[:, part] = col_acc[:, part] + by_col


def fold_rows(acc):
    return jnp.sum(jnp.transpose(acc[...]), axis=0, keepdims=True)


def first_kernel(own_ref, blocks_ref, ids_ref, sums_ref, col, row_acc):
    col[...] = as_column(ids_ref[0])
    row_acc[...] = jnp.zeros_like(row_acc)
    sums_ref[...] = jnp.zeros_like(sums_ref)

    def against(c):
        return lambda: pair(own_ref, col, block_part(blocks_ref, c), ids_ref[c], row_acc, sums_ref.at[c])

    listed_pairs([weight_of(own_ref, APART * c) for c in range(1, COPIES)], against(1), against(2))
    sums_ref[0] = fold_rows(row_acc)


def self_kernel(own_ref, sum_ref, out_ref, col, row_acc, col_acc):
    row = ids_row(own_ref)
    col[...] = as_column(row)
    row_acc[...] = jnp.zeros_like(row_acc)
    col_acc[...] = jnp.zeros_like(col_acc)
    own_pair(own_ref, col, row, row_acc, col_acc)
    out_ref[...] = sum_ref[...] + fold_rows(row_acc) + jnp.sum(col_acc[...], axis=0, keepdims=True)


def block_part(blocks_ref, which):
    def part(rows):
        at = pl.ds(rows.start // PER_PAIR, SIZE // PER_PAIR)
        return blocks_ref[which, at, :, :].reshape(SIZE, WIDTH)

    return part


def second_kernel(core_ref, blocks_ref, ids_ref, sums_ref, sw_ref, *refs):
    outs, (total, col, row_acc) = refs[:COPIES + 1], refs[COPIES + 1:]
    total[...] = sums_ref[...]
    col[...] = as_column(ids_row(sw_ref))
    row_acc[...] = jnp.zeros_like(row_acc)

    def against(n):
        def run():
            which = 1 - core_ref[0] + n
            pair(sw_ref, col, block_part(blocks_ref, which), ids_ref[which], row_acc, total.at[which])

        return run

    listed_pairs([weight_of(sw_ref, 1), weight_of(sw_ref, 3)], against(0), against(1))
    for c in range(COPIES):
        outs[c][...] = total[c]
    outs[COPIES][...] = fold_rows(row_acc)


def end_kernel(land_ref, *refs):
    out_ref = refs[-1]
    load = refs[0][...]
    for ref in refs[1:-1]:
        load = load + ref[...]
    result = 1.0 / (1.0 + load)
    high = result.astype(BF16).astype(F32)
    mid = (result - high).astype(BF16).astype(F32)
    low = result - high - mid
    which = iota((8, ROWS), 0)
    parts = jnp.where(which == 0, high, jnp.where(which == 1, mid, jnp.where(which == 2, low, 0.0))).astype(BF16)
    for step in range(4):
        placed = nt(parts, one_hot(256, step * 256, land_ref[...]))
        out_ref[:, step * 256:(step + 1) * 256] = placed[0:1, :] + placed[1:2, :] + placed[2:3, :]


def vec(n):
    return jax.ShapeDtypeStruct((1, n), F32)


def call(kernel, out_shape, in_specs, scratch, tasks, args, mib=40, out_spec=VMEM):
    single = not isinstance(out_shape, (list, tuple))
    return pl.pallas_call(
        kernel,
        out_shape=out_shape,
        in_specs=in_specs,
        out_specs=out_spec if single else [out_spec] * len(out_shape),
        scratch_shapes=scratch,
        compiler_params=pltpu.CompilerParams(vmem_limit_bytes=mib << 20),
        cost_estimate=pl.CostEstimate(
            flops=int(HINT * tasks * 2 * ROWS * ROWS * WIDTH),
            transcendentals=int(HINT * tasks * ROWS * ROWS),
            bytes_accessed=int(HINT * (1 + tasks) * 2 * ROWS * WIDTH),
        ),
    )(*args)


def move(value, devices, change, only=None):
    pairs = [
        (p, change(p))
        for p in range(devices)
        if 0 <= change(p) < devices and (only is None or p % 2 == only)
    ]
    return lax.ppermute(value, AXES, pairs)


def local(embeddings, sorted_slot, cluster_ids, block_list):
    devices = lax.axis_size(AXES)
    position = lax.axis_index(AXES)
    core = (position % 2).astype(jnp.int32).reshape(1)
    move_d = functools.partial(move, devices=devices)
    scratch = pltpu.VMEM

    outgoing = call(
        functools.partial(front_kernel, devices),
        jax.ShapeDtypeStruct((devices, MESSAGE, LANES), BF16), [ANY] * 2,
        [scratch((1, ROWS), jnp.int32), scratch((ROWS, WIDTH), BF16), scratch((ROWS, WIDTH + LANES), BF16)]
        + [scratch((devices, HALF, LANES), F32), scratch((devices, HALF, LANES), BF16)]
        + [scratch((devices, BODY, LANES), BF16), pltpu.SemaphoreType.DMA((24,))],
        1, (sorted_slot.reshape(1, ROWS), embeddings), 62, ANY,
    )
    got = lax.all_to_all(outgoing, AXES, split_axis=0, concat_axis=0, tiled=True)
    ids = cluster_ids.reshape(1, ROWS)
    far_ids = [move_d(ids, change=lambda p, c=c: p - APART * c) for c in range(1, COPIES)]
    reach = position + 1 + jnp.arange(SHIFTS, dtype=jnp.int32)
    entries = jnp.pad(jnp.where(reach[None, :] < devices, block_list, 0), ((0, 0), (0, LANES - SHIFTS)))
    sems = pltpu.SemaphoreType.DMA
    own, blocks, block_ids, land = call(
        split_kernel,
        [
            jax.ShapeDtypeStruct((ROWS + TAIL, WIDTH), BF16),
            jax.ShapeDtypeStruct((COPIES, devices, PER_PAIR, WIDTH), BF16),
            jax.ShapeDtypeStruct((COPIES, 1, ROWS), F32),
            jax.ShapeDtypeStruct((1, ROWS), jnp.int32),
        ],
        [ANY] + [VMEM] * (1 + COPIES), [scratch((devices, HALF, LANES), BF16), sems((COPIES, PIECES + 1))],
        0.5, (got, entries, ids, *far_ids), 16,
    )
    sw = move_d(own, change=lambda p: p ^ 1)
    sides = [scratch((ROWS, LANES), F32)] * 2 + [scratch((8, ROWS), F32)]
    sums = call(
        first_kernel, jax.ShapeDtypeStruct((COPIES, 1, ROWS), F32), [VMEM] * 3, sides[:2], 2, (own, blocks, block_ids), 16
    )
    sums = call(
        second_kernel, [vec(ROWS)] * (COPIES + 1), [SMEM] + [VMEM] * 4,
        [scratch((COPIES, 1, ROWS), F32)] + sides[:2],
        2, (core, blocks, block_ids, sums, sw), 16,
    )
    own_sum = call(self_kernel, vec(ROWS), [VMEM] * 2, sides, 0.6, (own, sums[0]), 16)
    returned = [own_sum, move_d(sums[COPIES], change=lambda p: p ^ 1)]
    returned += [move_d(sums[c], change=lambda p, c=c: p + APART * c) for c in range(1, COPIES)]
    weights = call(end_kernel, vec(ROWS), [VMEM] * (COPIES + 2), [], 0.2, (land, *returned))
    return weights.reshape(ROWS)


def solution(mesh):
    in_specs = (
        P(("grp", "gr", "gc"), None),
        P(("grp", "gr", "gc")),
        P(("grp", "gr", "gc")),
        P(("grp", "gr", "gc"), None),
    )
    out_specs = P(("grp", "gr", "gc"))
    return jax.shard_map(local, mesh=mesh, in_specs=in_specs, out_specs=out_specs, check_vma=False)
```
